32 devices in a mesh: dp: 16 (over z, y, x), seq: 2 (over core).
Axes of the slice: x: 2, y: 2, z: 4, core: 2. Of those that a mesh axis runs over, the one named last changes fastest.
Arguments:
- tokens: bfloat16 [32, 1024, 768], P('dp', 'seq'), may hold values from -6 to 6
- ln1_gain: bfloat16 [768], P('dp'), may hold values from 0.5 to 1.5
- ln1_bias: bfloat16 [768], P('dp'), may hold values from -2 to 2
- qkv_weight: bfloat16 [768, 2304], P('dp'), may hold values from -0.21875 to 0.21875
- shift_taps: bfloat16 [4, 768], P(None, 'dp'), may hold values from -3 to 3
- decay_rates: bfloat16 [768], P('dp'), may hold values from 9.727478e-05 to 0.03125
- out_weight: bfloat16 [768, 768], P('dp'), may hold values from -0.0017089844 to 0.0017089844
- ln2_gain: bfloat16 [768], P('dp'), may hold values from 0.5 to 1.5
- ln2_bias: bfloat16 [768], P('dp'), may hold values from -2 to 2
- up_weight: bfloat16 [768, 3072], P('dp'), may hold values from -0.21875 to 0.21875
- down_weight: bfloat16 [3072, 768], P('dp'), may hold values from -0.109375 to 0.109375
- lengths: int32 [32], P('dp'), may hold values from 256 to 1024, as said below
- out_grad: bfloat16 [32, 1024, 768], P('dp', 'seq'), may hold values from -6 to 6
Outputs:
- mixed: bfloat16 [32, 1024, 768], P('dp', 'seq')
- input_grad: float32 [32, 1024, 768], P('dp', 'seq')
- ln1_gain_grad: float32 [768], P('dp')
- ln1_bias_grad: float32 [768], P('dp')
- qkv_weight_grad: float32 [768, 2304], P('dp')
- shift_taps_grad: float32 [4, 768], P(None, 'dp')
- decay_rates_grad: float32 [768], P('dp')
- out_weight_grad: float32 [768, 768], P('dp')
- ln2_gain_grad: float32 [768], P('dp')
- ln2_bias_grad: float32 [768], P('dp')
- up_weight_grad: float32 [768, 3072], P('dp')
- down_weight_grad: float32 [3072, 768], P('dp')
The draws below stay inside these ranges and needn't reach their ends.
Inputs may be any that keep to these rules, and one draw needn't show every extreme that they name: `lengths`: of the 2 slots of each index of dp one, drawn from the seed, uses all 1024 positions; the others use 1024 // 4 to 1024.
All inputs are finite; a program needn't handle non-finite values.
Results may differ from the reference program's by a relative error of at most 0.0095.
Values may be sent and summed in bfloat16 or wider, within the bound.
A program may use at most 256 MiB of HBM per device.

```python
import math
from functools import partial
import jax
import jax.numpy as jnp
from jax import lax

D = 768
FF = 3072
HEADS = 12
HEAD_DIM = 64
SLOTS = 2
BLOCK = 512
SEQLEN = 1024
BATCH = 32


def draw_lengths(key, part):
    group_count = BATCH // SLOTS
    first_key, second_key, third_key = jax.random.split(jax.random.fold_in(key, 17), 3)
    lengths_drawn = jax.random.randint(first_key, (group_count, SLOTS), SEQLEN // 4, SEQLEN + 1)
    longest = jax.random.randint(second_key, (group_count,), 0, SLOTS)
    chosen = jax.random.randint(third_key, (), 0, group_count)
    slot_ids = jnp.arange(SLOTS)
    group_ids = jnp.arange(group_count)
    shortest = (longest[chosen] + 1) % SLOTS
    lengths_drawn = jnp.where(slot_ids[None, :] == longest[:, None], SEQLEN, lengths_drawn)
    lengths_drawn = jnp.where((group_ids[:, None] == chosen) & (slot_ids[None, :] == shortest), SEQLEN // 4, lengths_drawn)
    return lengths_drawn.reshape(BATCH).astype(jnp.int32)


def block_levels(rng, shape, pieces, smallest, high):
    level = 1.0
    for position, shards_of in pieces:
        heights = jax.random.uniform(jax.random.fold_in(jax.random.fold_in(rng, 6), position), (shards_of,), jnp.float32, smallest / len(pieces), high / len(pieces))
        level = level * jnp.repeat(jnp.exp(heights), shape[position] // shards_of).reshape((-1,) + (1,) * (len(shape) - 1 - position))
    return level


def noise(own_key, shape, scale, reach, cuts=(), held_as=jnp.bfloat16):
    values = jax.random.normal(own_key, shape, jnp.float32) * scale
    if len(cuts) > 0:
        values = block_levels(own_key, shape, cuts, -0.22, 0.18) * values
    return jnp.clip(values, min=-reach, max=reach).astype(held_as)


def setup_inputs(seed: int = 0) -> dict:
    arg_keys = jax.random.split(jax.random.key(seed), 14)
    return {
        "tokens": noise(arg_keys[0], (BATCH, SEQLEN, D), 1.0, 6.0, ((0, 16), (1, 2))),
        "ln1_gain": jnp.clip(1.0 + 0.1 * jax.random.normal(arg_keys[1], (D,), jnp.float32), 0.5, 1.5).astype(jnp.bfloat16),
        "ln1_bias": noise(arg_keys[2], (D,), 0.3, 2.0, ((0, 16),)),
        "qkv_weight": noise(arg_keys[3], (D, 3 * D), D ** -0.5, 0.21875, ((0, 16),)),
        "shift_taps": noise(arg_keys[4], (4, D), 0.5, 3.0, ((1, 16),)),
        "decay_rates": jnp.clip(jnp.exp(math.log(0.03125) - 5.772235 * jax.random.uniform(arg_keys[5], (D,), jnp.float32) ** block_levels(arg_keys[5], (D,), ((0, 16),), -0.2, 0.2)), 9.72747802734375e-05, 0.03125).astype(jnp.bfloat16),
        "out_weight": noise(arg_keys[6], (D, D), (16 * D * SEQLEN) ** -0.5, 0.0017089844, ((0, 16),)),
        "ln2_gain": jnp.clip(1.0 + 0.1 * jax.random.normal(arg_keys[7], (D,), jnp.float32), 0.5, 1.5).astype(jnp.bfloat16),
        "ln2_bias": noise(arg_keys[8], (D,), 0.3, 2.0, ((0, 16),)),
        "up_weight": noise(arg_keys[9], (D, FF), D ** -0.5, 0.21875, ((0, 16),)),
        "down_weight": noise(arg_keys[10], (FF, D), FF ** -0.5, 0.109375, ((0, 16),)),
        "lengths": draw_lengths(jax.random.fold_in(arg_keys[13], 71), 0),
        "out_grad": noise(arg_keys[12], (BATCH, SEQLEN, D), 1.0, 6.0, ((0, 16), (1, 2))),
    }


@jax.custom_vjp
def low(v):
    return lax.optimization_barrier(v.astype(jnp.bfloat16)).astype(jnp.float32)

@jax.custom_vjp
def low_back(v):
    return v

def low_keep(v):
    return (low(v), None)

def low_pass(kept, grad):
    return (grad,)

def back_keep(v):
    return (v, None)

def back_low(kept, grad):
    return (low(grad),)
low.defvjp(low_keep, low_pass)
low_back.defvjp(back_keep, back_low)
precise = lax.Precision.HIGHEST

def layer_norm(values, norm_gain, offset):
    center = lax.optimization_barrier(jnp.mean(values, axis=-1, keepdims=True))
    centered = values - center
    spread = lax.optimization_barrier(jnp.mean(centered * centered, axis=-1, keepdims=True))
    return centered * lax.rsqrt(spread + 1e-05) * norm_gain + offset

def shift_mix(extended, tap_table):
    block_len = extended.shape[-2] - 3
    mixed_sum = tap_table[0] * extended[..., 3:3 + block_len, :]
    for lag_step in range(1, 4):
        mixed_sum = mixed_sum + tap_table[lag_step] * extended[..., 3 - lag_step:3 - lag_step + block_len, :]
    return mixed_sum

def factors(queries, key_rows, rate_vector):
    block_len = queries.shape[1]
    rate_grid = rate_vector.reshape(queries.shape[2], -1)
    positions = jnp.arange(block_len, dtype=jnp.float32)[:, None, None]
    decayed = queries * jnp.exp(-rate_grid * positions)
    lifted = key_rows * jnp.exp(rate_grid * positions)
    tail_keys = key_rows * jnp.exp(-rate_grid * (block_len - 1.0 - positions))
    reaching = queries * jnp.exp(-rate_grid * (positions + 1.0))
    carry_decay = jnp.exp(-rate_grid * block_len)
    return (decayed, lifted, tail_keys, reaching, carry_decay)

def block_ssm(queries, key_rows, values, rate_vector, state_in):
    block_len = queries.shape[1]
    decayed, lifted, tail_keys, reaching, carry_decay = factors(queries, key_rows, rate_vector)
    decayed = low(decayed)
    lifted = low(lifted)
    tail_keys = low(tail_keys)
    reaching = low(reaching)
    scores = jnp.einsum('bthk,bshk->bhts', decayed, lifted, precision=precise)
    position_ids = jnp.arange(block_len)
    scores = low(low_back(jnp.where(position_ids[:, None] >= position_ids[None, :], scores, 0.0)))
    within = jnp.einsum('bhts,bshv->bthv', scores, values, precision=precise)
    fresh_state = jnp.einsum('bshk,bshv->bhkv', tail_keys, values, precision=precise)
    inter = jnp.einsum('bthk,bhkv->bthv', reaching, state_in, precision=precise)
    return (low_back(within + inter), carry_decay[None, :, :, None] * state_in + fresh_state)

def slot_forward(params, tokens):
    gain_one, bias_one, qkv_w, tap_table, rate_vector, out_w, gain_two, bias_two, up_w, down_w = params
    model_width = tokens.shape[1]
    normed = low(layer_norm(tokens, gain_one, bias_one))
    projected = low(low_back(jnp.dot(normed, qkv_w, precision=precise)))
    queries = projected[:, :model_width]
    key_rows = projected[:, model_width:2 * model_width]
    values = projected[:, 2 * model_width:]
    extended = jnp.concatenate([jnp.zeros((3, model_width), jnp.float32), key_rows], axis=0)
    shifted = shift_mix(extended, tap_table)
    block_count = tokens.shape[0] // BLOCK

    def blocks(array):
        return array.reshape(block_count, BLOCK, HEADS, HEAD_DIM)

    def advance(state, inputs):
        block_out, new_state = block_ssm(inputs[0][None], inputs[1][None], inputs[2][None], rate_vector, state[None])
        return (new_state[0], block_out[0])
    start_state = jnp.zeros((HEADS, HEAD_DIM, HEAD_DIM), jnp.float32)
    _, outputs = lax.scan(jax.checkpoint(advance), start_state, (blocks(queries), blocks(shifted), blocks(values)))
    mixer = low(outputs.reshape(tokens.shape[0], model_width))
    branch = low_back(jnp.dot(mixer, out_w, precision=precise))
    resid = tokens + branch
    normed_two = low(layer_norm(resid, gain_two, bias_two))
    hidden_pre = low_back(jnp.dot(normed_two, up_w, precision=precise))
    hidden = low(jax.nn.gelu(hidden_pre))
    return resid + low_back(jnp.dot(hidden, down_w, precision=precise))

def reference(tokens, ln1_gain, ln1_bias, qkv_weight, shift_taps, decay_rates, out_weight, ln2_gain, ln2_bias, up_weight, down_weight, lengths, out_grad):
    params = tuple((weight_arg.astype(jnp.float32) for weight_arg in (ln1_gain, ln1_bias, qkv_weight, shift_taps, decay_rates, out_weight, ln2_gain, ln2_bias, up_weight, down_weight)))

    def forward(inputs, *weights):
        return lax.map(jax.checkpoint(partial(slot_forward, weights)), inputs)
    result, pullback = jax.vjp(forward, tokens.astype(jnp.float32), *params)
    positions = jnp.arange(SEQLEN, dtype=jnp.int32)
    keep_mask = (positions[None, :] < lengths[:, None]).astype(jnp.float32)
    grads = pullback(out_grad.astype(jnp.float32) * keep_mask[:, :, None])
    return (result.astype(jnp.bfloat16), grads[0], grads[1], grads[2], grads[3], grads[4], grads[5], grads[6], grads[7], grads[8], grads[9], grads[10])
```

```python
import functools

import jax
import jax.numpy as jnp
from jax import lax
from jax.experimental import pallas as pl
from jax.experimental.pallas import tpu as pltpu
from jax.sharding import PartitionSpec as P

HEADS = 12
HEAD_DIM = 64
MESH = pl.DeviceIdType.MESH
MIB = 2**20


precise = lax.Precision.HIGHEST


class Place:
    def __init__(self):
        self.dp = lax.axis_index("dp")
        self.core = lax.axis_index("seq")
        self.z = self.dp // 4
        self.stride_a = 2 - self.core
        self.stride_b = 1 + self.core
        self.a = (self.dp // self.stride_a) % 2
        self.b = (self.dp // self.stride_b) % 2

    def block(self, dz, da, db):
        z = (self.z + dz) % 4
        a = (self.a + da) % 2
        b = (self.b + db) % 2
        return z * 4 + a * self.stride_a + b * self.stride_b

    def peer(self, dz, da, db):
        return (self.block(dz, da, db), self.core)

    def sibling(self):
        return (self.dp, 1 - self.core)


PEERS = ((1, 0, 0), (2, 0, 0), (3, 0, 0), (0, 1, 0), (0, 0, 1))


def enter(place):
    barrier = pltpu.get_barrier_semaphore()
    for step in PEERS:
        pl.semaphore_signal(barrier, inc=1, device_id=place.peer(*step), device_id_type=MESH)
    pl.semaphore_signal(barrier, inc=1, device_id=place.sibling(), device_id_type=MESH)
    pl.semaphore_wait(barrier, len(PEERS) + 1)


def index_of(dz, da, db):
    return dz * 4 + da * 2 + db


def gather_kernel(count, *refs):
    shards, wholes = refs[: count + 1], refs[count + 1 : 2 * count + 2]
    local_sem, send_sem, pass_sem, recv_sem, other_sem = refs[2 * count + 2 :]
    place = Place()
    core = place.core
    enter(place)
    started = []

    def half(ref, rows, start):
        columns = ref.shape[1] // 2
        return ref.at[
            pl.ds(pl.multiple_of(start, 16), rows), pl.ds(pl.multiple_of(core * columns, 128), columns)
        ]

    def window(which, block):
        if which == count:
            return wholes[which].at[block]
        rows = shards[which].shape[0]
        return half(wholes[which], rows, block * rows)

    def own(which):
        if which == count:
            return shards[which].at[...]
        return half(shards[which], shards[which].shape[0], 0)

    def send(which, what, step, slot):
        block = place.block(*what)
        source = own(which) if index_of(*what) == 0 else window(which, block)
        lands = tuple((w - s) % n for w, s, n in zip(what, step, (4, 2, 2)))
        copy = pltpu.make_async_remote_copy(
            src_ref=source,
            dst_ref=window(which, block),
            send_sem=send_sem.at[which, slot],
            recv_sem=recv_sem.at[which, index_of(*lands)],
            device_id=place.peer(*step),
            device_id_type=MESH,
        )
        copy.start()
        started.append(copy)

    def wait_block(which, what):
        block = window(which, place.block(*what))
        pltpu.make_async_copy(block, block, recv_sem.at[which, index_of(*what)]).wait()

    def pass_on(which, what):
        if which == count:
            return
        block = window(which, place.block(*what))
        copy = pltpu.make_async_remote_copy(
            src_ref=block,
            dst_ref=block,
            send_sem=pass_sem.at[which, index_of(*what)],
            recv_sem=other_sem.at[which, index_of(*what)],
            device_id=place.sibling(),
            device_id_type=MESH,
        )
        copy.start()
        started.append(copy)

    stays = []
    for which in range(count + 1):
        rows = shards[which].shape[0]
        target = (
            wholes[which].at[place.dp]
            if which == count
            else wholes[which].at[pl.ds(pl.multiple_of(place.dp * rows, 16), rows)]
        )
        copy = pltpu.make_async_copy(shards[which], target, local_sem.at[which])
        copy.start()
        stays.append(copy)
    order = (count,) + tuple(range(count))
    for which in order:
        for dz in range(1, 4):
            send(which, (0, 0, 0), (dz, 0, 0), dz)
        send(which, (0, 0, 0), (0, 1, 0), 4)
        send(which, (0, 0, 0), (0, 0, 1), 8)
    for turn in range(len(order) + 2):
        if turn < len(order):
            which = order[turn]
            for dz in range(1, 4):
                wait_block(which, (dz, 0, 0))
                send(which, (dz, 0, 0), (0, 1, 0), 4 + dz)
                send(which, (dz, 0, 0), (0, 0, 1), 8 + dz)
                pass_on(which, (dz, 0, 0))
        if 1 <= turn < len(order) + 1:
            which = order[turn - 1]
            for dz in range(4):
                wait_block(which, (dz, 1, 0))
                send(which, (dz, 1, 0), (0, 0, 1), 12 + dz)
                pass_on(which, (dz, 1, 0))
        if 2 <= turn:
            which = order[turn - 2]
            for da in range(2):
                for dz in range(4):
                    wait_block(which, (dz, da, 1))
                    pass_on(which, (dz, da, 1))
    for copy in started:
        copy.wait_send()
    for copy in stays:
        copy.wait()
    for which in range(count):
        rows, columns = shards[which].shape
        for dz in range(4):
            for da in range(2):
                for db in range(2):
                    if index_of(dz, da, db) == 0:
                        continue
                    block = (
                        (place.z + dz) % 4 * 4
                        + (place.b + da) % 2 * place.stride_b
                        + (place.a + db) % 2 * place.stride_a
                    )
                    arrived = wholes[which].at[
                        pl.ds(pl.multiple_of(block * rows, 16), rows),
                        pl.ds(pl.multiple_of((1 - core) * (columns // 2), 128), columns // 2),
                    ]
                    pltpu.make_async_copy(
                        arrived, arrived, other_sem.at[which, index_of(dz, da, db)]
                    ).wait()


def gather_blocks(matrices, small):
    count = len(matrices)
    operands = (*matrices, small)
    shapes = [
        jax.ShapeDtypeStruct((16 * m.shape[0], m.shape[1]), m.dtype) for m in matrices
    ] + [jax.ShapeDtypeStruct((16, *small.shape), small.dtype)]
    dma = pltpu.SemaphoreType.DMA
    return pl.pallas_call(
        functools.partial(gather_kernel, count),
        out_shape=shapes,
        in_specs=[pl.BlockSpec(memory_space=pltpu.HBM)] * (count + 1),
        out_specs=[pl.BlockSpec(memory_space=pltpu.HBM)] * (count + 1),
        scratch_shapes=[
            dma((count + 1,)),
            dma((count + 1, 16)),
            dma((count + 1, 16)),
            dma((count + 1, 16)),
            dma((count + 1, 16)),
        ],
        compiler_params=pltpu.CompilerParams(collective_id=0, has_side_effects=True),
        name="gather_weights",
    )(*operands)


def reduce_kernel(count, *refs):
    grads, small = refs[:count], refs[count]
    outs, small_out = refs[count + 1 : 2 * count + 1], refs[2 * count + 1]
    refs = refs[2 * count + 2 :]
    from_core, merged, from_b, from_a, from_z = (refs[k * count : (k + 1) * count] for k in range(5))
    small_sums, small_from, send_sem, recv_sem, small_send, small_recv = refs[5 * count :]
    place = Place()
    core = place.core
    enter(place)
    started = []

    def send(which, stage, source, target, device):
        copy = pltpu.make_async_remote_copy(
            src_ref=source,
            dst_ref=target,
            send_sem=send_sem.at[which, stage],
            recv_sem=recv_sem.at[which, stage],
            device_id=device,
            device_id_type=MESH,
        )
        copy.start()
        started.append(copy)
        return copy

    def half(which, side):
        columns = grads[which].shape[1] // 2
        return pl.ds(pl.multiple_of(side * columns, 128), columns)

    def rows_of(which, block):
        rows = grads[which].shape[0] // 16
        return pl.ds(pl.multiple_of(block * rows, 16), rows)

    def to_sibling(which):
        return send(
            which, 0, grads[which].at[:, half(which, 1 - core)], from_core[which], place.sibling()
        )

    def merge_cores(which, copy):
        copy.wait_recv()
        mine = half(which, core)

        def one(block, carry):
            z, b, a = block // 4, (block // place.stride_b) % 2, (block // place.stride_a) % 2
            rows = rows_of(which, block)
            total = grads[which][rows, mine].astype(jnp.float32)
            total = total + from_core[which][rows].astype(jnp.float32)
            merged[which][b, a, z] = total.astype(jnp.bfloat16)
            return carry

        lax.fori_loop(0, 16, one, 0)
        return send(which, 1, merged[which].at[1 - place.b], from_b[which], place.peer(0, 0, 1))

    def merge_b(which, copy):
        copy.wait_recv()

        def one(block, carry):
            a, z = block // 4, block % 4
            total = merged[which][place.b, a, z].astype(jnp.float32)
            total = total + from_b[which][a, z].astype(jnp.float32)
            from_b[which][a, z] = total.astype(jnp.bfloat16)
            return carry

        lax.fori_loop(0, 8, one, 0)
        return send(which, 2, from_b[which].at[1 - place.a], from_a[which], place.peer(0, 1, 0))

    def merge_a(which, copy):
        copy.wait_recv()

        def one(z, carry):
            total = from_b[which][place.a, z].astype(jnp.float32)
            total = total + from_a[which][z].astype(jnp.float32)
            from_a[which][z] = total.astype(jnp.bfloat16)
            return carry

        lax.fori_loop(0, 4, one, 0)
        return [
            send(
                which,
                2 + dz,
                from_a[which].at[(place.z + dz) % 4],
                from_z[which].at[dz - 1],
                place.peer(dz, 0, 0),
            )
            for dz in range(1, 4)
        ]

    def finish(which, copies):
        for copy in copies:
            copy.wait_recv()
        total = from_a[which][place.z].astype(jnp.float32)
        for slot in range(3):
            total = total + from_z[which][slot].astype(jnp.float32)
        mine = half(which, core)
        outs[which][:, mine] = total
        window = outs[which].at[:, mine]
        return send(which, 6, window, window, place.sibling())

    def send_small(slot, source, target, device):
        copy = pltpu.make_async_remote_copy(
            src_ref=source,
            dst_ref=target,
            send_sem=small_send.at[slot],
            recv_sem=small_recv.at[slot],
            device_id=device,
            device_id_type=MESH,
        )
        copy.start()
        started.append(copy)
        return copy

    def reduce_small():
        flip_x = (place.dp + 1 - 2 * (place.dp % 2), core)
        flip_y = (place.dp + 2 - 4 * ((place.dp // 2) % 2), core)
        current = small
        for slot, device in enumerate((place.sibling(), flip_x, flip_y)):
            copy = send_small(slot, current.at[...], small_from.at[slot], device)
            copy.wait_recv()
            small_sums[slot] = current[...] + small_from[slot]
            current = small_sums.at[slot]
            yield
        copies = [
            send_small(2 + dz, current.at[...], small_from.at[2 + dz], place.peer(dz, 0, 0))
            for dz in range(1, 4)
        ]
        for copy in copies:
            copy.wait_recv()
        total = jnp.zeros(small.shape, jnp.float32)
        small_from[2] = current[...]
        for z in range(4):
            total = total + small_from[2 + (place.z + 4 - z) % 4]
        small_out[...] = total
        yield

    tiny = reduce_small()
    flight = [to_sibling(which) for which in range(count)]
    steps = (merge_cores, merge_b, merge_a, finish)
    for turn in range(count + len(steps) - 1):
        next(tiny, None)
        for stage in range(len(steps)):
            which = turn - stage
            if 0 <= which < count:
                flight[which] = steps[stage](which, flight[which])
    for copy in flight:
        copy.wait_recv()
    for copy in started:
        copy.wait_send()


def reduce_blocks(grads, small):
    count = len(grads)
    dma = pltpu.SemaphoreType.DMA
    blocks = [(g.shape[0] // 16, g.shape[1]) for g in grads]

    def stages(*lead):
        return [pltpu.VMEM((*lead, rows, columns // 2), jnp.bfloat16) for rows, columns in blocks]

    scratch = [pltpu.VMEM((g.shape[0], g.shape[1] // 2), jnp.bfloat16) for g in grads]
    scratch += stages(2, 2, 4) + stages(2, 4) + stages(4) + stages(3)
    scratch += [
        pltpu.VMEM((3, *small.shape), jnp.float32),
        pltpu.VMEM((6, *small.shape), jnp.float32),
        dma((count, 7)),
        dma((count, 7)),
        dma((6,)),
        dma((6,)),
    ]
    return pl.pallas_call(
        functools.partial(reduce_kernel, count),
        out_shape=[jax.ShapeDtypeStruct(block, jnp.float32) for block in blocks]
        + [jax.ShapeDtypeStruct(small.shape, jnp.float32)],
        in_specs=[pl.BlockSpec(memory_space=pltpu.VMEM)] * (count + 1),
        out_specs=[pl.BlockSpec(memory_space=pltpu.VMEM)] * (count + 1),
        scratch_shapes=scratch,
        compiler_params=pltpu.CompilerParams(
            collective_id=1, has_side_effects=True, vmem_limit_bytes=58 * MIB
        ),
        name="reduce_grads",
    )(*grads, small)


GELU_A = 0.7978845608028654
GELU_B = 0.044715


def nt(left, right):
    return lax.dot_general(left, right, (((1,), (1,)), ((), ())), preferred_element_type=jnp.float32)


def tn(left, right):
    return lax.dot_general(left, right, (((0,), (0,)), ((), ())), preferred_element_type=jnp.float32)


def nn(left, right):
    return jnp.dot(left, right, preferred_element_type=jnp.float32)


def normalize(values):
    center = jnp.mean(values, axis=-1, keepdims=True)
    centered = values - center
    spread = jnp.mean(centered * centered, axis=-1, keepdims=True)
    scale = lax.rsqrt(spread + 1e-05)
    return centered * scale, scale


def normalize_back(grad, normed, scale, gain):
    weighted = grad * gain
    inner = weighted - jnp.mean(weighted, axis=-1, keepdims=True)
    inner = inner - normed * jnp.mean(weighted * normed, axis=-1, keepdims=True)
    return scale * inner


def ffn_kernel(
    tiles, lengths, normed, cotangent, resid, gain, up, down,
    mixed, resid_grad, vectors, up_grad, down_grad,
    grad_low, normed_t, out_sum, in_sum,
):
    step = pl.program_id(0)
    slots, block_len = cotangent.shape[0], cotangent.shape[1]

    @pl.when(step == 0)
    def _():
        base = lax.axis_index("seq") * block_len
        spots = base + lax.broadcasted_iota(jnp.int32, (block_len, 1), 0)
        for slot in range(slots):
            keep = (spots < lengths[slot]).astype(jnp.float32)
            grad_low[slot * block_len : (slot + 1) * block_len] = (
                cotangent[slot].astype(jnp.float32) * keep
            ).astype(jnp.bfloat16)
        normed_t[...] = normed[...].T
        out_sum[...] = resid[...]
        in_sum[...] = jnp.zeros_like(in_sum)

    pre = nn(normed[...], up[...])
    wide = nt(grad_low[...], down[...])
    square = pre * pre
    ramp = jnp.tanh(pre * (GELU_A + (GELU_A * GELU_B) * square))
    half = 0.5 + 0.5 * ramp
    slope = half + (0.5 * pre) * (1.0 - ramp * ramp) * (GELU_A + (3.0 * GELU_A * GELU_B) * square)
    act = (pre * half).astype(jnp.bfloat16)
    back = (wide * slope).astype(jnp.bfloat16)
    out_sum[...] += nn(act, down[...])
    in_sum[...] += nt(back, up[...])
    up_grad[...] = nn(normed_t[...], back).astype(jnp.bfloat16)
    down_grad[...] = tn(act, grad_low[...]).astype(jnp.bfloat16)

    @pl.when(step == tiles - 1)
    def _():
        gain_row = gain[...]
        sums = jnp.zeros((2, resid.shape[1]), jnp.float32)
        for slot in range(slots):
            rows = slice(slot * block_len, (slot + 1) * block_len)
            mixed[slot] = out_sum[rows].astype(jnp.bfloat16)
            hat, scale = normalize(resid[rows])
            grad = in_sum[rows]
            sums = sums + jnp.concatenate(
                [jnp.sum(grad * hat, axis=0, keepdims=True), jnp.sum(grad, axis=0, keepdims=True)],
                axis=0,
            )
            resid_grad[rows] = grad_low[rows].astype(jnp.float32) + normalize_back(
                grad, hat, scale, gain_row
            )
        vectors[...] = sums


def feed_forward(normed, cotangent, resid, gain, up_full, down_full, lengths, tiles=6):
    tokens, width = normed.shape
    hidden = up_full.shape[1]
    tile = hidden // tiles
    whole = lambda *shape: pl.BlockSpec(shape, lambda i, *_: (0,) * len(shape))
    return pl.pallas_call(
        functools.partial(ffn_kernel, tiles),
        grid_spec=pltpu.PrefetchScalarGridSpec(
            num_scalar_prefetch=1,
            grid=(tiles,),
            in_specs=[
                whole(tokens, width),
                whole(*cotangent.shape),
                whole(tokens, width),
                whole(1, width),
                pl.BlockSpec((width, tile), lambda i, *_: (0, i)),
                pl.BlockSpec((tile, width), lambda i, *_: (i, 0)),
            ],
            out_specs=[
                whole(*cotangent.shape),
                whole(tokens, width),
                whole(2, width),
                pl.BlockSpec((width, tile), lambda i, *_: (0, i)),
                pl.BlockSpec((tile, width), lambda i, *_: (i, 0)),
            ],
            scratch_shapes=[
                pltpu.VMEM((tokens, width), jnp.bfloat16),
                pltpu.VMEM((width, tokens), jnp.bfloat16),
                pltpu.VMEM((tokens, width), jnp.float32),
                pltpu.VMEM((tokens, width), jnp.float32),
            ],
        ),
        out_shape=[
            jax.ShapeDtypeStruct(cotangent.shape, jnp.bfloat16),
            jax.ShapeDtypeStruct((tokens, width), jnp.float32),
            jax.ShapeDtypeStruct((2, width), jnp.float32),
            jax.ShapeDtypeStruct((width, hidden), jnp.bfloat16),
            jax.ShapeDtypeStruct((hidden, width), jnp.bfloat16),
        ],
        compiler_params=pltpu.CompilerParams(vmem_limit_bytes=56 * MIB),
        name="feed_forward",
    )(lengths, normed, cotangent, resid, gain, up_full, down_full)


PAIR = 2 * HEAD_DIM


def lanes(pair):
    return pl.ds(pl.multiple_of(pair * PAIR, PAIR), PAIR)


def head_mask(rows, side):
    spots = lax.broadcasted_iota(jnp.int32, (rows, PAIR), 1)
    return (spots // HEAD_DIM) == side


def only(mask, values):
    return jnp.where(mask, values, jnp.zeros_like(values))


def same_head():
    first = lax.broadcasted_iota(jnp.int32, (PAIR, PAIR), 0) // HEAD_DIM
    second = lax.broadcasted_iota(jnp.int32, (PAIR, PAIR), 1) // HEAD_DIM
    return first == second


def lower(size):
    return lax.broadcasted_iota(jnp.int32, (size, size), 0) >= lax.broadcasted_iota(
        jnp.int32, (size, size), 1
    )


def split(values):
    high = values.astype(jnp.bfloat16)
    low = (values - high.astype(jnp.float32)).astype(jnp.bfloat16)
    return high, low


def spots_of(block_len):
    return lax.broadcasted_iota(jnp.int32, (block_len, 1), 0).astype(jnp.float32)


def meet_sibling(place):
    barrier = pltpu.get_barrier_semaphore()
    pl.semaphore_signal(barrier, inc=1, device_id=place.sibling(), device_id_type=MESH)
    pl.semaphore_wait(barrier, 1)


def to_core(place, source, target, send_sem, recv_sem):
    return pltpu.make_async_remote_copy(
        src_ref=source,
        dst_ref=target,
        send_sem=send_sem,
        recv_sem=recv_sem,
        device_id=place.sibling(),
        device_id_type=MESH,
    )


def shifted_keys(keys, slot, window, taps):
    block_len = keys.shape[1] - 8
    total = taps[0:1] * keys[slot, 8 : 8 + block_len, window]
    for lag in range(1, 4):
        total = total + taps[lag : lag + 1] * keys[slot, 8 - lag : 8 - lag + block_len, window]
    return total


ROW_RATE, ROW_TAPS = 2, 5


def mixer_kernel(
    tokens, vectors, qkv_weight, out_weight,
    normed, queries, key_rows, values, edges, state_in, mixed, resid, normed_two,
    keys, summed, state_out, send_sem, recv_sem,
):
    slots, block_len, width = tokens.shape
    pairs = width // PAIR
    size = block_len // 2
    place = Place()
    meet_sibling(place)
    first = place.core == 0
    gain, bias = vectors[0:1], vectors[1:2]

    for slot in range(slots):
        rows = slice(slot * block_len, (slot + 1) * block_len)
        hat, _ = normalize(tokens[slot].astype(jnp.float32))
        normed[rows] = (hat * gain + bias).astype(jnp.bfloat16)

    def project(third, target):
        for slot in range(slots):
            rows = slice(slot * block_len, (slot + 1) * block_len)
            target[slot] = nn(
                normed[rows], qkv_weight[:, third * width : (third + 1) * width]
            ).astype(jnp.bfloat16)

    project(1, key_rows)
    edge_copy = to_core(
        place, key_rows.at[:, pl.ds(block_len - 16, 16)], edges, send_sem.at[0], recv_sem.at[0]
    )

    @pl.when(first)
    def _():
        edge_copy.start()

    project(2, values)
    project(0, queries)

    @pl.when(first)
    def _():
        edge_copy.wait_send()
        edges[...] = jnp.zeros_like(edges)

    @pl.when(place.core == 1)
    def _():
        edge_copy.wait_recv()

    for slot in range(slots):
        keys[slot, 0:8] = edges[slot].astype(jnp.float32)[8:16]
        keys[slot, 8:] = key_rows[slot].astype(jnp.float32)
    spots = spots_of(block_len)
    state_copy = to_core(place, state_out, state_in, send_sem.at[1], recv_sem.at[1])

    @pl.when(first)
    def _():
        def fresh(pair, carry):
            window = lanes(pair)
            rate = vectors[ROW_RATE : ROW_RATE + 1, window]
            taps = vectors[ROW_TAPS : ROW_TAPS + 4, window]
            tail = jnp.exp(-rate * (block_len - 1.0 - spots))
            for slot in range(slots):
                tail_keys = (shifted_keys(keys, slot, window, taps) * tail).astype(jnp.bfloat16)
                state_out[pair, slot] = only(same_head(), tn(tail_keys, values[slot, :, window]))
            return carry

        lax.fori_loop(0, pairs, fresh, 0)
        state_copy.start()

    def within(pair, carry):
        window = lanes(pair)
        rate = vectors[ROW_RATE : ROW_RATE + 1, window]
        taps = vectors[ROW_TAPS : ROW_TAPS + 4, window]
        fall = jnp.exp(-rate * spots)
        rise = jnp.exp(rate * spots)
        for slot in range(slots):
            decayed = (queries[slot, :, window].astype(jnp.float32) * fall).astype(jnp.bfloat16)
            lifted = (shifted_keys(keys, slot, window, taps) * rise).astype(jnp.bfloat16)
            value = values[slot, :, window]
            top = jnp.zeros((size, PAIR), jnp.float32)
            low = jnp.zeros((size, PAIR), jnp.float32)
            for side in range(2):
                query_side = only(head_mask(block_len, side), decayed)
                value_side = only(head_mask(block_len, side), value)
                near = jnp.where(lower(size), nt(query_side[:size], lifted[:size]), 0.0)
                top = top + nn(near.astype(jnp.bfloat16), value_side[:size])
                far = nt(query_side[size:], lifted[:size]).astype(jnp.bfloat16)
                near = jnp.where(lower(size), nt(query_side[size:], lifted[size:]), 0.0)
                low = low + nn(far, value_side[:size]) + nn(near.astype(jnp.bfloat16), value_side[size:])
            summed[slot, :size, window] = top
            summed[slot, size:, window] = low
        return carry

    lax.fori_loop(0, pairs, within, 0)

    @pl.when(first)
    def _():
        state_copy.wait_send()
        state_in[...] = jnp.zeros_like(state_in)

    @pl.when(place.core == 1)
    def _():
        state_copy.wait_recv()

        def reach(pair, carry):
            window = lanes(pair)
            rate = vectors[ROW_RATE : ROW_RATE + 1, window]
            decay = jnp.exp(-rate * (spots + 1.0))
            for slot in range(slots):
                reaching = (queries[slot, :, window].astype(jnp.float32) * decay).astype(jnp.bfloat16)
                high, low = split(state_in[pair, slot])
                summed[slot, :, window] += nn(reaching, high) + nn(reaching, low)
            return carry

        lax.fori_loop(0, pairs, reach, 0)

    gain_two, bias_two = vectors[3:4], vectors[4:5]
    for slot in range(slots):
        rows = slice(slot * block_len, (slot + 1) * block_len)
        mixed[rows] = summed[slot].astype(jnp.bfloat16)
        total = tokens[slot].astype(jnp.float32) + nn(mixed[rows], out_weight[...])
        resid[rows] = total
        hat, _ = normalize(total)
        normed_two[rows] = (hat * gain_two + bias_two).astype(jnp.bfloat16)


def mixer_forward(tokens, vectors, qkv_weight, out_weight):
    slots, block_len, width = tokens.shape
    count = slots * block_len
    pairs = width // PAIR
    low, wide = jnp.bfloat16, jnp.float32
    shape = jax.ShapeDtypeStruct
    vmem = pl.BlockSpec(memory_space=pltpu.VMEM)
    outs = [
        shape((count, width), low),
        shape((slots, block_len, width), low),
        shape((slots, block_len, width), low),
        shape((slots, block_len, width), low),
        shape((slots, 16, width), low),
        shape((pairs, slots, PAIR, PAIR), wide),
        shape((count, width), low),
        shape((count, width), wide),
        shape((count, width), low),
    ]
    return pl.pallas_call(
        mixer_kernel,
        out_shape=outs,
        in_specs=[vmem] * 4,
        out_specs=[vmem] * len(outs),
        scratch_shapes=[
            pltpu.VMEM((slots, block_len + 8, width), wide),
            pltpu.VMEM((slots, block_len, width), wide),
            pltpu.VMEM((pairs, slots, PAIR, PAIR), wide),
            pltpu.SemaphoreType.DMA((2,)),
            pltpu.SemaphoreType.DMA((2,)),
        ],
        compiler_params=pltpu.CompilerParams(
            collective_id=2, has_side_effects=True, vmem_limit_bytes=56 * MIB
        ),
        name="mixer_forward",
    )(tokens, vectors, qkv_weight, out_weight)


def mixer_back_kernel(
    resid_grad, mixed, queries, key_rows, values, edges, state_in, normed, tokens, vectors,
    qkv_weight, out_weight,
    input_grad, out_grad, qkv_grad, small,
    keys, branch, back_rows, projected, key_back, turned, state_send, state_grad, send_sem, recv_sem,
):
    slots, block_len, width = tokens.shape
    pairs = width // PAIR
    size = block_len // 2
    low_type = jnp.bfloat16
    place = Place()
    meet_sibling(place)
    first = place.core == 0
    spots = spots_of(block_len)

    for slot in range(slots):
        rows = slice(slot * block_len, (slot + 1) * block_len)
        branch[rows] = resid_grad[rows].astype(low_type)
        back_rows[slot] = nt(branch[rows], out_weight[...]).astype(low_type)
    state_copy = to_core(place, state_send, state_grad, send_sem.at[0], recv_sem.at[0])

    @pl.when(place.core == 1)
    def _():
        def gather_state(pair, carry):
            window = lanes(pair)
            rate = vectors[ROW_RATE : ROW_RATE + 1, window]
            decay = jnp.exp(-rate * (spots + 1.0))
            for slot in range(slots):
                reaching = (queries[slot, :, window].astype(jnp.float32) * decay).astype(low_type)
                back = back_rows[slot, :, window]
                state_send[pair, slot] = only(same_head(), tn(reaching, back)).astype(low_type)
            return carry

        lax.fori_loop(0, pairs, gather_state, 0)
        state_copy.start()

    turned[...] = mixed[...].T
    out_grad[...] = nn(turned[...], branch[...]).astype(low_type)
    for slot in range(slots):
        keys[slot, 0:8] = edges[slot].astype(jnp.float32)[8:16]
        keys[slot, 8:] = key_rows[slot].astype(jnp.float32)

    @pl.when(place.core == 1)
    def _():
        state_copy.wait_send()
        state_grad[...] = jnp.zeros_like(state_grad)

    @pl.when(first)
    def _():
        state_copy.wait_recv()

    def back_pair(pair, carry):
        window = lanes(pair)
        rate = vectors[ROW_RATE : ROW_RATE + 1, window]
        taps = vectors[ROW_TAPS : ROW_TAPS + 4, window]
        fall = jnp.exp(-rate * spots)
        rise = jnp.exp(rate * spots)
        tail = jnp.exp(-rate * (block_len - 1.0 - spots))
        decay = jnp.exp(-rate * (spots + 1.0))
        rate_grad = jnp.zeros((1, PAIR), jnp.float32)
        taps_grad = [jnp.zeros((1, PAIR), jnp.float32) for _ in range(4)]
        for slot in range(slots):
            query = queries[slot, :, window].astype(jnp.float32)
            key = shifted_keys(keys, slot, window, taps)
            value = values[slot, :, window]
            back = back_rows[slot, :, window]
            wide_decayed, wide_lifted = query * fall, key * rise
            wide_tail, wide_reach = key * tail, query * decay
            decayed, lifted = wide_decayed.astype(low_type), wide_lifted.astype(low_type)
            tail_keys = wide_tail.astype(low_type)
            decayed_turned, back_turned = decayed.T, back.T
            decayed_top = jnp.zeros((size, PAIR), jnp.float32)
            decayed_low = jnp.zeros((size, PAIR), jnp.float32)
            lifted_top = jnp.zeros((PAIR, size), jnp.float32)
            lifted_low = jnp.zeros((PAIR, size), jnp.float32)
            value_top = jnp.zeros((PAIR, size), jnp.float32)
            value_low = jnp.zeros((PAIR, size), jnp.float32)
            row_head = lax.broadcasted_iota(jnp.int32, (PAIR, block_len), 0) // HEAD_DIM
            for side in range(2):
                mask = head_mask(block_len, side)
                query_side, back_side = only(mask, decayed), only(mask, back)
                lifted_side = only(mask, lifted)
                query_turned = only(row_head == side, decayed_turned)
                back_side_turned = only(row_head == side, back_turned)
                causal = lower(size)
                halves = (slice(0, size), slice(size, block_len))
                for t, s in ((0, 0), (1, 0), (1, 1)):
                    score = nt(query_side[halves[t]], lifted[halves[s]])
                    grad = nt(back_side[halves[t]], value[halves[s]])
                    if t == s:
                        score, grad = jnp.where(causal, score, 0.0), jnp.where(causal, grad, 0.0)
                    score, grad = score.astype(low_type), grad.astype(low_type)
                    query_part = nn(grad, lifted_side[halves[s]])
                    lifted_part = nn(query_turned[:, halves[t]], grad)
                    value_part = nn(back_side_turned[:, halves[t]], score)
                    if t == 0:
                        decayed_top = decayed_top + query_part
                    else:
                        decayed_low = decayed_low + query_part
                    if s == 0:
                        lifted_top, value_top = lifted_top + lifted_part, value_top + value_part
                    else:
                        lifted_low, value_low = lifted_low + lifted_part, value_low + value_part
            decayed_grad = jnp.concatenate([decayed_top, decayed_low], axis=0)
            lifted_grad = jnp.concatenate([lifted_top.T, lifted_low.T], axis=0)
            value_grad = jnp.concatenate([value_top.T, value_low.T], axis=0)
            leaving = state_grad[pair, slot]
            entering = state_in[pair, slot]
            high, low = split(entering)
            value_grad = value_grad + nn(tail_keys, leaving)
            tail_grad = nt(value, leaving)
            reach_grad = nt(back, high) + nt(back, low)
            carry_grad = jnp.sum((leaving.astype(jnp.float32) * entering).T, axis=0, keepdims=True)
            key_grad = lifted_grad * rise + tail_grad * tail
            steps = (
                spots * (lifted_grad * wide_lifted - decayed_grad * wide_decayed)
                - (block_len - 1.0 - spots) * (tail_grad * wide_tail)
                - (spots + 1.0) * (reach_grad * wide_reach)
            )
            rate_grad = rate_grad + jnp.sum(steps, axis=0, keepdims=True)
            rate_grad = rate_grad - block_len * jnp.exp(-rate * block_len) * carry_grad
            projected[0, slot, :, window] = (decayed_grad * fall + reach_grad * decay).astype(low_type)
            projected[2, slot, :, window] = value_grad.astype(low_type)
            key_back[slot, 0:block_len, window] = key_grad
            for lag in range(4):
                lagged = keys[slot, 8 - lag : 8 - lag + block_len, window]
                taps_grad[lag] = taps_grad[lag] + jnp.sum(lagged * key_grad, axis=0, keepdims=True)
        small[0:8, window] = jnp.concatenate(
            [jnp.zeros((2, PAIR), jnp.float32), rate_grad, *taps_grad, jnp.zeros((1, PAIR), jnp.float32)],
            axis=0,
        )
        return carry

    lax.fori_loop(0, pairs, back_pair, 0)
    spill = to_core(
        place,
        key_back.at[:, pl.ds(0, 8)],
        key_back.at[:, pl.ds(block_len, 8)],
        send_sem.at[1],
        recv_sem.at[1],
    )

    @pl.when(place.core == 1)
    def _():
        spill.start()
        key_back[:, block_len : block_len + 8] = jnp.zeros((slots, 8, width), jnp.float32)

    turned[...] = normed[...].T

    def weight_grad(third):
        for slot in range(1):
            rows = projected[third].reshape(slots * block_len, width)
            qkv_grad[:, third * width : (third + 1) * width] = nn(turned[...], rows).astype(low_type)

    weight_grad(2)
    weight_grad(0)

    @pl.when(first)
    def _():
        spill.wait_recv()

    def key_pair(pair, carry):
        window = lanes(pair)
        taps = vectors[ROW_TAPS : ROW_TAPS + 4, window]
        for slot in range(slots):
            total = taps[0:1] * key_back[slot, 0:block_len, window]
            for lag in range(1, 4):
                total = total + taps[lag : lag + 1] * key_back[slot, lag : lag + block_len, window]
            projected[1, slot, :, window] = total.astype(low_type)
        return carry

    lax.fori_loop(0, pairs, key_pair, 0)
    weight_grad(1)
    gain = vectors[0:1]
    sums = jnp.zeros((2, width), jnp.float32)
    for slot in range(slots):
        rows = slice(slot * block_len, (slot + 1) * block_len)
        grad = nt(projected[0, slot], qkv_weight[:, 0:width])
        for third in range(1, 3):
            grad = grad + nt(projected[third, slot], qkv_weight[:, third * width : (third + 1) * width])
        hat, scale = normalize(tokens[slot].astype(jnp.float32))
        sums = sums + jnp.concatenate(
            [jnp.sum(grad * hat, axis=0, keepdims=True), jnp.sum(grad, axis=0, keepdims=True)], axis=0
        )
        input_grad[slot] = resid_grad[rows] + normalize_back(grad, hat, scale, gain)
    small[0:2] = sums

    @pl.when(place.core == 1)
    def _():
        spill.wait_send()


def mixer_backward(
    resid_grad, mixed, queries, key_rows, values, edges, state_in, normed, tokens, vectors,
    qkv_weight, out_weight,
):
    slots, block_len, width = tokens.shape
    count = slots * block_len
    pairs = width // PAIR
    low, wide = jnp.bfloat16, jnp.float32
    shape = jax.ShapeDtypeStruct
    vmem = pl.BlockSpec(memory_space=pltpu.VMEM)
    outs = [
        shape(tokens.shape, wide),
        shape((width, width), low),
        shape((width, 3 * width), low),
        shape((8, width), wide),
    ]
    return pl.pallas_call(
        mixer_back_kernel,
        out_shape=outs,
        in_specs=[vmem] * 12,
        out_specs=[vmem] * len(outs),
        scratch_shapes=[
            pltpu.VMEM((slots, block_len + 8, width), wide),
            pltpu.VMEM((count, width), low),
            pltpu.VMEM((slots, block_len, width), low),
            pltpu.VMEM((3, slots, block_len, width), low),
            pltpu.VMEM((slots, block_len + 8, width), wide),
            pltpu.VMEM((width, count), low),
            pltpu.VMEM((pairs, slots, PAIR, PAIR), low),
            pltpu.VMEM((pairs, slots, PAIR, PAIR), low),
            pltpu.SemaphoreType.DMA((2,)),
            pltpu.SemaphoreType.DMA((2,)),
        ],
        compiler_params=pltpu.CompilerParams(
            collective_id=3, has_side_effects=True, vmem_limit_bytes=58 * MIB
        ),
        name="mixer_backward",
    )(
        resid_grad, mixed, queries, key_rows, values, edges, state_in, normed, tokens, vectors,
        qkv_weight, out_weight,
    )


def from_behind(value, axis, steps):
    count = lax.axis_size(axis)
    leading, last = (max(0, -steps), min(count, count - steps))
    return lax.ppermute(value, axis, [(source, source + steps) for source in range(leading, last)])


def as_sent(array):

    def short(part):
        return part.astype(jnp.bfloat16) if part.dtype == jnp.float32 else part

    return jax.tree.map(short, array)


def layer_norm(values, norm_gain, offset):
    center = jnp.mean(values, axis=-1, keepdims=True)
    centered = values - center
    spread = jnp.mean(centered * centered, axis=-1, keepdims=True)
    return centered * lax.rsqrt(spread + 1e-05) * norm_gain + offset


def shift_mix(extended, tap_table):
    block_len = extended.shape[-2] - 3
    mixed_sum = tap_table[0] * extended[..., 3 : 3 + block_len, :]
    for lag_step in range(1, 4):
        mixed_sum = (
            mixed_sum
            + tap_table[lag_step] * extended[..., 3 - lag_step : 3 - lag_step + block_len, :]
        )
    return mixed_sum


def factors(queries, key_rows, rate_vector):
    block_len = queries.shape[1]
    rate_grid = rate_vector.reshape(queries.shape[2], -1)
    positions = jnp.arange(block_len, dtype=jnp.float32)[:, None, None]
    decayed = queries * jnp.exp(-rate_grid * positions)
    lifted = key_rows * jnp.exp(rate_grid * positions)
    tail_keys = key_rows * jnp.exp(-rate_grid * (block_len - 1.0 - positions))
    reaching = queries * jnp.exp(-rate_grid * (positions + 1.0))
    carry_decay = jnp.exp(-rate_grid * block_len)
    return (decayed, lifted, tail_keys, reaching, carry_decay)


def outer_sum(left_rows, right_rows):
    return lax.dot_general(
        left_rows, right_rows, (((0,), (0,)), ((), ())), preferred_element_type=jnp.float32
    )


def back_product(grad_rows, weight):
    return lax.dot_general(
        grad_rows, weight, (((1,), (1,)), ((), ())), preferred_element_type=jnp.float32
    )


def general(
    tokens,
    ln1_gain,
    ln1_bias,
    qkv_weight,
    shift_taps,
    decay_rates,
    out_weight,
    ln2_gain,
    ln2_bias,
    up_weight,
    down_weight,
    lengths,
    out_grad,
):
    slot_count, block_len, model_width = tokens.shape
    token_count = slot_count * block_len
    gathered = (
        lax.all_gather(ln1_gain, "dp", axis=0, tiled=True),
        lax.all_gather(ln1_bias, "dp", axis=0, tiled=True),
        lax.all_gather(qkv_weight, "dp", axis=0, tiled=True),
        lax.all_gather(shift_taps, "dp", axis=1, tiled=True),
        lax.all_gather(decay_rates, "dp", axis=0, tiled=True),
        lax.all_gather(out_weight, "dp", axis=0, tiled=True),
        lax.all_gather(ln2_gain, "dp", axis=0, tiled=True),
        lax.all_gather(ln2_bias, "dp", axis=0, tiled=True),
        lax.all_gather(up_weight, "dp", axis=0, tiled=True),
        lax.all_gather(down_weight, "dp", axis=0, tiled=True),
    )
    gain_one = gathered[0].astype(jnp.float32)
    bias_one = gathered[1].astype(jnp.float32)
    tap_table = gathered[3].astype(jnp.float32)
    rate_vector = gathered[4].astype(jnp.float32)
    gain_two = gathered[6].astype(jnp.float32)
    bias_two = gathered[7].astype(jnp.float32)
    qkv_full = gathered[2]
    out_full = gathered[5]
    up_full = gathered[8]
    down_full = gathered[9]
    inputs = tokens.reshape(token_count, model_width).astype(jnp.float32)
    normed_one = layer_norm(inputs, gain_one, bias_one).astype(jnp.bfloat16)
    projected = jnp.dot(normed_one, qkv_full, preferred_element_type=jnp.float32).astype(
        jnp.bfloat16
    )
    projected = projected.reshape(slot_count, block_len, 3 * model_width)
    key_rows = projected[:, :, model_width : 2 * model_width]
    edge_rows = from_behind(key_rows[:, block_len - 3 :], "seq", 1)
    extended = jnp.concatenate([edge_rows, key_rows], axis=1).astype(jnp.float32)
    shifted = shift_mix(extended, tap_table)
    head_shape = (slot_count, block_len, HEADS, HEAD_DIM)
    flat_shape = (slot_count, block_len, model_width)
    head_queries = projected[:, :, :model_width].astype(jnp.float32).reshape(head_shape)
    head_keys = shifted.reshape(head_shape)
    head_values = projected[:, :, 2 * model_width :].reshape(head_shape)
    decayed, lifted, tail_keys, reaching, carry_decay = factors(
        head_queries, head_keys, rate_vector
    )
    decayed_low = decayed.astype(jnp.bfloat16)
    lifted_low = lifted.astype(jnp.bfloat16)
    tail_low = tail_keys.astype(jnp.bfloat16)
    reach_wide = reaching.astype(jnp.bfloat16).astype(jnp.float32)
    position_ids = jnp.arange(block_len)
    causal = position_ids[:, None] >= position_ids[None, :]
    scores = jnp.einsum(
        "bthk,bshk->bhts", decayed_low, lifted_low, preferred_element_type=jnp.float32
    )
    scores_low = jnp.where(causal, scores, 0.0).astype(jnp.bfloat16)
    within = jnp.einsum(
        "bhts,bshv->bthv", scores_low, head_values, preferred_element_type=jnp.float32
    )
    fresh_state = jnp.einsum(
        "bshk,bshv->bhkv", tail_low, head_values, preferred_element_type=jnp.float32
    )
    empty_state = jnp.zeros_like(fresh_state)
    state_in = empty_state
    for relay_turn in range(lax.axis_size("seq") - 1):
        state_in = from_behind(carry_decay[None, :, :, None] * state_in + fresh_state, "seq", 1)
    inter = jnp.einsum("bthk,bhkv->bthv", reach_wide, state_in, precision=precise)
    mixer = (within + inter).reshape(token_count, model_width).astype(jnp.bfloat16)
    resid = inputs + jnp.dot(mixer, out_full, preferred_element_type=jnp.float32)
    normed_two = layer_norm(resid, gain_two, bias_two).astype(jnp.bfloat16)
    hidden_pre = jnp.dot(normed_two, up_full, preferred_element_type=jnp.float32)
    hidden = jax.nn.gelu(hidden_pre).astype(jnp.bfloat16)
    result = resid + jnp.dot(hidden, down_full, preferred_element_type=jnp.float32)
    mixed = result.reshape(flat_shape).astype(jnp.bfloat16)
    qkv_full, out_full, up_full, down_full = (
        lax.all_gather(qkv_weight, "dp", axis=0, tiled=True),
        lax.all_gather(out_weight, "dp", axis=0, tiled=True),
        lax.all_gather(up_weight, "dp", axis=0, tiled=True),
        lax.all_gather(down_weight, "dp", axis=0, tiled=True),
    )
    positions = lax.axis_index("seq") * block_len + jnp.arange(block_len, dtype=jnp.int32)
    keep_mask = (positions[None, :] < lengths[:, None]).astype(jnp.float32)
    grad_rows = (out_grad.astype(jnp.float32) * keep_mask[:, :, None]).reshape(
        token_count, model_width
    )
    grad_low = grad_rows.astype(jnp.bfloat16)
    down_grad = outer_sum(hidden, grad_low)
    hidden_grad = back_product(grad_low, down_full)
    _, gelu_back = jax.vjp(jax.nn.gelu, hidden_pre)
    pre_grad = gelu_back(hidden_grad)[0].astype(jnp.bfloat16)
    up_grad = outer_sum(normed_two, pre_grad)
    _, norm_two_back = jax.vjp(layer_norm, resid, gain_two, bias_two)
    resid_part, gain_two_grad, bias_two_grad = norm_two_back(back_product(pre_grad, up_full))
    resid_grad = grad_rows + resid_part
    branch_grad = resid_grad.astype(jnp.bfloat16)
    proj_grad = outer_sum(mixer, branch_grad)
    mixer_low = back_product(branch_grad, out_full).astype(jnp.bfloat16).reshape(head_shape)
    mixer_wide = mixer_low.astype(jnp.float32)
    local_grad = jnp.einsum("bthk,bthv->bhkv", reach_wide, mixer_wide, precision=precise)
    state_grad = empty_state
    for relay_turn in range(lax.axis_size("seq") - 1):
        state_grad = from_behind(
            as_sent(carry_decay[None, :, :, None] * state_grad + local_grad), "seq", -1
        )
    score_grad = jnp.einsum(
        "bthv,bshv->bhts", mixer_low, head_values, preferred_element_type=jnp.float32
    ).astype(jnp.bfloat16)
    score_grad = jnp.where(causal, score_grad, jnp.zeros_like(score_grad))
    decayed_grad = jnp.einsum(
        "bhts,bshk->bthk", score_grad, lifted_low, preferred_element_type=jnp.float32
    )
    lifted_grad = jnp.einsum(
        "bhts,bthk->bshk", score_grad, decayed_low, preferred_element_type=jnp.float32
    )
    value_grad = jnp.einsum(
        "bhts,bthv->bshv", scores_low, mixer_low, preferred_element_type=jnp.float32
    )
    value_grad = value_grad + jnp.einsum(
        "bshk,bhkv->bshv", tail_low.astype(jnp.float32), state_grad, precision=precise
    )
    tail_grad = jnp.einsum(
        "bshv,bhkv->bshk", head_values.astype(jnp.float32), state_grad, precision=precise
    )
    reach_grad = jnp.einsum("bthv,bhkv->bthk", mixer_wide, state_in, precision=precise)
    carry_grad = jnp.sum(state_grad * state_in, axis=(0, 3))
    _, factor_back = jax.vjp(factors, head_queries, head_keys, rate_vector)
    query_grad, key_grad, rate_grad = factor_back(
        (decayed_grad, lifted_grad, tail_grad, reach_grad, carry_grad)
    )
    _, shift_back = jax.vjp(shift_mix, extended, tap_table)
    extended_grad, taps_grad = shift_back(key_grad.reshape(flat_shape))
    spill = from_behind(extended_grad[:, :3], "seq", -1)
    keys_grad = jnp.concatenate(
        [extended_grad[:, 3:block_len], extended_grad[:, block_len:] + spill], axis=1
    )
    qkv_grad_low = jnp.concatenate(
        [query_grad.reshape(flat_shape), keys_grad, value_grad.reshape(flat_shape)], axis=2
    )
    qkv_grad_low = qkv_grad_low.reshape(token_count, 3 * model_width).astype(jnp.bfloat16)
    qkv_grad = outer_sum(normed_one, qkv_grad_low)
    _, norm_one_back = jax.vjp(layer_norm, inputs, gain_one, bias_one)
    input_part, gain_one_grad, bias_one_grad = norm_one_back(back_product(qkv_grad_low, qkv_full))
    input_grad = (resid_grad + input_part).reshape(flat_shape)
    reduced = (
        lax.psum_scatter(gain_one_grad, "dp", scatter_dimension=0, tiled=True),
        lax.psum_scatter(bias_one_grad, "dp", scatter_dimension=0, tiled=True),
        lax.psum_scatter(qkv_grad, "dp", scatter_dimension=0, tiled=True),
        lax.psum_scatter(taps_grad, "dp", scatter_dimension=1, tiled=True),
        lax.psum_scatter(rate_grad, "dp", scatter_dimension=0, tiled=True),
        lax.psum_scatter(proj_grad, "dp", scatter_dimension=0, tiled=True),
        lax.psum_scatter(gain_two_grad, "dp", scatter_dimension=0, tiled=True),
        lax.psum_scatter(bias_two_grad, "dp", scatter_dimension=0, tiled=True),
        lax.psum_scatter(up_grad, "dp", scatter_dimension=0, tiled=True),
        lax.psum_scatter(down_grad, "dp", scatter_dimension=0, tiled=True),
    )
    summed = lax.psum(
        (
            reduced[0],
            reduced[1],
            reduced[2],
            reduced[3],
            reduced[4],
            reduced[5],
            reduced[6],
            reduced[7],
            reduced[8],
            reduced[9],
        ),
        "seq",
    )
    return (
        mixed,
        input_grad,
        summed[0],
        summed[1],
        summed[2],
        summed[3],
        summed[4],
        summed[5],
        summed[6],
        summed[7],
        summed[8],
        summed[9],
    )


def near(
    tokens,
    ln1_gain,
    ln1_bias,
    qkv_weight,
    shift_taps,
    decay_rates,
    out_weight,
    ln2_gain,
    ln2_bias,
    up_weight,
    down_weight,
    lengths,
    out_grad,
):
    width = tokens.shape[2]
    part = ln1_gain.shape[0]
    packed = jnp.concatenate(
        [jnp.stack([ln1_gain, ln1_bias, decay_rates, ln2_gain, ln2_bias]), shift_taps], axis=0
    )
    packed = jnp.pad(packed, ((0, 7), (0, 128 - part)))
    qkv_full, out_full, up_full, down_full, wide = gather_blocks(
        (qkv_weight, out_weight, up_weight, down_weight), packed
    )
    vectors = wide[:, :, :part].transpose(1, 0, 2).reshape(16, width).astype(jnp.float32)
    normed, queries, key_rows, values, edges, state_in, mixer, resid, normed_two = mixer_forward(
        tokens, vectors, qkv_full, out_full
    )
    mixed, resid_grad, two_sums, up_grad, down_grad = feed_forward(
        normed_two, out_grad, resid, vectors[3:4], up_full, down_full, lengths
    )
    input_grad, proj_grad, qkv_grad, one_sums = mixer_backward(
        resid_grad, mixer, queries, key_rows, values, edges, state_in, normed, tokens, vectors,
        qkv_full, out_full,
    )
    small = jnp.concatenate([one_sums, two_sums, jnp.zeros((6, width), jnp.float32)], axis=0)
    down_sum, up_sum, proj_sum, qkv_sum, small_sum = reduce_blocks(
        (down_grad, up_grad, proj_grad, qkv_grad), small
    )
    own = lax.dynamic_slice(small_sum, (0, lax.axis_index("dp") * part), (16, part))
    return (
        mixed, input_grad, own[0], own[1], qkv_sum, own[3:7], own[2], proj_sum, own[8], own[9], up_sum, down_sum,
    )


def solution(mesh):
    in_specs = (
        P("dp", "seq", None),
        P("dp"),
        P("dp"),
        P("dp", None),
        P(None, "dp"),
        P("dp"),
        P("dp", None),
        P("dp"),
        P("dp"),
        P("dp", None),
        P("dp", None),
        P("dp"),
        P("dp", "seq", None),
    )
    out_specs = (
        P("dp", "seq", None),
        P("dp", "seq", None),
        P("dp"),
        P("dp"),
        P("dp", None),
        P(None, "dp"),
        P("dp"),
        P("dp", None),
        P("dp"),
        P("dp"),
        P("dp", None),
        P("dp", None),
    )
    local = near if dict(mesh.shape) == {"dp": 16, "seq": 2} else general
    return jax.shard_map(local, mesh=mesh, in_specs=in_specs, out_specs=out_specs, check_vma=False)
```

```python
import functools

import jax
import jax.numpy as jnp
from jax import lax
from jax.experimental import pallas as pl
from jax.experimental.pallas import tpu as pltpu
from jax.sharding import PartitionSpec as P

HEADS = 12
HEAD_DIM = 64
PAIR = 2 * HEAD_DIM
MESH = pl.DeviceIdType.MESH
MIB = 2**20
GELU_A = 0.7978845608028654
GELU_B = 0.044715
ROW_RATE, ROW_TAPS = 2, 5
LOW = jnp.bfloat16
WIDE = jnp.float32


precise = lax.Precision.HIGHEST


class Place:
    def __init__(self):
        self.dp = lax.axis_index("dp")
        self.core = lax.axis_index("seq")
        self.z = self.dp // 4
        self.stride_a = 2 - self.core
        self.stride_b = 1 + self.core
        self.a = (self.dp // self.stride_a) % 2
        self.b = (self.dp // self.stride_b) % 2

    def spot(self, da, db):
        return (self.a + da) % 2 * self.stride_a + (self.b + db) % 2 * self.stride_b

    def sibling_spot(self, da, db):
        return (self.b + da) % 2 * self.stride_b + (self.a + db) % 2 * self.stride_a

    def peer(self, dz, da, db):
        return ((self.z + dz) % 4 * 4 + self.spot(da, db), self.core)

    def sibling(self):
        return (self.dp, 1 - self.core)


PEERS = ((1, 0, 0), (2, 0, 0), (3, 0, 0), (0, 1, 0), (0, 0, 1))


def enter(place):
    barrier = pltpu.get_barrier_semaphore()
    for step in PEERS:
        pl.semaphore_signal(barrier, inc=1, device_id=place.peer(*step), device_id_type=MESH)
    pl.semaphore_signal(barrier, inc=1, device_id=place.sibling(), device_id_type=MESH)
    pl.semaphore_wait(barrier, len(PEERS) + 1)


def remote(source, target, send_sem, recv_sem, device):
    return pltpu.make_async_remote_copy(
        src_ref=source,
        dst_ref=target,
        send_sem=send_sem,
        recv_sem=recv_sem,
        device_id=device,
        device_id_type=MESH,
    )


def part(start, size, step):
    return pl.ds(pl.multiple_of(start, step), size)


class Unit:
    def __init__(self, shard, buffer, rows, lead=None, start=0, width=None, shared=False):
        self.shard, self.buffer, self.rows, self.lead = shard, buffer, rows, lead
        self.start, self.width, self.shared = start, width, shared

    def columns(self, side):
        if self.shared:
            return slice(None)
        return part(self.start + side * (self.width // 2), self.width // 2, 128)

    def own(self, side):
        row, columns = self.shard[1], self.shard[2]
        if self.shared:
            return self.shard[0]
        return self.shard[0].at[
            pl.ds(row, self.rows), part(columns + side * (self.width // 2), self.width // 2, 128)
        ]

    def slab(self, spot, columns):
        rows = part(spot * self.rows, self.rows, 16)
        if self.lead is None:
            return self.buffer.at[:, rows, columns]
        return self.buffer.at[pl.ds(self.lead, 4), rows, columns]

    def block(self, z, spot, columns):
        rows = part(spot * self.rows, self.rows, 16)
        return self.buffer.at[z if self.lead is None else self.lead + z, rows, columns]


class Gather:
    def __init__(self, place, units, send_sem, recv_sem, local_sem):
        self.place, self.units = place, units
        self.send_sem, self.recv_sem, self.local_sem = send_sem, recv_sem, local_sem
        self.events = []
        self.ready = {}
        count = len(units)
        for turn in range(count + 2):
            if turn < count:
                self.events.append(functools.partial(self.after_z, turn))
            if 1 <= turn < count + 1:
                self.events.append(functools.partial(self.after_a, turn - 1))
            if 2 <= turn:
                self.events.append(functools.partial(self.after_b, turn - 2))
                self.ready[turn - 2] = len(self.events)
        self.done = 0

    def tick(self, count=1):
        for event in self.events[self.done : self.done + count]:
            event()
        self.done = min(self.done + count, len(self.events))

    def spread(self, index, trips, each):
        for trip in range(trips):
            chosen = self.events[self.done : self.done + each]
            self.done += len(chosen)
            if chosen:
                @pl.when(index == trip)
                def _(chosen=chosen):
                    for event in chosen:
                        event()

    def need(self, which):
        self.tick(max(0, self.ready[which] - self.done))
        self.land(which)

    def land(self, which):
        unit = self.units[which]
        if unit.shared:
            return
        other = unit.columns(1 - self.place.core)
        for slot, (da, db) in enumerate(((0, 0), (1, 0), (0, 1), (1, 1))):
            window = unit.slab(self.place.sibling_spot(da, db), other)
            pltpu.make_async_copy(window, window, self.recv_sem.at[which, 6 + slot]).wait()

    def copy(self, which, slot):
        unit, place = self.units[which], self.place
        mine = unit.columns(place.core)
        if slot < 3:
            step = (slot + 1, 0, 0)
            source = unit.own(place.core)
            target = unit.block(place.z, place.spot(0, 0), mine)
            landing = 2 - slot
            device = place.peer(*step)
        else:
            da, db = {3: (0, 0), 4: (0, 0), 5: (1, 0), 6: (0, 0), 7: (1, 0), 8: (0, 1), 9: (1, 1)}[slot]
            source = target = unit.slab(place.spot(da, db), mine)
            landing = slot
            if slot == 3:
                device = place.peer(0, 1, 0)
            elif slot < 6:
                device = place.peer(0, 0, 1)
            else:
                device = place.sibling()
        return remote(
            source, target, self.send_sem.at[which, slot], self.recv_sem.at[which, landing], device
        )

    def stay(self, which):
        unit, place = self.units[which], self.place
        return pltpu.make_async_copy(
            unit.own(place.core),
            unit.block(place.z, place.spot(0, 0), unit.columns(place.core)),
            self.local_sem.at[which],
        )

    def start(self, which):
        self.stay(which).start()
        for slot in range(3):
            self.copy(which, slot).start()

    def arrive(self, which, slot):
        unit, place = self.units[which], self.place
        mine = unit.columns(place.core)
        if slot < 3:
            window = unit.block((place.z + slot + 1) % 4, place.spot(0, 0), mine)
        else:
            da, db = {3: (1, 0), 4: (0, 1), 5: (1, 1)}[slot]
            window = unit.slab(place.spot(da, db), mine)
        pltpu.make_async_copy(window, window, self.recv_sem.at[which, slot]).wait()

    def pass_on(self, which, slot):
        if not self.units[which].shared:
            self.copy(which, slot).start()

    def after_z(self, which):
        self.stay(which).wait()
        for slot in range(3):
            self.arrive(which, slot)
        self.copy(which, 3).start()
        self.copy(which, 4).start()
        self.pass_on(which, 6)

    def after_a(self, which):
        self.arrive(which, 3)
        self.copy(which, 5).start()
        self.pass_on(which, 7)

    def after_b(self, which):
        self.arrive(which, 4)
        self.pass_on(which, 8)
        self.arrive(which, 5)
        self.pass_on(which, 9)

    def drain(self):
        for which, unit in enumerate(self.units):
            for slot in range(6 if unit.shared else 10):
                self.copy(which, slot).wait_send()


def nt(left, right):
    return lax.dot_general(left, right, (((1,), (1,)), ((), ())), preferred_element_type=WIDE)


def tn(left, right):
    return lax.dot_general(left, right, (((0,), (0,)), ((), ())), preferred_element_type=WIDE)


def nn(left, right):
    return jnp.dot(left, right, preferred_element_type=WIDE)


def normalize(values):
    center = jnp.mean(values, axis=-1, keepdims=True)
    centered = values - center
    spread = jnp.mean(centered * centered, axis=-1, keepdims=True)
    scale = lax.rsqrt(spread + 1e-05)
    return centered * scale, scale


def normalize_back(grad, normed, scale, gain):
    weighted = grad * gain
    inner = weighted - jnp.mean(weighted, axis=-1, keepdims=True)
    inner = inner - normed * jnp.mean(weighted * normed, axis=-1, keepdims=True)
    return scale * inner


def lanes(pair):
    return pl.ds(pl.multiple_of(pair * PAIR, PAIR), PAIR)


def head_mask(rows, side):
    spots = lax.broadcasted_iota(jnp.int32, (rows, PAIR), 1)
    return (spots // HEAD_DIM) == side


def only(mask, values):
    return jnp.where(mask, values, jnp.zeros_like(values))


def same_head():
    first = lax.broadcasted_iota(jnp.int32, (PAIR, PAIR), 0) // HEAD_DIM
    second = lax.broadcasted_iota(jnp.int32, (PAIR, PAIR), 1) // HEAD_DIM
    return first == second


def lower(size):
    return lax.broadcasted_iota(jnp.int32, (size, size), 0) >= lax.broadcasted_iota(
        jnp.int32, (size, size), 1
    )


def split(values):
    high = values.astype(LOW)
    low = (values - high.astype(WIDE)).astype(LOW)
    return high, low


def spots_of(block_len):
    return lax.broadcasted_iota(jnp.int32, (block_len, 1), 0).astype(WIDE)


def shifted_keys(keys, slot, window, taps):
    block_len = keys.shape[1] - 8
    total = taps[0:1] * keys[slot, 8 : 8 + block_len, window]
    for lag in range(1, 4):
        total = total + taps[lag : lag + 1] * keys[slot, 8 - lag : 8 - lag + block_len, window]
    return total


def hidden_order(shard):
    pieces = [
        shard[:, device * 192 + lot * 64 : device * 192 + lot * 64 + 64]
        for lot in range(3)
        for device in range(16)
    ]
    return jnp.concatenate(pieces, axis=1)


def hidden_disorder(columns):
    pieces = [
        columns[:, lot * 1024 + device * 64 : lot * 1024 + device * 64 + 64]
        for device in range(16)
        for lot in range(3)
    ]
    return jnp.concatenate(pieces, axis=1)


VEC, KEY, VALUE, QUERY, OUT, DOWN, UP = range(7)


def front_kernel(
    lengths, packed, qkv_shard, out_shard, up_shard, down_shard, tokens_in, cotangent_in,
    mixed_out, normed_out, qkv_out, edges_out, state_out, mixer_out, resid_grad_out, weights_out,
    vectors_out, sums_out, up_out, down_out,
    vec_all, weights, up_all, down_all, up_own, tokens, grad_low, normed, qkv, edges, state_in,
    state_send, mixer, resid, normed_two, normed_turned, keys, summed, mixed, vectors, sums,
    up_stage, down_stage, up_half, down_half,
    send_sem, recv_sem, local_sem, load_sem, save_sem, pair_send, pair_recv, tile_send, tile_recv,
):
    slots, block_len, width = tokens.shape
    pairs = width // PAIR
    size = block_len // 2
    tiles = up_half.shape[0]
    place = Place()
    core = place.core
    first = core == 0
    queries, key_rows, values = qkv.at[0], qkv.at[1], qkv.at[2]

    def load(slot, source, target):
        return pltpu.make_async_copy(source, target, load_sem.at[slot])

    def save(slot):
        source, target = (
            (mixed, mixed_out), (normed, normed_out), (qkv, qkv_out), (edges, edges_out),
            (state_in, state_out), (mixer, mixer_out), (keys.at[:, pl.ds(0, block_len)], resid_grad_out),
            (weights, weights_out), (vectors, vectors_out), (sums, sums_out), (up_half, up_out),
            (down_half, down_out),
        )[slot]
        return pltpu.make_async_copy(source, target, save_sem.at[slot])

    load(0, up_shard, up_own).start()
    load(1, tokens_in, tokens).start()
    load(2, cotangent_in, grad_low).start()
    enter(place)
    units = [
        Unit((packed, 0, 0), vec_all, 16, shared=True),
        Unit((qkv_shard, 0, width), weights.at[1], 48, width=width),
        Unit((qkv_shard, 0, 2 * width), weights.at[2], 48, width=width),
        Unit((qkv_shard, 0, 0), weights.at[0], 48, width=width),
        Unit((out_shard, 0, 0), weights.at[3], 48, width=width),
    ]
    for lot in range(3):
        units.append(Unit((down_shard, lot * 64, 0), down_all, 64, lead=4 * lot, width=width))
        units.append(Unit((up_own, 0, lot * 1024), up_all, 48, start=lot * 1024, width=1024))
    gather = Gather(place, units, send_sem, recv_sem, local_sem)
    for which in range(5):
        gather.start(which)
    load(0, up_shard, up_own).wait()
    up_own[...] = hidden_order(up_own[...])
    for which in range(5, len(units)):
        gather.start(which)

    load(1, tokens_in, tokens).wait()
    gather.need(VEC)
    vectors[...] = sum(
        vec_all[z, spot * 16 : spot * 16 + 16].astype(WIDE) for z in range(4) for spot in range(4)
    )
    gain, bias = vectors[0:1], vectors[1:2]
    for slot in range(slots):
        rows = slice(slot * block_len, (slot + 1) * block_len)
        hat, _ = normalize(tokens[slot].astype(WIDE))
        normed[rows] = (hat * gain + bias).astype(LOW)
    save(1).start()
    save(8).start()
    load(2, cotangent_in, grad_low).wait()
    base = core * block_len
    for slot in range(slots):
        keep = base + lax.broadcasted_iota(jnp.int32, (block_len, 1), 0) < lengths[slot]
        grad_low[slot] = (grad_low[slot].astype(WIDE) * keep.astype(WIDE)).astype(LOW)

    def weight(which):
        return weights[which].reshape(width, width)

    def project(which):
        for slot in range(slots):
            rows = slice(slot * block_len, (slot + 1) * block_len)
            qkv[which, slot] = nn(normed[rows], weight(which)).astype(LOW)

    gather.need(KEY)
    project(1)
    edge_copy = remote(
        key_rows.at[:, pl.ds(block_len - 16, 16)], edges, pair_send.at[0], pair_recv.at[0], place.sibling()
    )

    @pl.when(first)
    def _():
        edge_copy.start()

    gather.need(VALUE)
    project(2)
    gather.need(QUERY)
    project(0)
    save(2).start()

    @pl.when(first)
    def _():
        edge_copy.wait_send()
        edges[...] = jnp.zeros_like(edges)

    @pl.when(core == 1)
    def _():
        edge_copy.wait_recv()

    save(3).start()
    for slot in range(slots):
        keys[slot, 0:8] = edges[slot].astype(WIDE)[8:16]
        keys[slot, 8:] = key_rows[slot].astype(WIDE)
    spots = spots_of(block_len)
    state_copy = remote(state_send, state_in, pair_send.at[1], pair_recv.at[1], place.sibling())

    @pl.when(first)
    def _():
        def fresh(pair, carry):
            window = lanes(pair)
            rate = vectors[ROW_RATE : ROW_RATE + 1, window]
            taps = vectors[ROW_TAPS : ROW_TAPS + 4, window]
            tail = jnp.exp(-rate * (block_len - 1.0 - spots))
            for slot in range(slots):
                tail_keys = (shifted_keys(keys, slot, window, taps) * tail).astype(LOW)
                state_send[pair, slot] = only(same_head(), tn(tail_keys, values[slot, :, window]))
            return carry

        lax.fori_loop(0, pairs, fresh, 0)
        state_copy.start()

    gather.tick(2)

    def within(pair, carry):
        gather.spread(pair, pairs, TICKS_WITHIN)
        window = lanes(pair)
        rate = vectors[ROW_RATE : ROW_RATE + 1, window]
        taps = vectors[ROW_TAPS : ROW_TAPS + 4, window]
        fall = jnp.exp(-rate * spots)
        rise = jnp.exp(rate * spots)
        for slot in range(slots):
            decayed = (queries[slot, :, window].astype(WIDE) * fall).astype(LOW)
            lifted = (shifted_keys(keys, slot, window, taps) * rise).astype(LOW)
            value = values[slot, :, window]
            top = jnp.zeros((size, PAIR), WIDE)
            low = jnp.zeros((size, PAIR), WIDE)
            for side in range(2):
                query_side = only(head_mask(block_len, side), decayed)
                value_side = only(head_mask(block_len, side), value)
                near = jnp.where(lower(size), nt(query_side[:size], lifted[:size]), 0.0)
                top = top + nn(near.astype(LOW), value_side[:size])
                far = nt(query_side[size:], lifted[:size]).astype(LOW)
                near = jnp.where(lower(size), nt(query_side[size:], lifted[size:]), 0.0)
                low = low + nn(far, value_side[:size]) + nn(near.astype(LOW), value_side[size:])
            summed[slot, :size, window] = top
            summed[slot, size:, window] = low
        return carry

    lax.fori_loop(0, pairs, within, 0)

    @pl.when(first)
    def _():
        state_copy.wait_send()
        state_in[...] = jnp.zeros_like(state_in)

    @pl.when(core == 1)
    def _():
        state_copy.wait_recv()

        def reach(pair, carry):
            window = lanes(pair)
            rate = vectors[ROW_RATE : ROW_RATE + 1, window]
            decay = jnp.exp(-rate * (spots + 1.0))
            for slot in range(slots):
                reaching = (queries[slot, :, window].astype(WIDE) * decay).astype(LOW)
                high, low = split(state_in[pair, slot])
                summed[slot, :, window] += nn(reaching, high) + nn(reaching, low)
            return carry

        lax.fori_loop(0, pairs, reach, 0)

    save(4).start()
    gather.need(OUT)
    save(7).start()
    gain_two, bias_two = vectors[3:4], vectors[4:5]
    for slot in range(slots):
        rows = slice(slot * block_len, (slot + 1) * block_len)
        mixer[rows] = summed[slot].astype(LOW)
        total = tokens[slot].astype(WIDE) + nn(mixer[rows], weight(3))
        resid[slot] = total
        summed[slot] = total
        hat, _ = normalize(total)
        normed_two[rows] = (hat * gain_two + bias_two).astype(LOW)
    save(5).start()
    normed_turned[...] = normed_two[...].T
    keys[:, 0:block_len] = jnp.zeros((slots, block_len, width), WIDE)
    gather.need(DOWN)
    gather.need(UP)

    def tile_copies(tile):
        slot = tile % 2
        other = 1 - core
        return (
            remote(
                up_stage.at[slot, :, part(other * 256, 256, 128)],
                up_half.at[tile],
                tile_send.at[tile, 0],
                tile_recv.at[tile, 0],
                place.sibling(),
            ),
            remote(
                down_stage.at[slot, :, :, part(other * 384, 384, 128)],
                down_half.at[pl.ds(2 * tile, 2)],
                tile_send.at[tile, 1],
                tile_recv.at[tile, 1],
                place.sibling(),
            ),
        )

    def merge(tile):
        for copy in tile_copies(tile):
            copy.wait_recv()
        slot = tile % 2
        up_half[tile] = up_half[tile] + up_stage[slot, :, part(core * 256, 256, 128)]
        window = pl.ds(2 * tile, 2)
        down_half[window] = down_half[window] + down_stage[slot, :, :, part(core * 384, 384, 128)]

    def ffn_tile(tile, carry):
        for lot in range(1, 3):
            @pl.when(tile == 2 * lot)
            def _(lot=lot):
                gather.land(DOWN + 2 * lot)
                gather.land(UP + 2 * lot)

        columns = part(tile * 512, 512, 512)
        up = up_all[:, :, columns].reshape(width, 512)
        down = down_all[pl.ds(2 * tile, 2)].reshape(512, width)
        cotangent = grad_low[...].reshape(slots * block_len, width)
        pre = nn(normed_two[...], up)
        wide = nt(cotangent, down)
        square = pre * pre
        ramp = jnp.tanh(pre * (GELU_A + (GELU_A * GELU_B) * square))
        half = 0.5 + 0.5 * ramp
        slope = half + (0.5 * pre) * (1.0 - ramp * ramp) * (
            GELU_A + (3.0 * GELU_A * GELU_B) * square
        )
        act = (pre * half).astype(LOW)
        back = (wide * slope).astype(LOW)
        for slot in range(slots):
            rows = slice(slot * block_len, (slot + 1) * block_len)
            summed[slot] += nn(act[rows], down)
            keys[slot, 0:block_len] += nt(back[rows], up)
        turn = tile % 2

        @pl.when(tile >= 2)
        def _():
            for copy in tile_copies(tile - 2):
                copy.wait_send()

        gather.spread(tile, tiles, TICKS_FFN)
        up_stage[turn] = nn(normed_turned[...], back).astype(LOW)
        down_stage[turn] = tn(act, cotangent).astype(LOW).reshape(2, 256, width)
        for copy in tile_copies(tile):
            copy.start()

        @pl.when(tile >= 1)
        def _():
            merge(tile - 1)

        return carry

    lax.fori_loop(0, tiles, ffn_tile, 0)
    sums[...] = jnp.zeros_like(sums)
    for slot in range(slots):
        mixed[slot] = summed[slot].astype(LOW)
        hat, scale = normalize(resid[slot])
        grad = keys[slot, 0:block_len]
        sums[0:1] += jnp.sum(grad * hat, axis=0, keepdims=True)
        sums[1:2] += jnp.sum(grad, axis=0, keepdims=True)
        keys[slot, 0:block_len] = grad_low[slot].astype(WIDE) + normalize_back(grad, hat, scale, gain_two)
    save(0).start()
    save(6).start()
    save(9).start()
    merge(tiles - 1)
    save(10).start()
    save(11).start()
    for tile in (tiles - 2, tiles - 1):
        for copy in tile_copies(tile):
            copy.wait_send()
    gather.tick(len(gather.events))
    gather.drain()
    for slot in range(12):
        save(slot).wait()


TICKS_WITHIN, TICKS_FFN = 1, 3


def front(packed, qkv_weight, out_weight, up_weight, down_weight, tokens, cotangent, lengths):
    slots, block_len, width = tokens.shape
    count = slots * block_len
    pairs = width // PAIR
    hidden = up_weight.shape[1]
    tiles = hidden // 512
    shape = jax.ShapeDtypeStruct
    outs = [
        shape(tokens.shape, LOW),
        shape((count, width), LOW),
        shape((3, slots, block_len, width), LOW),
        shape((slots, 16, width), LOW),
        shape((pairs, slots, PAIR, PAIR), WIDE),
        shape((count, width), LOW),
        shape(tokens.shape, WIDE),
        shape((4, 4, width // 4, width), LOW),
        shape((16, width), WIDE),
        shape((8, width), WIDE),
        shape((tiles, width, 256), LOW),
        shape((2 * tiles, 256, width // 2), LOW),
    ]
    vmem = lambda *dims: pltpu.VMEM(dims, LOW)
    wide = lambda *dims: pltpu.VMEM(dims, WIDE)
    dma = pltpu.SemaphoreType.DMA
    anywhere = pl.BlockSpec(memory_space=pltpu.HBM)
    return pl.pallas_call(
        front_kernel,
        out_shape=outs,
        in_specs=[pl.BlockSpec(memory_space=pltpu.SMEM)] + [anywhere] * 7,
        out_specs=[anywhere] * len(outs),
        scratch_shapes=[
            vmem(4, 64, width),
            vmem(4, 4, width // 4, width),
            vmem(4, width // 4, hidden),
            vmem(12, 256, width),
            vmem(width // 16, hidden),
            vmem(slots, block_len, width),
            vmem(slots, block_len, width),
            vmem(count, width),
            vmem(3, slots, block_len, width),
            vmem(slots, 16, width),
            wide(pairs, slots, PAIR, PAIR),
            wide(pairs, slots, PAIR, PAIR),
            vmem(count, width),
            wide(slots, block_len, width),
            vmem(count, width),
            vmem(width, count),
            wide(slots, block_len + 8, width),
            wide(slots, block_len, width),
            vmem(slots, block_len, width),
            wide(16, width),
            wide(8, width),
            vmem(2, width, 512),
            vmem(2, 2, 256, width),
            vmem(tiles, width, 256),
            vmem(2 * tiles, 256, width // 2),
            dma((11, 10)),
            dma((11, 10)),
            dma((11,)),
            dma((3,)),
            dma((12,)),
            dma((2,)),
            dma((2,)),
            dma((tiles, 2)),
            dma((tiles, 2)),
        ],
        compiler_params=pltpu.CompilerParams(
            collective_id=0, has_side_effects=True, vmem_limit_bytes=63 * MIB
        ),
        name="gather_forward_ffn",
    )(lengths, packed, qkv_weight, out_weight, up_weight, down_weight, tokens, cotangent)


class Share:
    def __init__(self, source, own, from_b, from_a, from_z, final, rows):
        self.source, self.own, self.rows = source, own, rows
        self.from_b, self.from_a, self.from_z, self.final = from_b, from_a, from_z, final

    def slab(self, ref, spot):
        return ref.at[:, part(spot * self.rows, self.rows, 16)]


class Reduction:
    def __init__(self, place, shares, send_sem, recv_sem):
        self.place, self.shares = place, shares
        self.send_sem, self.recv_sem = send_sem, recv_sem

    def copy(self, which, slot):
        share, place = self.shares[which], self.place
        if slot < 2:
            da = 1 - slot
            source = share.slab(share.source, place.spot(da, 1))
            target = share.from_b.at[(place.a + da) % 2]
            device = place.peer(0, 0, 1)
        elif slot == 2:
            source, target = share.from_b.at[1 - place.a], share.from_a
            device = place.peer(0, 1, 0)
        elif slot < 6:
            dz = slot - 2
            source, target = share.from_a.at[(place.z + dz) % 4], share.from_z.at[dz - 1]
            device = place.peer(dz, 0, 0)
        else:
            source = target = share.final.at[place.core]
            device = place.sibling()
        return remote(source, target, self.send_sem.at[which, slot], self.recv_sem.at[which, slot], device)

    def start(self, which):
        for slot in range(2):
            self.copy(which, slot).start()

    def merge_b(self, which):
        share, place = self.shares[which], self.place
        for slot in range(2):
            self.copy(which, slot).wait_recv()
            da = 1 - slot
            a = (place.a + da) % 2
            rows = part(place.spot(da, 0) * share.rows, share.rows, 16)
            share.from_b[a] = share.from_b[a] + share.own[:, rows]
            if slot == 0:
                self.copy(which, 2).start()

    def merge_a(self, which):
        share = self.shares[which]
        self.copy(which, 2).wait_recv()
        share.from_a[...] = share.from_a[...] + share.from_b[self.place.a]
        for slot in range(3, 6):
            self.copy(which, slot).start()

    def finish(self, which):
        share, place = self.shares[which], self.place
        total = share.from_a[place.z].astype(WIDE)
        for slot in range(3):
            self.copy(which, 3 + slot).wait_recv()
            total = total + share.from_z[slot].astype(WIDE)
        share.final[place.core] = total
        self.copy(which, 6).start()

    def land(self, which):
        share, place = self.shares[which], self.place
        other = share.final.at[1 - place.core]
        pltpu.make_async_copy(other, other, self.recv_sem.at[which, 6]).wait()

    def drain(self):
        for which in range(len(self.shares)):
            for slot in range(7):
                self.copy(which, slot).wait_send()


class Script:
    def __init__(self, events):
        self.events, self.done = events, 0

    def tick(self, count):
        for event in self.events[self.done : self.done + count]:
            event()
        self.done = min(self.done + count, len(self.events))

    def spread(self, index, trips, each):
        for trip in range(trips):
            chosen = self.events[self.done : self.done + each]
            self.done += len(chosen)
            if chosen:
                @pl.when(index == trip)
                def _(chosen=chosen):
                    for event in chosen:
                        event()


def staggered(reduction, which):
    events = []
    which = list(which)
    for turn in range(len(which) + 2):
        for lag, step in enumerate((reduction.merge_b, reduction.merge_a, reduction.finish)):
            if 0 <= turn - lag < len(which):
                events.append(functools.partial(step, which[turn - lag]))
    return events


UPS, DOWNS, OUTS, PAIRS, KEYS = 0, 6, 9, 10, 16


def back_kernel(
    resid_grad_in, mixer_in, qkv_in, edges_in, state_in_in, normed_in, tokens_in, weights_in,
    vectors_in, two_sums, up_in, down_in,
    input_grad_out, up_sum, down_sum, out_sum, qkv_sum, small_out,
    resid_grad, mixer, qkv, edges, state_in, normed, weights, vectors, up_half, down_half,
    keys, branch, back_rows, projected, key_back, normed_turned, state_send, state_grad,
    out_stage, out_half, pair_stage, pair_half, key_half,
    up_b, up_a, up_z, up_final, down_b, down_a, down_z, down_final, wide_b, wide_a, wide_z, wide_final,
    pair_b, pair_a, pair_z, pair_final, small, small_sums, small_from,
    send_sem, recv_sem, load_sem, save_sem, core_send, core_recv, pair_send, pair_recv,
    small_send, small_recv,
):
    slots, block_len, width = resid_grad.shape
    pairs = width // PAIR
    size = block_len // 2
    place = Place()
    core = place.core
    first = core == 0
    second = core == 1
    queries, key_rows, values = qkv.at[0], qkv.at[1], qkv.at[2]
    inputs = (
        (resid_grad_in, resid_grad), (weights_in, weights), (vectors_in, vectors), (qkv_in, qkv),
        (mixer_in, mixer), (edges_in, edges), (state_in_in, state_in), (normed_in, normed),
        (up_in, up_half), (down_in, down_half), (tokens_in, mixer),
    )
    LOAD_GRAD, LOAD_WEIGHTS, LOAD_VECTORS, LOAD_QKV, LOAD_MIXER, LOAD_EDGES, LOAD_STATE = range(7)
    LOAD_NORMED, LOAD_UP, LOAD_DOWN, LOAD_TOKENS = range(7, 11)

    def load(slot):
        return pltpu.make_async_copy(*inputs[slot], load_sem.at[slot])

    for slot in range(LOAD_TOKENS):
        load(slot).start()
    enter(place)
    shares = [
        Share(
            up_in.at[k], up_half.at[k],
            up_b.at[k], up_a.at[k], up_z.at[k], up_final.at[k], 48,
        )
        for k in range(6)
    ]
    shares += [
        Share(
            down_in.at[pl.ds(4 * k, 4)], down_half.at[pl.ds(4 * k, 4)],
            down_b.at[k], down_a.at[k], down_z.at[k], down_final.at[k], 64,
        )
        for k in range(3)
    ]
    shares.append(
        Share(out_half, out_half, wide_b.at[0], wide_a.at[0], wide_z.at[0], wide_final.at[0], 48)
    )
    shares += [
        Share(
            pair_half.at[k], pair_half.at[k], pair_b.at[k], pair_a.at[k], pair_z.at[k],
            pair_final.at[k], 48,
        )
        for k in range(6)
    ]
    shares.append(
        Share(key_half, key_half, wide_b.at[1], wide_a.at[1], wide_z.at[1], wide_final.at[1], 48)
    )
    reduction = Reduction(place, shares, send_sem, recv_sem)
    for k in range(3):
        reduction.start(UPS + 2 * k)
        reduction.start(UPS + 2 * k + 1)
        reduction.start(DOWNS + k)
    script = Script(staggered(reduction, (0, 1, 6, 2, 3, 7, 4, 5, 8, 9)))
    spots = spots_of(block_len)

    load(LOAD_GRAD).wait()
    load(LOAD_WEIGHTS).wait()
    out_weight = weights[3].reshape(width, width)
    for slot in range(slots):
        rows = slice(slot * block_len, (slot + 1) * block_len)
        branch[rows] = resid_grad[slot].astype(LOW)
        back_rows[slot] = nt(branch[rows], out_weight).astype(LOW)
    load(LOAD_VECTORS).wait()
    load(LOAD_QKV).wait()
    state_copy = remote(state_send, state_grad, core_send.at[0], core_recv.at[0], place.sibling())

    @pl.when(second)
    def _():
        def gather_state(pair, carry):
            window = lanes(pair)
            rate = vectors[ROW_RATE : ROW_RATE + 1, window]
            decay = jnp.exp(-rate * (spots + 1.0))
            for slot in range(slots):
                reaching = (queries[slot, :, window].astype(WIDE) * decay).astype(LOW)
                back = back_rows[slot, :, window]
                state_send[pair, slot] = only(same_head(), tn(reaching, back)).astype(LOW)
            return carry

        lax.fori_loop(0, pairs, gather_state, 0)
        state_copy.start()

    load(LOAD_MIXER).wait()
    load(LOAD_UP).wait()
    load(LOAD_DOWN).wait()
    normed_turned[...] = mixer[...].T
    out_stage[...] = nn(normed_turned[...], branch[...]).astype(LOW).reshape(4, width // 4, width)

    def halves(stage, half, sem):
        window = part((1 - core) * (width // 2), width // 2, 128)
        return remote(stage.at[:, :, window], half, core_send.at[sem], core_recv.at[sem], place.sibling())

    def own_half(stage, half):
        half[...] = half[...] + stage[:, :, part(core * (width // 2), width // 2, 128)]

    load(LOAD_TOKENS).start()
    out_copy = halves(out_stage, out_half, 2)
    out_copy.start()
    load(LOAD_EDGES).wait()
    load(LOAD_STATE).wait()
    load(LOAD_NORMED).wait()
    normed_turned[...] = normed[...].T
    for slot in range(slots):
        keys[slot, 0:8] = edges[slot].astype(WIDE)[8:16]
        keys[slot, 8:] = key_rows[slot].astype(WIDE)
    out_copy.wait_recv()
    own_half(out_stage, out_half)
    reduction.start(OUTS)

    @pl.when(second)
    def _():
        state_copy.wait_send()
        state_grad[...] = jnp.zeros_like(state_grad)

    @pl.when(first)
    def _():
        state_copy.wait_recv()

    def pair_copy(pair):
        return remote(
            pair_stage.at[pair, 1 - core], pair_half.at[pair], pair_send.at[pair], pair_recv.at[pair],
            place.sibling(),
        )

    def merge_pair(pair):
        pair_copy(pair).wait_recv()
        pair_half[pair] = pair_half[pair] + pair_stage[pair, core]

    def back_pair(pair, carry):
        script.spread(pair, pairs, TICKS_BACK)
        window = lanes(pair)
        rate = vectors[ROW_RATE : ROW_RATE + 1, window]
        taps = vectors[ROW_TAPS : ROW_TAPS + 4, window]
        fall = jnp.exp(-rate * spots)
        rise = jnp.exp(rate * spots)
        tail = jnp.exp(-rate * (block_len - 1.0 - spots))
        decay = jnp.exp(-rate * (spots + 1.0))
        rate_grad = jnp.zeros((1, PAIR), WIDE)
        taps_grad = [jnp.zeros((1, PAIR), WIDE) for _ in range(4)]
        weight_grad = jnp.zeros((width, 2 * PAIR), WIDE)
        for slot in range(slots):
            query = queries[slot, :, window].astype(WIDE)
            key = shifted_keys(keys, slot, window, taps)
            value = values[slot, :, window]
            back = back_rows[slot, :, window]
            wide_decayed, wide_lifted = query * fall, key * rise
            wide_tail, wide_reach = key * tail, query * decay
            decayed, lifted = wide_decayed.astype(LOW), wide_lifted.astype(LOW)
            tail_keys = wide_tail.astype(LOW)
            decayed_turned, back_turned = decayed.T, back.T
            decayed_top = jnp.zeros((size, PAIR), WIDE)
            decayed_low = jnp.zeros((size, PAIR), WIDE)
            lifted_top = jnp.zeros((PAIR, size), WIDE)
            lifted_low = jnp.zeros((PAIR, size), WIDE)
            value_top = jnp.zeros((PAIR, size), WIDE)
            value_low = jnp.zeros((PAIR, size), WIDE)
            row_head = lax.broadcasted_iota(jnp.int32, (PAIR, block_len), 0) // HEAD_DIM
            for side in range(2):
                mask = head_mask(block_len, side)
                query_side, back_side = only(mask, decayed), only(mask, back)
                lifted_side = only(mask, lifted)
                query_turned = only(row_head == side, decayed_turned)
                back_side_turned = only(row_head == side, back_turned)
                causal = lower(size)
                halves_of = (slice(0, size), slice(size, block_len))
                for t, s in ((0, 0), (1, 0), (1, 1)):
                    score = nt(query_side[halves_of[t]], lifted[halves_of[s]])
                    grad = nt(back_side[halves_of[t]], value[halves_of[s]])
                    if t == s:
                        score, grad = jnp.where(causal, score, 0.0), jnp.where(causal, grad, 0.0)
                    score, grad = score.astype(LOW), grad.astype(LOW)
                    query_part = nn(grad, lifted_side[halves_of[s]])
                    lifted_part = nn(query_turned[:, halves_of[t]], grad)
                    value_part = nn(back_side_turned[:, halves_of[t]], score)
                    if t == 0:
                        decayed_top = decayed_top + query_part
                    else:
                        decayed_low = decayed_low + query_part
                    if s == 0:
                        lifted_top, value_top = lifted_top + lifted_part, value_top + value_part
                    else:
                        lifted_low, value_low = lifted_low + lifted_part, value_low + value_part
            decayed_grad = jnp.concatenate([decayed_top, decayed_low], axis=0)
            lifted_grad = jnp.concatenate([lifted_top.T, lifted_low.T], axis=0)
            value_grad = jnp.concatenate([value_top.T, value_low.T], axis=0)
            leaving = state_grad[pair, slot]
            entering = state_in[pair, slot]
            high, low = split(entering)
            value_grad = value_grad + nn(tail_keys, leaving)
            tail_grad = nt(value, leaving)
            reach_grad = nt(back, high) + nt(back, low)
            carry_grad = jnp.sum((leaving.astype(WIDE) * entering).T, axis=0, keepdims=True)
            key_grad = lifted_grad * rise + tail_grad * tail
            steps = (
                spots * (lifted_grad * wide_lifted - decayed_grad * wide_decayed)
                - (block_len - 1.0 - spots) * (tail_grad * wide_tail)
                - (spots + 1.0) * (reach_grad * wide_reach)
            )
            rate_grad = rate_grad + jnp.sum(steps, axis=0, keepdims=True)
            rate_grad = rate_grad - block_len * jnp.exp(-rate * block_len) * carry_grad
            query_low = (decayed_grad * fall + reach_grad * decay).astype(LOW)
            value_low_grad = value_grad.astype(LOW)
            projected[0, slot, :, window] = query_low
            projected[2, slot, :, window] = value_low_grad
            key_back[slot, 0:block_len, window] = key_grad
            for lag in range(4):
                lagged = keys[slot, 8 - lag : 8 - lag + block_len, window]
                taps_grad[lag] = taps_grad[lag] + jnp.sum(lagged * key_grad, axis=0, keepdims=True)
            rows = slice(slot * block_len, (slot + 1) * block_len)
            weight_grad = weight_grad + nn(
                normed_turned[:, rows], jnp.concatenate([query_low, value_low_grad], axis=1)
            )
        small[0:8, window] = jnp.concatenate(
            [jnp.zeros((2, PAIR), WIDE), rate_grad, *taps_grad, jnp.zeros((1, PAIR), WIDE)], axis=0
        )
        for side in range(2):
            pair_stage[pair, side] = (
                weight_grad[:, side * PAIR : (side + 1) * PAIR].astype(LOW).reshape(4, width // 4, PAIR)
            )
        pair_copy(pair).start()

        @pl.when(pair >= 1)
        def _():
            merge_pair(pair - 1)

        for k in range(1, pairs):
            @pl.when(pair == k)
            def _(k=k):
                reduction.start(PAIRS + k - 1)

        return carry

    lax.fori_loop(0, pairs, back_pair, 0)
    spill = remote(
        key_back.at[:, pl.ds(0, 8)],
        key_back.at[:, pl.ds(block_len, 8)],
        core_send.at[1],
        core_recv.at[1],
        place.sibling(),
    )

    @pl.when(second)
    def _():
        spill.start()
        key_back[:, block_len : block_len + 8] = jnp.zeros((slots, 8, width), WIDE)

    script.tick(3)
    merge_pair(pairs - 1)
    reduction.start(PAIRS + pairs - 1)

    @pl.when(first)
    def _():
        spill.wait_recv()

    def key_pair(pair, carry):
        window = lanes(pair)
        taps = vectors[ROW_TAPS : ROW_TAPS + 4, window]
        for slot in range(slots):
            total = taps[0:1] * key_back[slot, 0:block_len, window]
            for lag in range(1, 4):
                total = total + taps[lag : lag + 1] * key_back[slot, lag : lag + block_len, window]
            projected[1, slot, :, window] = total.astype(LOW)
        return carry

    lax.fori_loop(0, pairs, key_pair, 0)
    rows_all = projected[1].reshape(slots * block_len, width)
    out_copy.wait_send()
    out_stage[...] = nn(normed_turned[...], rows_all).astype(LOW).reshape(4, width // 4, width)
    key_copy = halves(out_stage, key_half, 3)
    key_copy.start()
    script.tick(len(script.events))
    late = Script(staggered(reduction, (*range(PAIRS, PAIRS + pairs), KEYS)))
    late.tick(3)
    load(LOAD_TOKENS).wait()
    gain = vectors[0:1]
    key_copy.wait_recv()
    own_half(out_stage, key_half)
    reduction.start(KEYS)
    gain_sum = jnp.zeros((1, width), WIDE)
    bias_sum = jnp.zeros((1, width), WIDE)
    for slot in range(slots):
        late.tick(4)
        grad = nt(projected[0, slot], weights[0].reshape(width, width))
        for third in range(1, 3):
            grad = grad + nt(projected[third, slot], weights[third].reshape(width, width))
        hat, scale = normalize(mixer[slot * block_len : (slot + 1) * block_len].astype(WIDE))
        gain_sum = gain_sum + jnp.sum(grad * hat, axis=0, keepdims=True)
        bias_sum = bias_sum + jnp.sum(grad, axis=0, keepdims=True)
        resid_grad[slot] = resid_grad[slot] + normalize_back(grad, hat, scale, gain)
        pltpu.make_async_copy(
            resid_grad.at[slot], input_grad_out.at[slot], save_sem.at[slot]
        ).start()
    small[0:1], small[1:2] = gain_sum, bias_sum
    small[8:16] = two_sums[...]

    def small_copy(slot):
        flip_x = (place.dp + 1 - 2 * (place.dp % 2), core)
        flip_y = (place.dp + 2 - 4 * ((place.dp // 2) % 2), core)
        source = small if slot == 0 else small_sums.at[min(slot, 3) - 1]
        device = (place.sibling(), flip_x, flip_y)[slot] if slot < 3 else place.peer(slot - 2, 0, 0)
        return remote(source, small_from.at[slot], small_send.at[slot], small_recv.at[slot], device)

    small_copy(0).start()
    for slot in range(3):
        late.tick(2)
        small_copy(slot).wait_recv()
        before = small[...] if slot == 0 else small_sums[slot - 1]
        small_sums[slot] = before + small_from[slot]
        if slot < 2:
            small_copy(slot + 1).start()
    for slot in range(3, 6):
        small_copy(slot).start()
    late.tick(len(late.events))
    for slot in range(3, 6):
        small_copy(slot).wait_recv()
    small_from[2] = small_sums[2]
    total = jnp.zeros(small.shape, WIDE)
    for z in range(4):
        total = total + small_from[2 + (place.z + 4 - z) % 4]
    small_out[...] = total
    for which in range(len(shares)):
        reduction.land(which)
    ups = [up_final[tile, side] for tile in range(6) for side in range(2)]
    up_sum[...] = hidden_disorder(jnp.concatenate(ups, axis=1))
    for lot in range(3):
        for side in range(2):
            down_sum[lot * 64 : lot * 64 + 64, side * 384 : side * 384 + 384] = down_final[lot, side]
    for side in range(2):
        out_sum[:, side * 384 : side * 384 + 384] = wide_final[0, side]
        qkv_sum[:, width + side * 384 : width + side * 384 + 384] = wide_final[1, side]
        for pair in range(pairs):
            start = 2 * width * side + pair * PAIR
            qkv_sum[:, start : start + PAIR] = pair_final[pair, side]
    reduction.drain()
    for slot in range(6):
        small_copy(slot).wait_send()
    for pair in range(pairs):
        pair_copy(pair).wait_send()
    key_copy.wait_send()

    @pl.when(second)
    def _():
        spill.wait_send()

    for slot in range(slots):
        pltpu.make_async_copy(
            resid_grad.at[slot], input_grad_out.at[slot], save_sem.at[slot]
        ).wait()


TICKS_BACK = 4


def back(
    resid_grad, mixer, qkv, edges, state_in, normed, tokens, weights, vectors, two_sums, up_half, down_half,
):
    slots, block_len, width = tokens.shape
    count = slots * block_len
    pairs = width // PAIR
    shape = jax.ShapeDtypeStruct
    up_half = up_half.reshape(6, 4, width // 4, 256)
    outs = [
        shape(tokens.shape, WIDE),
        shape((width // 16, 4 * width), WIDE),
        shape((4 * width // 16, width), WIDE),
        shape((width // 16, width), WIDE),
        shape((width // 16, 3 * width), WIDE),
        shape((16, width), WIDE),
    ]
    low = lambda *dims: pltpu.VMEM(dims, LOW)
    wide = lambda *dims: pltpu.VMEM(dims, WIDE)
    dma = pltpu.SemaphoreType.DMA
    vmem = pl.BlockSpec(memory_space=pltpu.VMEM)
    anywhere = pl.BlockSpec(memory_space=pltpu.HBM)
    held = (resid_grad, mixer, qkv, edges, state_in, normed, weights, vectors, up_half, down_half)

    def stages(lead, rows, columns):
        return [
            low(lead, 2, 4, rows, columns), low(lead, 4, rows, columns),
            low(lead, 3, rows, columns), wide(lead, 2, rows, columns),
        ]

    return pl.pallas_call(
        back_kernel,
        out_shape=outs,
        in_specs=[anywhere] * 9 + [vmem] + [anywhere] * 2,
        out_specs=[anywhere] + [vmem] * 5,
        scratch_shapes=[pltpu.VMEM(array.shape, array.dtype) for array in held]
        + [
            wide(slots, block_len + 8, width),
            low(count, width),
            low(slots, block_len, width),
            low(3, slots, block_len, width),
            wide(slots, block_len + 8, width),
            low(width, count),
            low(pairs, slots, PAIR, PAIR),
            low(pairs, slots, PAIR, PAIR),
            low(4, width // 4, width),
            low(4, width // 4, width // 2),
            low(pairs, 2, 4, width // 4, PAIR),
            low(pairs, 4, width // 4, PAIR),
            low(4, width // 4, width // 2),
        ]
        + stages(6, 48, 256) + stages(3, 64, 384) + stages(2, 48, 384) + stages(6, 48, PAIR)
        + [
            wide(16, width),
            wide(3, 16, width),
            wide(6, 16, width),
            dma((17, 7)),
            dma((17, 7)),
            dma((11,)),
            dma((2,)),
            dma((4,)),
            dma((4,)),
            dma((6,)),
            dma((6,)),
            dma((6,)),
            dma((6,)),
        ],
        compiler_params=pltpu.CompilerParams(
            collective_id=1, has_side_effects=True, vmem_limit_bytes=63 * MIB
        ),
        name="backward_reduce",
    )(
        resid_grad, mixer, qkv, edges, state_in, normed, tokens.reshape(count, width), weights, vectors,
        two_sums, up_half, down_half,
    )


def from_behind(value, axis, steps):
    count = lax.axis_size(axis)
    leading, last = (max(0, -steps), min(count, count - steps))
    return lax.ppermute(value, axis, [(source, source + steps) for source in range(leading, last)])


def as_sent(array):

    def short(part):
        return part.astype(jnp.bfloat16) if part.dtype == jnp.float32 else part

    return jax.tree.map(short, array)


def layer_norm(values, norm_gain, offset):
    center = jnp.mean(values, axis=-1, keepdims=True)
    centered = values - center
    spread = jnp.mean(centered * centered, axis=-1, keepdims=True)
    return centered * lax.rsqrt(spread + 1e-05) * norm_gain + offset


def shift_mix(extended, tap_table):
    block_len = extended.shape[-2] - 3
    mixed_sum = tap_table[0] * extended[..., 3 : 3 + block_len, :]
    for lag_step in range(1, 4):
        mixed_sum = (
            mixed_sum
            + tap_table[lag_step] * extended[..., 3 - lag_step : 3 - lag_step + block_len, :]
        )
    return mixed_sum


def factors(queries, key_rows, rate_vector):
    block_len = queries.shape[1]
    rate_grid = rate_vector.reshape(queries.shape[2], -1)
    positions = jnp.arange(block_len, dtype=jnp.float32)[:, None, None]
    decayed = queries * jnp.exp(-rate_grid * positions)
    lifted = key_rows * jnp.exp(rate_grid * positions)
    tail_keys = key_rows * jnp.exp(-rate_grid * (block_len - 1.0 - positions))
    reaching = queries * jnp.exp(-rate_grid * (positions + 1.0))
    carry_decay = jnp.exp(-rate_grid * block_len)
    return (decayed, lifted, tail_keys, reaching, carry_decay)


def outer_sum(left_rows, right_rows):
    return lax.dot_general(
        left_rows, right_rows, (((0,), (0,)), ((), ())), preferred_element_type=jnp.float32
    )


def back_product(grad_rows, weight):
    return lax.dot_general(
        grad_rows, weight, (((1,), (1,)), ((), ())), preferred_element_type=jnp.float32
    )


def general(
    tokens,
    ln1_gain,
    ln1_bias,
    qkv_weight,
    shift_taps,
    decay_rates,
    out_weight,
    ln2_gain,
    ln2_bias,
    up_weight,
    down_weight,
    lengths,
    out_grad,
):
    slot_count, block_len, model_width = tokens.shape
    token_count = slot_count * block_len
    gathered = (
        lax.all_gather(ln1_gain, "dp", axis=0, tiled=True),
        lax.all_gather(ln1_bias, "dp", axis=0, tiled=True),
        lax.all_gather(qkv_weight, "dp", axis=0, tiled=True),
        lax.all_gather(shift_taps, "dp", axis=1, tiled=True),
        lax.all_gather(decay_rates, "dp", axis=0, tiled=True),
        lax.all_gather(out_weight, "dp", axis=0, tiled=True),
        lax.all_gather(ln2_gain, "dp", axis=0, tiled=True),
        lax.all_gather(ln2_bias, "dp", axis=0, tiled=True),
        lax.all_gather(up_weight, "dp", axis=0, tiled=True),
        lax.all_gather(down_weight, "dp", axis=0, tiled=True),
    )
    gain_one = gathered[0].astype(jnp.float32)
    bias_one = gathered[1].astype(jnp.float32)
    tap_table = gathered[3].astype(jnp.float32)
    rate_vector = gathered[4].astype(jnp.float32)
    gain_two = gathered[6].astype(jnp.float32)
    bias_two = gathered[7].astype(jnp.float32)
    qkv_full = gathered[2]
    out_full = gathered[5]
    up_full = gathered[8]
    down_full = gathered[9]
    inputs = tokens.reshape(token_count, model_width).astype(jnp.float32)
    normed_one = layer_norm(inputs, gain_one, bias_one).astype(jnp.bfloat16)
    projected = jnp.dot(normed_one, qkv_full, preferred_element_type=jnp.float32).astype(
        jnp.bfloat16
    )
    projected = projected.reshape(slot_count, block_len, 3 * model_width)
    key_rows = projected[:, :, model_width : 2 * model_width]
    edge_rows = from_behind(key_rows[:, block_len - 3 :], "seq", 1)
    extended = jnp.concatenate([edge_rows, key_rows], axis=1).astype(jnp.float32)
    shifted = shift_mix(extended, tap_table)
    head_shape = (slot_count, block_len, HEADS, HEAD_DIM)
    flat_shape = (slot_count, block_len, model_width)
    head_queries = projected[:, :, :model_width].astype(jnp.float32).reshape(head_shape)
    head_keys = shifted.reshape(head_shape)
    head_values = projected[:, :, 2 * model_width :].reshape(head_shape)
    decayed, lifted, tail_keys, reaching, carry_decay = factors(
        head_queries, head_keys, rate_vector
    )
    decayed_low = decayed.astype(jnp.bfloat16)
    lifted_low = lifted.astype(jnp.bfloat16)
    tail_low = tail_keys.astype(jnp.bfloat16)
    reach_wide = reaching.astype(jnp.bfloat16).astype(jnp.float32)
    position_ids = jnp.arange(block_len)
    causal = position_ids[:, None] >= position_ids[None, :]
    scores = jnp.einsum(
        "bthk,bshk->bhts", decayed_low, lifted_low, preferred_element_type=jnp.float32
    )
    scores_low = jnp.where(causal, scores, 0.0).astype(jnp.bfloat16)
    within = jnp.einsum(
        "bhts,bshv->bthv", scores_low, head_values, preferred_element_type=jnp.float32
    )
    fresh_state = jnp.einsum(
        "bshk,bshv->bhkv", tail_low, head_values, preferred_element_type=jnp.float32
    )
    empty_state = jnp.zeros_like(fresh_state)
    state_in = empty_state
    for relay_turn in range(lax.axis_size("seq") - 1):
        state_in = from_behind(carry_decay[None, :, :, None] * state_in + fresh_state, "seq", 1)
    inter = jnp.einsum("bthk,bhkv->bthv", reach_wide, state_in, precision=precise)
    mixer = (within + inter).reshape(token_count, model_width).astype(jnp.bfloat16)
    resid = inputs + jnp.dot(mixer, out_full, preferred_element_type=jnp.float32)
    normed_two = layer_norm(resid, gain_two, bias_two).astype(jnp.bfloat16)
    hidden_pre = jnp.dot(normed_two, up_full, preferred_element_type=jnp.float32)
    hidden = jax.nn.gelu(hidden_pre).astype(jnp.bfloat16)
    result = resid + jnp.dot(hidden, down_full, preferred_element_type=jnp.float32)
    mixed = result.reshape(flat_shape).astype(jnp.bfloat16)
    qkv_full, out_full, up_full, down_full = (
        lax.all_gather(qkv_weight, "dp", axis=0, tiled=True),
        lax.all_gather(out_weight, "dp", axis=0, tiled=True),
        lax.all_gather(up_weight, "dp", axis=0, tiled=True),
        lax.all_gather(down_weight, "dp", axis=0, tiled=True),
    )
    positions = lax.axis_index("seq") * block_len + jnp.arange(block_len, dtype=jnp.int32)
    keep_mask = (positions[None, :] < lengths[:, None]).astype(jnp.float32)
    grad_rows = (out_grad.astype(jnp.float32) * keep_mask[:, :, None]).reshape(
        token_count, model_width
    )
    grad_low = grad_rows.astype(jnp.bfloat16)
    down_grad = outer_sum(hidden, grad_low)
    hidden_grad = back_product(grad_low, down_full)
    _, gelu_back = jax.vjp(jax.nn.gelu, hidden_pre)
    pre_grad = gelu_back(hidden_grad)[0].astype(jnp.bfloat16)
    up_grad = outer_sum(normed_two, pre_grad)
    _, norm_two_back = jax.vjp(layer_norm, resid, gain_two, bias_two)
    resid_part, gain_two_grad, bias_two_grad = norm_two_back(back_product(pre_grad, up_full))
    resid_grad = grad_rows + resid_part
    branch_grad = resid_grad.astype(jnp.bfloat16)
    proj_grad = outer_sum(mixer, branch_grad)
    mixer_low = back_product(branch_grad, out_full).astype(jnp.bfloat16).reshape(head_shape)
    mixer_wide = mixer_low.astype(jnp.float32)
    local_grad = jnp.einsum("bthk,bthv->bhkv", reach_wide, mixer_wide, precision=precise)
    state_grad = empty_state
    for relay_turn in range(lax.axis_size("seq") - 1):
        state_grad = from_behind(
            as_sent(carry_decay[None, :, :, None] * state_grad + local_grad), "seq", -1
        )
    score_grad = jnp.einsum(
        "bthv,bshv->bhts", mixer_low, head_values, preferred_element_type=jnp.float32
    ).astype(jnp.bfloat16)
    score_grad = jnp.where(causal, score_grad, jnp.zeros_like(score_grad))
    decayed_grad = jnp.einsum(
        "bhts,bshk->bthk", score_grad, lifted_low, preferred_element_type=jnp.float32
    )
    lifted_grad = jnp.einsum(
        "bhts,bthk->bshk", score_grad, decayed_low, preferred_element_type=jnp.float32
    )
    value_grad = jnp.einsum(
        "bhts,bthv->bshv", scores_low, mixer_low, preferred_element_type=jnp.float32
    )
    value_grad = value_grad + jnp.einsum(
        "bshk,bhkv->bshv", tail_low.astype(jnp.float32), state_grad, precision=precise
    )
    tail_grad = jnp.einsum(
        "bshv,bhkv->bshk", head_values.astype(jnp.float32), state_grad, precision=precise
    )
    reach_grad = jnp.einsum("bthv,bhkv->bthk", mixer_wide, state_in, precision=precise)
    carry_grad = jnp.sum(state_grad * state_in, axis=(0, 3))
    _, factor_back = jax.vjp(factors, head_queries, head_keys, rate_vector)
    query_grad, key_grad, rate_grad = factor_back(
        (decayed_grad, lifted_grad, tail_grad, reach_grad, carry_grad)
    )
    _, shift_back = jax.vjp(shift_mix, extended, tap_table)
    extended_grad, taps_grad = shift_back(key_grad.reshape(flat_shape))
    spill = from_behind(extended_grad[:, :3], "seq", -1)
    keys_grad = jnp.concatenate(
        [extended_grad[:, 3:block_len], extended_grad[:, block_len:] + spill], axis=1
    )
    qkv_grad_low = jnp.concatenate(
        [query_grad.reshape(flat_shape), keys_grad, value_grad.reshape(flat_shape)], axis=2
    )
    qkv_grad_low = qkv_grad_low.reshape(token_count, 3 * model_width).astype(jnp.bfloat16)
    qkv_grad = outer_sum(normed_one, qkv_grad_low)
    _, norm_one_back = jax.vjp(layer_norm, inputs, gain_one, bias_one)
    input_part, gain_one_grad, bias_one_grad = norm_one_back(back_product(qkv_grad_low, qkv_full))
    input_grad = (resid_grad + input_part).reshape(flat_shape)
    reduced = (
        lax.psum_scatter(gain_one_grad, "dp", scatter_dimension=0, tiled=True),
        lax.psum_scatter(bias_one_grad, "dp", scatter_dimension=0, tiled=True),
        lax.psum_scatter(qkv_grad, "dp", scatter_dimension=0, tiled=True),
        lax.psum_scatter(taps_grad, "dp", scatter_dimension=1, tiled=True),
        lax.psum_scatter(rate_grad, "dp", scatter_dimension=0, tiled=True),
        lax.psum_scatter(proj_grad, "dp", scatter_dimension=0, tiled=True),
        lax.psum_scatter(gain_two_grad, "dp", scatter_dimension=0, tiled=True),
        lax.psum_scatter(bias_two_grad, "dp", scatter_dimension=0, tiled=True),
        lax.psum_scatter(up_grad, "dp", scatter_dimension=0, tiled=True),
        lax.psum_scatter(down_grad, "dp", scatter_dimension=0, tiled=True),
    )
    summed = lax.psum(
        (
            reduced[0],
            reduced[1],
            reduced[2],
            reduced[3],
            reduced[4],
            reduced[5],
            reduced[6],
            reduced[7],
            reduced[8],
            reduced[9],
        ),
        "seq",
    )
    return (
        mixed,
        input_grad,
        summed[0],
        summed[1],
        summed[2],
        summed[3],
        summed[4],
        summed[5],
        summed[6],
        summed[7],
        summed[8],
        summed[9],
    )


def near(
    tokens,
    ln1_gain,
    ln1_bias,
    qkv_weight,
    shift_taps,
    decay_rates,
    out_weight,
    ln2_gain,
    ln2_bias,
    up_weight,
    down_weight,
    lengths,
    out_grad,
):
    width = tokens.shape[2]
    own = ln1_gain.shape[0]
    packed = jnp.concatenate(
        [
            jnp.stack([ln1_gain, ln1_bias, decay_rates, ln2_gain, ln2_bias]),
            shift_taps,
            jnp.zeros((7, own), LOW),
        ],
        axis=0,
    )
    start = lax.axis_index("dp") * own
    packed = lax.dynamic_update_slice(jnp.zeros((16, width), LOW), packed, (0, start))
    (
        mixed, normed, qkv, edges, state_in, mixer, resid_grad, weights, vectors, two_sums, up_half, down_half,
    ) = front(packed, qkv_weight, out_weight, up_weight, down_weight, tokens, out_grad, lengths)
    input_grad, up_sum, down_sum, out_sum, qkv_sum, small = back(
        resid_grad, mixer, qkv, edges, state_in, normed, tokens, weights, vectors, two_sums, up_half, down_half,
    )
    small = lax.dynamic_slice(small, (0, start), (16, own))
    return (
        mixed, input_grad, small[0], small[1], qkv_sum, small[3:7], small[2], out_sum, small[8], small[9],
        up_sum, down_sum,
    )


def solution(mesh):
    in_specs = (
        P("dp", "seq", None),
        P("dp"),
        P("dp"),
        P("dp", None),
        P(None, "dp"),
        P("dp"),
        P("dp", None),
        P("dp"),
        P("dp"),
        P("dp", None),
        P("dp", None),
        P("dp"),
        P("dp", "seq", None),
    )
    out_specs = (
        P("dp", "seq", None),
        P("dp", "seq", None),
        P("dp"),
        P("dp"),
        P("dp", None),
        P(None, "dp"),
        P("dp"),
        P("dp", None),
        P("dp"),
        P("dp"),
        P("dp", None),
        P("dp", None),
    )
    local = near if dict(mesh.shape) == {"dp": 16, "seq": 2} else general
    return jax.shard_map(local, mesh=mesh, in_specs=in_specs, out_specs=out_specs, check_vma=False)
```

```python
import functools

import jax
import jax.numpy as jnp
from jax import lax
from jax.experimental import pallas as pl
from jax.experimental.pallas import tpu as pltpu
from jax.sharding import PartitionSpec as P

HEADS = 12
HEAD_DIM = 64
PAIR = 2 * HEAD_DIM
MESH = pl.DeviceIdType.MESH
MIB = 2**20
GELU_A = 0.7978845608028654
GELU_B = 0.044715
ROW_RATE, ROW_TAPS = 2, 5
LOW = jnp.bfloat16
WIDE = jnp.float32


precise = lax.Precision.HIGHEST


class Place:
    def __init__(self):
        self.dp = lax.axis_index("dp")
        self.core = lax.axis_index("seq")
        self.z = self.dp // 4
        self.stride_a = 2 - self.core
        self.stride_b = 1 + self.core
        self.a = (self.dp // self.stride_a) % 2
        self.b = (self.dp // self.stride_b) % 2

    def spot(self, da, db):
        return (self.a + da) % 2 * self.stride_a + (self.b + db) % 2 * self.stride_b

    def sibling_spot(self, da, db):
        return (self.b + da) % 2 * self.stride_b + (self.a + db) % 2 * self.stride_a

    def peer(self, dz, da, db):
        return ((self.z + dz) % 4 * 4 + self.spot(da, db), self.core)

    def sibling(self):
        return (self.dp, 1 - self.core)


PEERS = ((1, 0, 0), (2, 0, 0), (3, 0, 0), (0, 1, 0), (0, 0, 1))


def enter(place):
    barrier = pltpu.get_barrier_semaphore()
    for step in PEERS:
        pl.semaphore_signal(barrier, inc=1, device_id=place.peer(*step), device_id_type=MESH)
    pl.semaphore_signal(barrier, inc=1, device_id=place.sibling(), device_id_type=MESH)
    pl.semaphore_wait(barrier, len(PEERS) + 1)


def remote(source, target, send_sem, recv_sem, device):
    return pltpu.make_async_remote_copy(
        src_ref=source,
        dst_ref=target,
        send_sem=send_sem,
        recv_sem=recv_sem,
        device_id=device,
        device_id_type=MESH,
    )


def part(start, size, step):
    return pl.ds(pl.multiple_of(start, step), size)


class Unit:
    def __init__(self, shard, buffer, rows, tiles=None, start=0, width=None, shared=False, plane=False):
        self.shard, self.buffer, self.rows, self.tiles = shard, buffer, rows, tiles
        self.start, self.width, self.shared, self.plane = start, width, shared, plane

    def columns(self, side):
        if self.shared:
            return slice(None)
        return part(self.start + side * (self.width // 2), self.width // 2, 128)

    def own(self, side):
        if self.shared:
            return self.shard[0]
        columns = part(self.shard[1] + side * (self.width // 2), self.width // 2, 128)
        if self.tiles:
            return self.shard[0].at[pl.ds(*self.tiles), :, columns]
        return self.shard[0].at[:, columns]

    def at(self, z, rows, columns):
        if self.tiles:
            return self.buffer.at[pl.ds(*self.tiles), z, rows, columns]
        return self.buffer.at[z, rows, columns]

    def slab(self, spot, columns):
        return self.at(slice(None), part(spot * self.rows, self.rows, 16), columns)

    def floor(self, z, columns):
        return self.at(z, slice(None), columns)

    def block(self, z, spot, columns):
        return self.at(z, part(spot * self.rows, self.rows, 16), columns)


class Script:
    def __init__(self, events):
        self.events, self.done, self.held = events, 0, set()

    def take(self, count):
        chosen = []
        while len(chosen) < count and self.done < len(self.events):
            which, event = self.events[self.done]
            if which in self.held:
                break
            chosen.append(event)
            self.done += 1
        return chosen

    def tick(self, count=1000):
        for event in self.take(count):
            event()

    def points(self, trips, count, each=1, release=None):
        chosen = []
        for trip in range(trips):
            if release is not None:
                self.held -= release(trip)
            for _ in range(count):
                chosen.append(self.take(each))

        def run(index, point):
            for trip in range(trips):
                events = chosen[trip * count + point]
                if events:
                    @pl.when(index == trip)
                    def _(events=events):
                        for event in events:
                            event()

        return run


class Gather:
    def __init__(self, place, units, send_sem, recv_sem, local_sem):
        self.place, self.units = place, units
        self.send_sem, self.recv_sem, self.local_sem = send_sem, recv_sem, local_sem
        self.script = Script([])
        self.ready = {}
        events = self.script.events
        count = len(units)
        for turn in range(count + 2):
            for lag, step in enumerate((self.one, self.two, self.three)):
                if 0 <= turn - lag < count:
                    which = ORDER[turn - lag]
                    events.append((which, functools.partial(step, which)))
                    self.ready[which] = len(events)

    def need(self, which):
        self.script.tick(max(0, self.ready[which] - self.script.done))
        self.land(which)

    def land(self, which):
        unit, place = self.units[which], self.place
        if unit.shared:
            return
        other = unit.columns(1 - place.core)
        for slot, (da, db) in enumerate(((0, 0), (1, 0), (0, 1), (1, 1))):
            if unit.plane:
                window = unit.floor((place.z + slot) % 4, other)
            else:
                window = unit.slab(place.sibling_spot(da, db), other)
            pltpu.make_async_copy(window, window, self.recv_sem.at[which, 6 + slot]).wait()

    def copy(self, which, slot):
        unit, place = self.units[which], self.place
        mine = unit.columns(place.core)
        landing = slot
        if slot >= 6:
            device = place.sibling()
        elif unit.plane:
            device = place.peer(*((0, 1, 0), (0, 0, 1), (0, 0, 1), (1, 0, 0), (2, 0, 0), (3, 0, 0))[slot])
            landing = 8 - slot if slot >= 3 else slot
        else:
            device = place.peer(*((1, 0, 0), (2, 0, 0), (3, 0, 0), (0, 1, 0), (0, 0, 1), (0, 0, 1))[slot])
            landing = 2 - slot if slot < 3 else slot
        if unit.plane and slot < 3:
            target = unit.block(place.z, place.spot(1 if slot == 2 else 0, 0), mine)
            source = target if slot == 2 else unit.own(place.core)
        elif unit.plane:
            source = target = unit.floor((place.z + max(0, slot - 6)) % 4, mine)
        elif slot < 3:
            source, target = unit.own(place.core), unit.block(place.z, place.spot(0, 0), mine)
        else:
            da, db = ((0, 0), (0, 0), (1, 0), (0, 0), (1, 0), (0, 1), (1, 1))[slot - 3]
            source = target = unit.slab(place.spot(da, db), mine)
        return remote(
            source, target, self.send_sem.at[which, slot], self.recv_sem.at[which, landing], device
        )

    def stay(self, which):
        unit, place = self.units[which], self.place
        return pltpu.make_async_copy(
            unit.own(place.core),
            unit.block(place.z, place.spot(0, 0), unit.columns(place.core)),
            self.local_sem.at[which],
        )

    def start(self, which):
        self.stay(which).start()
        for slot in range(2 if self.units[which].plane else 3):
            self.copy(which, slot).start()

    def arrive(self, which, slot):
        unit, place = self.units[which], self.place
        mine = unit.columns(place.core)
        if unit.plane and slot < 3:
            window = unit.block(place.z, place.spot(*((1, 0), (0, 1), (1, 1))[slot]), mine)
        elif unit.plane:
            window = unit.floor((place.z + slot - 2) % 4, mine)
        elif slot < 3:
            window = unit.block((place.z + slot + 1) % 4, place.spot(0, 0), mine)
        else:
            window = unit.slab(place.spot(*((1, 0), (0, 1), (1, 1))[slot - 3]), mine)
        pltpu.make_async_copy(window, window, self.recv_sem.at[which, slot]).wait()

    def send(self, which, *slots):
        for slot in slots:
            if slot < 6 or not self.units[which].shared:
                self.copy(which, slot).start()

    def one(self, which):
        self.stay(which).wait()
        if self.units[which].plane:
            self.arrive(which, 0)
            self.send(which, 2)
            return
        for slot in range(3):
            self.arrive(which, slot)
        self.send(which, 3, 4, 6)

    def two(self, which):
        if self.units[which].plane:
            self.arrive(which, 1)
            self.arrive(which, 2)
            self.send(which, 3, 4, 5, 6)
            return
        self.arrive(which, 3)
        self.send(which, 5, 7)

    def three(self, which):
        if self.units[which].plane:
            for slot in range(3, 6):
                self.arrive(which, slot)
                self.send(which, slot + 4)
            return
        self.arrive(which, 4)
        self.send(which, 8)
        self.arrive(which, 5)
        self.send(which, 9)

    def drain(self):
        for which, unit in enumerate(self.units):
            for slot in range(6 if unit.shared else 10):
                self.copy(which, slot).wait_send()


def nt(left, right):
    return lax.dot_general(left, right, (((1,), (1,)), ((), ())), preferred_element_type=WIDE)


def tn(left, right):
    return lax.dot_general(left, right, (((0,), (0,)), ((), ())), preferred_element_type=WIDE)


def nn(left, right):
    return jnp.dot(left, right, preferred_element_type=WIDE)


def normalize(values):
    center = jnp.mean(values, axis=-1, keepdims=True)
    centered = values - center
    spread = jnp.mean(centered * centered, axis=-1, keepdims=True)
    scale = lax.rsqrt(spread + 1e-05)
    return centered * scale, scale


def normalize_back(grad, normed, scale, gain):
    weighted = grad * gain
    inner = weighted - jnp.mean(weighted, axis=-1, keepdims=True)
    inner = inner - normed * jnp.mean(weighted * normed, axis=-1, keepdims=True)
    return scale * inner


def lanes(pair):
    return pl.ds(pl.multiple_of(pair * PAIR, PAIR), PAIR)


def head_mask(rows, side):
    spots = lax.broadcasted_iota(jnp.int32, (rows, PAIR), 1)
    return (spots // HEAD_DIM) == side


def only(mask, values):
    return jnp.where(mask, values, jnp.zeros_like(values))


def same_head():
    first = lax.broadcasted_iota(jnp.int32, (PAIR, PAIR), 0) // HEAD_DIM
    second = lax.broadcasted_iota(jnp.int32, (PAIR, PAIR), 1) // HEAD_DIM
    return first == second


def lower(size):
    return lax.broadcasted_iota(jnp.int32, (size, size), 0) >= lax.broadcasted_iota(
        jnp.int32, (size, size), 1
    )


def split(values):
    high = values.astype(LOW)
    low = (values - high.astype(WIDE)).astype(LOW)
    return high, low


def spots_of(block_len):
    return lax.broadcasted_iota(jnp.int32, (block_len, 1), 0).astype(WIDE)


def shifted_keys(keys, slot, window, taps):
    block_len = keys.shape[1] - 8
    total = taps[0:1] * keys[slot, 8 : 8 + block_len, window]
    for lag in range(1, 4):
        total = total + taps[lag : lag + 1] * keys[slot, 8 - lag : 8 - lag + block_len, window]
    return total


LOTS = 6


def hidden_order(shard):
    size = shard.shape[1] // (16 * LOTS)
    pieces = [
        shard[:, (device * LOTS + lot) * size : (device * LOTS + lot + 1) * size]
        for lot in range(LOTS)
        for device in range(16)
    ]
    return jnp.concatenate(pieces, axis=1)


def hidden_disorder(columns):
    size = columns.shape[1] // (16 * LOTS)
    pieces = [
        columns[:, (lot * 16 + device) * size : (lot * 16 + device + 1) * size]
        for device in range(16)
        for lot in range(LOTS)
    ]
    return jnp.concatenate(pieces, axis=1)


VEC, KEY, VALUE, QUERY, OUT, DOWN, UP = range(7)
GROUPS = ((0, 2), (2, 2), (4, 1), (5, 1))
EARLY = 4
ORDER = tuple(range(13))
APART = 3


def front_kernel(
    lengths, packed, qkv_shard, out_shard, up_shard, down_shard, tokens_in, cotangent_in,
    mixed_out, normed_out, qkv_out, edges_out, state_out, mixer_out, resid_grad_out, weights_out,
    vectors_out, sums_out, up_out, down_out, up_b_out, down_b_out,
    vec_all, weights, up_all, down_all, up_own, tokens, grad_low, normed, qkv, edges, state_in,
    state_send, mixer, resid, normed_turned, keys, summed, vectors, sums,
    up_stage, down_stage, up_half, down_half, up_b, down_b,
    send_sem, recv_sem, local_sem, load_sem, save_sem, pair_send, pair_recv, tile_send, tile_recv,
    early_send, early_recv,
):
    slots, block_len, width = tokens.shape
    pairs = width // PAIR
    size = block_len // 2
    tiles = up_half.shape[0]
    place = Place()
    core = place.core
    first = core == 0
    queries, key_rows, values = qkv.at[0], qkv.at[1], qkv.at[2]
    normed_two, mixer_view = normed, mixer

    def load(slot, source, target):
        return pltpu.make_async_copy(source, target, load_sem.at[slot])

    def save(slot):
        source, target = (
            (mixer_view, mixed_out), (normed, normed_out), (qkv, qkv_out), (edges, edges_out),
            (state_in, state_out), (mixer, mixer_out), (keys.at[:, pl.ds(0, block_len)], resid_grad_out),
            (weights, weights_out), (vectors, vectors_out), (sums, sums_out),
            (up_half.at[pl.ds(EARLY, tiles - EARLY)], up_out),
            (down_half.at[pl.ds(EARLY, tiles - EARLY)], down_out), (up_b, up_b_out), (down_b, down_b_out),
        )[slot]
        return pltpu.make_async_copy(source, target, save_sem.at[slot])

    load(0, up_shard, up_own).start()
    load(1, tokens_in, tokens).start()
    load(2, cotangent_in, grad_low).start()
    enter(place)
    units = [
        Unit((packed, 0), vec_all, 16, shared=True),
        Unit((qkv_shard, width), weights.at[1], 48, width=width),
        Unit((qkv_shard, 2 * width), weights.at[2], 48, width=width),
        Unit((qkv_shard, 0), weights.at[0], 48, width=width),
        Unit((out_shard, 0), weights.at[3], 48, width=width),
    ]
    for lot, count in GROUPS:
        units.append(Unit((down_shard, 0), down_all, 32, tiles=(lot, count), width=width))
        units.append(Unit((up_own, lot * 512), up_all, 48, start=lot * 512, width=count * 512))
    gather = Gather(place, units, send_sem, recv_sem, local_sem)
    for which in range(5):
        gather.start(which)
    load(0, up_shard, up_own).wait()
    up_own[...] = hidden_order(up_own[...])
    for which in range(5, len(units)):
        gather.start(which)

    load(1, tokens_in, tokens).wait()
    gather.need(VEC)
    vectors[...] = sum(
        vec_all[z, spot * 16 : spot * 16 + 16].astype(WIDE) for z in range(4) for spot in range(4)
    )
    gain, bias = vectors[0:1], vectors[1:2]
    for slot in range(slots):
        rows = slice(slot * block_len, (slot + 1) * block_len)
        hat, _ = normalize(tokens[slot].astype(WIDE))
        normed[rows] = (hat * gain + bias).astype(LOW)
    save(1).start()
    save(8).start()
    load(2, cotangent_in, grad_low).wait()
    base = core * block_len
    for slot in range(slots):
        keep = base + lax.broadcasted_iota(jnp.int32, (block_len, 1), 0) < lengths[slot]
        grad_low[slot] = (grad_low[slot].astype(WIDE) * keep.astype(WIDE)).astype(LOW)

    def weight(which):
        return weights[which].reshape(width, width)

    def project(which):
        for slot in range(slots):
            rows = slice(slot * block_len, (slot + 1) * block_len)
            qkv[which, slot] = nn(normed[rows], weight(which)).astype(LOW)

    gather.need(KEY)
    project(1)
    edge_copy = remote(
        key_rows.at[:, pl.ds(block_len - 16, 16)], edges, pair_send.at[0], pair_recv.at[0], place.sibling()
    )

    @pl.when(first)
    def _():
        edge_copy.start()

    gather.need(VALUE)
    project(2)
    gather.need(QUERY)
    project(0)
    save(2).start()

    @pl.when(first)
    def _():
        edge_copy.wait_send()
        edges[...] = jnp.zeros_like(edges)

    @pl.when(core == 1)
    def _():
        edge_copy.wait_recv()

    save(3).start()
    for slot in range(slots):
        keys[slot, 0:8] = edges[slot].astype(WIDE)[8:16]
        keys[slot, 8:] = key_rows[slot].astype(WIDE)
    spots = spots_of(block_len)
    state_copy = remote(state_send, state_in, pair_send.at[1], pair_recv.at[1], place.sibling())

    @pl.when(first)
    def _():
        def fresh(pair, carry):
            window = lanes(pair)
            rate = vectors[ROW_RATE : ROW_RATE + 1, window]
            taps = vectors[ROW_TAPS : ROW_TAPS + 4, window]
            tail = jnp.exp(-rate * (block_len - 1.0 - spots))
            for slot in range(slots):
                tail_keys = (shifted_keys(keys, slot, window, taps) * tail).astype(LOW)
                state_send[pair, slot] = only(same_head(), tn(tail_keys, values[slot, :, window]))
            return carry

        lax.fori_loop(0, pairs, fresh, 0)
        state_copy.start()

    gather.script.tick(2)

    spread_within = gather.script.points(pairs, 1)

    def within(pair, carry):
        spread_within(pair, 0)
        window = lanes(pair)
        rate = vectors[ROW_RATE : ROW_RATE + 1, window]
        taps = vectors[ROW_TAPS : ROW_TAPS + 4, window]
        fall = jnp.exp(-rate * spots)
        rise = jnp.exp(rate * spots)
        for slot in range(slots):
            decayed = (queries[slot, :, window].astype(WIDE) * fall).astype(LOW)
            lifted = (shifted_keys(keys, slot, window, taps) * rise).astype(LOW)
            value = values[slot, :, window]
            top = jnp.zeros((size, PAIR), WIDE)
            low = jnp.zeros((size, PAIR), WIDE)
            for side in range(2):
                query_side = only(head_mask(block_len, side), decayed)
                value_side = only(head_mask(block_len, side), value)
                near = jnp.where(lower(size), nt(query_side[:size], lifted[:size]), 0.0)
                top = top + nn(near.astype(LOW), value_side[:size])
                far = nt(query_side[size:], lifted[:size]).astype(LOW)
                near = jnp.where(lower(size), nt(query_side[size:], lifted[size:]), 0.0)
                low = low + nn(far, value_side[:size]) + nn(near.astype(LOW), value_side[size:])
            summed[slot, :size, window] = top
            summed[slot, size:, window] = low
        return carry

    lax.fori_loop(0, pairs, within, 0)

    @pl.when(first)
    def _():
        state_copy.wait_send()
        state_in[...] = jnp.zeros_like(state_in)

    @pl.when(core == 1)
    def _():
        state_copy.wait_recv()

        def reach(pair, carry):
            window = lanes(pair)
            rate = vectors[ROW_RATE : ROW_RATE + 1, window]
            decay = jnp.exp(-rate * (spots + 1.0))
            for slot in range(slots):
                reaching = (queries[slot, :, window].astype(WIDE) * decay).astype(LOW)
                high, low = split(state_in[pair, slot])
                summed[slot, :, window] += nn(reaching, high) + nn(reaching, low)
            return carry

        lax.fori_loop(0, pairs, reach, 0)

    save(4).start()
    gather.need(OUT)
    save(7).start()
    gain_two, bias_two = vectors[3:4], vectors[4:5]
    for slot in range(slots):
        rows = slice(slot * block_len, (slot + 1) * block_len)
        if slot == 0:
            save(1).wait()
        mixer[slot] = summed[slot].astype(LOW)
        total = tokens[slot].astype(WIDE) + nn(mixer[slot], weight(3))
        resid[slot] = total
        summed[slot] = total
        hat, _ = normalize(total)
        normed_two[rows] = (hat * gain_two + bias_two).astype(LOW)
    save(5).start()
    normed_turned[...] = normed_two[...].T
    keys[:, 0:block_len] = jnp.zeros((slots, block_len, width), WIDE)
    gather.need(DOWN)
    gather.need(UP)

    def tile_copies(tile):
        slot = tile % 2
        other = 1 - core
        return (
            remote(
                up_stage.at[slot, :, :, part(other * 256, 256, 128)],
                up_half.at[tile],
                tile_send.at[tile, 0],
                tile_recv.at[tile, 0],
                place.sibling(),
            ),
            remote(
                down_stage.at[slot, :, :, part(other * 384, 384, 128)],
                down_half.at[tile],
                tile_send.at[tile, 1],
                tile_recv.at[tile, 1],
                place.sibling(),
            ),
        )

    def merge(tile):
        for copy in tile_copies(tile):
            copy.wait_recv()
        slot = tile % 2
        up_half[tile] = up_half[tile] + up_stage[slot, :, :, part(core * 256, 256, 128)]
        down_half[tile] = down_half[tile] + down_stage[slot, :, :, part(core * 384, 384, 128)]

    shares = [
        Share(up_half.at[k], up_half.at[k], up_b.at[k], None, None, None, 48) for k in range(EARLY)
    ] + [
        Share(down_half.at[k], down_half.at[k], down_b.at[k], None, None, None, 32) for k in range(EARLY)
    ]
    early = Reduction(place, shares, early_send, early_recv)
    spread = gather.script.points(tiles, 3)

    def ffn_tile(tile, carry):
        for group in range(1, len(GROUPS)):
            @pl.when(tile == GROUPS[group][0])
            def _(group=group):
                gather.land(DOWN + 2 * group)
                gather.land(UP + 2 * group)

        spread(tile, 0)
        columns = part(tile * 512, 512, 512)
        up = up_all[:, :, columns].reshape(width, 512)
        down = down_all[tile].reshape(512, width)
        cotangent = grad_low[...].reshape(slots * block_len, width)
        pre = nn(normed_two[...], up)
        wide = nt(cotangent, down)
        square = pre * pre
        ramp = jnp.tanh(pre * (GELU_A + (GELU_A * GELU_B) * square))
        half = 0.5 + 0.5 * ramp
        slope = half + (0.5 * pre) * (1.0 - ramp * ramp) * (
            GELU_A + (3.0 * GELU_A * GELU_B) * square
        )
        act = (pre * half).astype(LOW)
        back = (wide * slope).astype(LOW)
        spread(tile, 1)

        @pl.when(tile >= 1)
        def _():
            merge(tile - 1)

        for k in range(EARLY):
            @pl.when(tile == k + 1)
            def _(k=k):
                early.start(k)
                early.start(EARLY + k)

        for slot in range(slots):
            rows = slice(slot * block_len, (slot + 1) * block_len)
            summed[slot] += nn(act[rows], down)
            keys[slot, 0:block_len] += nt(back[rows], up)
        turn = tile % 2
        spread(tile, 2)

        @pl.when(tile >= 2)
        def _():
            for copy in tile_copies(tile - 2):
                copy.wait_send()

        up_stage[turn] = nn(normed_turned[...], back).astype(LOW).reshape(4, width // 4, 512)
        down_stage[turn] = tn(act, cotangent).astype(LOW).reshape(4, 128, width)
        for copy in tile_copies(tile):
            copy.start()
        return carry

    lax.fori_loop(0, tiles, ffn_tile, 0)
    sums[...] = jnp.zeros_like(sums)
    for slot in range(slots):
        if slot == 0:
            save(5).wait()
        mixer[slot] = summed[slot].astype(LOW)
        hat, scale = normalize(resid[slot])
        grad = keys[slot, 0:block_len]
        sums[0:1] += jnp.sum(grad * hat, axis=0, keepdims=True)
        sums[1:2] += jnp.sum(grad, axis=0, keepdims=True)
        keys[slot, 0:block_len] = grad_low[slot].astype(WIDE) + normalize_back(grad, hat, scale, gain_two)
    save(0).start()
    save(6).start()
    save(9).start()
    for k in range(EARLY):
        early.merge_b(k)
        early.merge_b(EARLY + k)
    save(12).start()
    save(13).start()
    merge(tiles - 1)
    save(10).start()
    save(11).start()
    for tile in (tiles - 2, tiles - 1):
        for copy in tile_copies(tile):
            copy.wait_send()
    gather.script.tick()
    gather.drain()
    early.drain()
    for slot in (0, 2, 3, 4, 6, 7, 8, 9, 10, 11, 12, 13):
        save(slot).wait()


def front(packed, qkv_weight, out_weight, up_weight, down_weight, tokens, cotangent, lengths):
    slots, block_len, width = tokens.shape
    count = slots * block_len
    pairs = width // PAIR
    hidden = up_weight.shape[1]
    tiles = hidden // 512
    shape = jax.ShapeDtypeStruct
    outs = [
        shape(tokens.shape, LOW),
        shape((count, width), LOW),
        shape((3, slots, block_len, width), LOW),
        shape((slots, 16, width), LOW),
        shape((pairs, slots, PAIR, PAIR), WIDE),
        shape(tokens.shape, LOW),
        shape(tokens.shape, WIDE),
        shape((4, 4, width // 4, width), LOW),
        shape((16, width), WIDE),
        shape((8, width), WIDE),
        shape((tiles - EARLY, 4, width // 4, 256), LOW),
        shape((tiles - EARLY, 4, 128, width // 2), LOW),
        shape((EARLY, 2, 4, width // 16, 256), LOW),
        shape((EARLY, 2, 4, 32, width // 2), LOW),
    ]
    vmem = lambda *dims: pltpu.VMEM(dims, LOW)
    wide = lambda *dims: pltpu.VMEM(dims, WIDE)
    dma = pltpu.SemaphoreType.DMA
    anywhere = pl.BlockSpec(memory_space=pltpu.HBM)
    return pl.pallas_call(
        front_kernel,
        out_shape=outs,
        in_specs=[pl.BlockSpec(memory_space=pltpu.SMEM)] + [anywhere] * 7,
        out_specs=[anywhere] * len(outs),
        scratch_shapes=[
            vmem(4, 64, width),
            vmem(4, 4, width // 4, width),
            vmem(4, width // 4, hidden),
            vmem(tiles, 4, 128, width),
            vmem(width // 16, hidden),
            vmem(slots, block_len, width),
            vmem(slots, block_len, width),
            vmem(count, width),
            vmem(3, slots, block_len, width),
            vmem(slots, 16, width),
            wide(pairs, slots, PAIR, PAIR),
            wide(pairs, slots, PAIR, PAIR),
            vmem(slots, block_len, width),
            wide(slots, block_len, width),
            vmem(width, count),
            wide(slots, block_len + 8, width),
            wide(slots, block_len, width),
            wide(16, width),
            wide(8, width),
            vmem(2, 4, width // 4, 512),
            vmem(2, 4, 128, width),
            vmem(tiles, 4, width // 4, 256),
            vmem(tiles, 4, 128, width // 2),
            vmem(EARLY, 2, 4, width // 16, 256),
            vmem(EARLY, 2, 4, 32, width // 2),
            dma((13, 10)),
            dma((13, 10)),
            dma((13,)),
            dma((3,)),
            dma((14,)),
            dma((2,)),
            dma((2,)),
            dma((tiles, 2)),
            dma((tiles, 2)),
            dma((2 * EARLY, 2)),
            dma((2 * EARLY, 2)),
        ],
        compiler_params=pltpu.CompilerParams(
            collective_id=0, has_side_effects=True, vmem_limit_bytes=63 * MIB
        ),
        name="gather_forward_ffn",
    )(
        lengths, packed, qkv_weight, out_weight, up_weight, down_weight.reshape(tiles, 32, width), tokens,
        cotangent,
    )


class Share:
    def __init__(self, source, own, from_b, from_a, from_z, final, rows):
        self.source, self.own, self.rows = source, own, rows
        self.from_b, self.from_a, self.from_z, self.final = from_b, from_a, from_z, final

    def slab(self, ref, spot):
        return ref.at[:, part(spot * self.rows, self.rows, 16)]


class Reduction:
    def __init__(self, place, shares, send_sem, recv_sem):
        self.place, self.shares = place, shares
        self.send_sem, self.recv_sem = send_sem, recv_sem

    def copy(self, which, slot):
        share, place = self.shares[which], self.place
        if slot < 2:
            da = 1 - slot
            source = share.slab(share.source, place.spot(da, 1))
            target = share.from_b.at[(place.a + da) % 2]
            device = place.peer(0, 0, 1)
        elif slot == 2:
            source, target = share.from_b.at[1 - place.a], share.from_a
            device = place.peer(0, 1, 0)
        elif slot < 6:
            dz = slot - 2
            source, target = share.from_a.at[(place.z + dz) % 4], share.from_z.at[dz - 1]
            device = place.peer(dz, 0, 0)
        else:
            source = target = share.final.at[place.core]
            device = place.sibling()
        return remote(source, target, self.send_sem.at[which, slot], self.recv_sem.at[which, slot], device)

    def start(self, which):
        if self.shares[which].source is None:
            self.copy(which, 2).start()
            return
        for slot in range(2):
            self.copy(which, slot).start()

    def merge_b(self, which):
        share, place = self.shares[which], self.place
        for slot in range(2):
            self.copy(which, slot).wait_recv()
            da = 1 - slot
            a = (place.a + da) % 2
            rows = part(place.spot(da, 0) * share.rows, share.rows, 16)
            share.from_b[a] = share.from_b[a] + share.own[:, rows]
            if slot == 0 and share.from_a is not None:
                self.copy(which, 2).start()

    def merge_a(self, which):
        share = self.shares[which]
        self.copy(which, 2).wait_recv()
        share.from_a[...] = share.from_a[...] + share.from_b[self.place.a]
        for slot in range(3, 6):
            self.copy(which, slot).start()

    def finish(self, which):
        share, place = self.shares[which], self.place
        total = share.from_a[place.z].astype(WIDE)
        for slot in range(3):
            self.copy(which, 3 + slot).wait_recv()
            total = total + share.from_z[slot].astype(WIDE)
        share.final[place.core] = total
        self.copy(which, 6).start()

    def land(self, which):
        share, place = self.shares[which], self.place
        other = share.final.at[1 - place.core]
        pltpu.make_async_copy(other, other, self.recv_sem.at[which, 6]).wait()

    def drain(self):
        for which, share in enumerate(self.shares):
            first = 2 if share.source is None else 0
            for slot in range(first, 2 if share.from_a is None else 7):
                self.copy(which, slot).wait_send()

    def events(self, order):
        steps = []
        for which in order:
            own = [self.merge_b] if self.shares[which].source is not None else []
            steps.append([functools.partial(f, which) for f in own + [self.merge_a, self.finish]])
        events = []
        for turn in range(len(steps) + 3 * APART):
            for which in range(len(steps)):
                step, rest = divmod(turn - which, APART)
                if rest == 0 and 0 <= step < len(steps[which]):
                    events.append((order[which], steps[which][step]))
        return events


UPS, DOWNS, OUTS, PAIRS, KEYS = 0, 6, 12, 13, 19


def back_kernel(
    resid_grad_in, mixer_in, qkv_in, edges_in, state_in_in, normed_in, tokens_in, weights_in,
    vectors_in, two_sums, up_in, down_in, up_b_in, down_b_in,
    input_grad_out, up_sum, down_sum, out_sum, qkv_sum, small_out,
    resid_grad, mixer, qkv, edges, state_in, normed, weights, vectors, up_half, down_half,
    keys, branch, back_rows, projected, key_back, normed_turned, state_send, state_grad,
    out_stage, out_half, pair_stage, pair_half, key_half,
    up_b, up_a, up_z, up_final, down_b, down_a, down_z, down_final, wide_b, wide_a, wide_z, wide_final,
    pair_b, pair_a, pair_z, pair_final, small, small_sums, small_from,
    send_sem, recv_sem, load_sem, save_sem, core_send, core_recv, pair_send, pair_recv,
    small_send, small_recv, key_send, key_recv,
):
    slots, block_len, width = resid_grad.shape
    pairs = width // PAIR
    size = block_len // 2
    place = Place()
    core = place.core
    first = core == 0
    second = core == 1
    queries, key_rows, values = qkv.at[0], qkv.at[1], qkv.at[2]
    inputs = (
        (resid_grad_in, resid_grad), (weights_in, weights), (vectors_in, vectors), (qkv_in, qkv),
        (mixer_in, mixer), (edges_in, edges), (state_in_in, state_in), (normed_in, normed),
        (up_in, up_half), (down_in, down_half), (up_b_in, up_b.at[pl.ds(0, EARLY)]),
        (down_b_in, down_b.at[pl.ds(0, EARLY)]), (tokens_in, mixer),
    )
    LOAD_GRAD, LOAD_WEIGHTS, LOAD_VECTORS, LOAD_QKV, LOAD_MIXER, LOAD_EDGES, LOAD_STATE = range(7)
    LOAD_NORMED, LOAD_UP, LOAD_DOWN, LOAD_UP_B, LOAD_DOWN_B, LOAD_TOKENS = range(7, 13)

    def load(slot):
        return pltpu.make_async_copy(*inputs[slot], load_sem.at[slot])

    for slot in (
        LOAD_UP, LOAD_DOWN, LOAD_UP_B, LOAD_DOWN_B, LOAD_GRAD, LOAD_WEIGHTS, LOAD_VECTORS, LOAD_QKV,
        LOAD_MIXER, LOAD_EDGES, LOAD_STATE, LOAD_NORMED,
    ):
        load(slot).start()
    enter(place)
    tiles = EARLY + up_half.shape[0]

    def tile_share(k, halves, from_b, from_a, from_z, final, rows):
        own = None if k < EARLY else halves.at[k - EARLY]
        return Share(own, own, from_b.at[k], from_a.at[k], from_z.at[k], final.at[k], rows)

    def column_share(half, k):
        return Share(half, half, wide_b.at[k], wide_a.at[k], wide_z.at[k], wide_final.at[k], 48)

    def pair_share(half, k):
        return Share(half, half, pair_b.at[k], pair_a.at[k], pair_z.at[k], pair_final.at[k], 48)

    shares = [tile_share(k, up_half, up_b, up_a, up_z, up_final, 48) for k in range(tiles)]
    shares += [tile_share(k, down_half, down_b, down_a, down_z, down_final, 32) for k in range(tiles)]
    shares.append(column_share(out_half, 0))
    shares += [pair_share(pair_half.at[k], k) for k in range(pairs)]
    shares += [pair_share(key_half.at[k], pairs + k) for k in range(3)]
    reduction = Reduction(place, shares, send_sem, recv_sem)
    for slot in (LOAD_UP, LOAD_DOWN, LOAD_UP_B, LOAD_DOWN_B):
        load(slot).wait()
    order = [kind + k for k in range(tiles) for kind in (UPS, DOWNS)]
    for which in order[2 * EARLY :] + order[: 2 * EARLY]:
        reduction.start(which)
    order += [OUTS, *range(PAIRS, PAIRS + pairs), *range(KEYS, KEYS + 3)]
    script = Script(reduction.events(order))
    script.held = {OUTS, *range(PAIRS, PAIRS + pairs), *range(KEYS, KEYS + 3)}
    spots = spots_of(block_len)

    load(LOAD_GRAD).wait()
    load(LOAD_WEIGHTS).wait()
    out_weight = weights[3].reshape(width, width)
    for slot in range(slots):
        rows = slice(slot * block_len, (slot + 1) * block_len)
        branch[rows] = resid_grad[slot].astype(LOW)
        back_rows[slot] = nt(branch[rows], out_weight).astype(LOW)
    load(LOAD_VECTORS).wait()
    load(LOAD_QKV).wait()
    state_copy = remote(state_send, state_grad, core_send.at[0], core_recv.at[0], place.sibling())

    @pl.when(second)
    def _():
        def gather_state(pair, carry):
            window = lanes(pair)
            rate = vectors[ROW_RATE : ROW_RATE + 1, window]
            decay = jnp.exp(-rate * (spots + 1.0))
            for slot in range(slots):
                reaching = (queries[slot, :, window].astype(WIDE) * decay).astype(LOW)
                back = back_rows[slot, :, window]
                state_send[pair, slot] = only(same_head(), tn(reaching, back)).astype(LOW)
            return carry

        lax.fori_loop(0, pairs, gather_state, 0)
        state_copy.start()

    load(LOAD_MIXER).wait()
    normed_turned[...] = mixer[...].T
    out_stage[...] = nn(normed_turned[...], branch[...]).astype(LOW).reshape(4, width // 4, width)

    load(LOAD_TOKENS).start()

    def key_copy(k):
        window = part((1 - core) * (width // 2) + k * PAIR, PAIR, 128)
        return remote(
            out_stage.at[:, :, window], key_half.at[k], key_send.at[k], key_recv.at[k], place.sibling()
        )

    out_copy = remote(
        out_stage.at[:, :, part((1 - core) * (width // 2), width // 2, 128)],
        out_half,
        core_send.at[2],
        core_recv.at[2],
        place.sibling(),
    )
    out_copy.start()
    load(LOAD_EDGES).wait()
    load(LOAD_STATE).wait()
    load(LOAD_NORMED).wait()
    normed_turned[...] = normed[...].T
    for slot in range(slots):
        keys[slot, 0:8] = edges[slot].astype(WIDE)[8:16]
        keys[slot, 8:] = key_rows[slot].astype(WIDE)
    out_copy.wait_recv()
    out_half[...] = out_half[...] + out_stage[:, :, part(core * (width // 2), width // 2, 128)]
    reduction.start(OUTS)
    script.held -= {OUTS}

    @pl.when(second)
    def _():
        state_copy.wait_send()
        state_grad[...] = jnp.zeros_like(state_grad)

    @pl.when(first)
    def _():
        state_copy.wait_recv()

    def pair_copy(pair):
        return remote(
            pair_stage.at[pair, 1 - core], pair_half.at[pair], pair_send.at[pair], pair_recv.at[pair],
            place.sibling(),
        )

    def merge_pair(pair):
        pair_copy(pair).wait_recv()
        pair_half[pair] = pair_half[pair] + pair_stage[pair, core]

    spread = script.points(
        pairs, 2, TICKS_BACK, lambda trip: {PAIRS + trip - 2} if trip >= 2 else set()
    )

    def back_pair(pair, carry):
        spread(pair, 0)
        window = lanes(pair)
        rate = vectors[ROW_RATE : ROW_RATE + 1, window]
        taps = vectors[ROW_TAPS : ROW_TAPS + 4, window]
        fall = jnp.exp(-rate * spots)
        rise = jnp.exp(rate * spots)
        tail = jnp.exp(-rate * (block_len - 1.0 - spots))
        decay = jnp.exp(-rate * (spots + 1.0))
        rate_grad = jnp.zeros((1, PAIR), WIDE)
        taps_grad = [jnp.zeros((1, PAIR), WIDE) for _ in range(4)]
        weight_grad = jnp.zeros((width, 2 * PAIR), WIDE)
        for slot in range(slots):
            if slot == 1:
                spread(pair, 1)
            query = queries[slot, :, window].astype(WIDE)
            key = shifted_keys(keys, slot, window, taps)
            value = values[slot, :, window]
            back = back_rows[slot, :, window]
            wide_decayed, wide_lifted = query * fall, key * rise
            wide_tail, wide_reach = key * tail, query * decay
            decayed, lifted = wide_decayed.astype(LOW), wide_lifted.astype(LOW)
            tail_keys = wide_tail.astype(LOW)
            decayed_turned, back_turned = decayed.T, back.T
            decayed_top = jnp.zeros((size, PAIR), WIDE)
            decayed_low = jnp.zeros((size, PAIR), WIDE)
            lifted_top = jnp.zeros((PAIR, size), WIDE)
            lifted_low = jnp.zeros((PAIR, size), WIDE)
            value_top = jnp.zeros((PAIR, size), WIDE)
            value_low = jnp.zeros((PAIR, size), WIDE)
            row_head = lax.broadcasted_iota(jnp.int32, (PAIR, block_len), 0) // HEAD_DIM
            for side in range(2):
                mask = head_mask(block_len, side)
                query_side, back_side = only(mask, decayed), only(mask, back)
                lifted_side = only(mask, lifted)
                query_turned = only(row_head == side, decayed_turned)
                back_side_turned = only(row_head == side, back_turned)
                causal = lower(size)
                halves_of = (slice(0, size), slice(size, block_len))
                for t, s in ((0, 0), (1, 0), (1, 1)):
                    score = nt(query_side[halves_of[t]], lifted[halves_of[s]])
                    grad = nt(back_side[halves_of[t]], value[halves_of[s]])
                    if t == s:
                        score, grad = jnp.where(causal, score, 0.0), jnp.where(causal, grad, 0.0)
                    score, grad = score.astype(LOW), grad.astype(LOW)
                    query_part = nn(grad, lifted_side[halves_of[s]])
                    lifted_part = nn(query_turned[:, halves_of[t]], grad)
                    value_part = nn(back_side_turned[:, halves_of[t]], score)
                    if t == 0:
                        decayed_top = decayed_top + query_part
                    else:
                        decayed_low = decayed_low + query_part
                    if s == 0:
                        lifted_top, value_top = lifted_top + lifted_part, value_top + value_part
                    else:
                        lifted_low, value_low = lifted_low + lifted_part, value_low + value_part
            decayed_grad = jnp.concatenate([decayed_top, decayed_low], axis=0)
            lifted_grad = jnp.concatenate([lifted_top.T, lifted_low.T], axis=0)
            value_grad = jnp.concatenate([value_top.T, value_low.T], axis=0)
            leaving = state_grad[pair, slot]
            entering = state_in[pair, slot]
            high, low = split(entering)
            value_grad = value_grad + nn(tail_keys, leaving)
            tail_grad = nt(value, leaving)
            reach_grad = nt(back, high) + nt(back, low)
            carry_grad = jnp.sum((leaving.astype(WIDE) * entering).T, axis=0, keepdims=True)
            key_grad = lifted_grad * rise + tail_grad * tail
            steps = (
                spots * (lifted_grad * wide_lifted - decayed_grad * wide_decayed)
                - (block_len - 1.0 - spots) * (tail_grad * wide_tail)
                - (spots + 1.0) * (reach_grad * wide_reach)
            )
            rate_grad = rate_grad + jnp.sum(steps, axis=0, keepdims=True)
            rate_grad = rate_grad - block_len * jnp.exp(-rate * block_len) * carry_grad
            query_low = (decayed_grad * fall + reach_grad * decay).astype(LOW)
            value_low_grad = value_grad.astype(LOW)
            projected[0, slot, :, window] = query_low
            projected[2, slot, :, window] = value_low_grad
            key_back[slot, 0:block_len, window] = key_grad
            for lag in range(4):
                lagged = keys[slot, 8 - lag : 8 - lag + block_len, window]
                taps_grad[lag] = taps_grad[lag] + jnp.sum(lagged * key_grad, axis=0, keepdims=True)
            rows = slice(slot * block_len, (slot + 1) * block_len)
            weight_grad = weight_grad + nn(
                normed_turned[:, rows], jnp.concatenate([query_low, value_low_grad], axis=1)
            )
        small[0:8, window] = jnp.concatenate(
            [jnp.zeros((2, PAIR), WIDE), rate_grad, *taps_grad, jnp.zeros((1, PAIR), WIDE)], axis=0
        )
        for side in range(2):
            pair_stage[pair, side] = (
                weight_grad[:, side * PAIR : (side + 1) * PAIR].astype(LOW).reshape(4, width // 4, PAIR)
            )
        pair_copy(pair).start()

        @pl.when(pair >= 1)
        def _():
            merge_pair(pair - 1)

        for k in range(1, pairs):
            @pl.when(pair == k)
            def _(k=k):
                reduction.start(PAIRS + k - 1)

        return carry

    lax.fori_loop(0, pairs, back_pair, 0)
    spill = remote(
        key_back.at[:, pl.ds(0, 8)],
        key_back.at[:, pl.ds(block_len, 8)],
        core_send.at[1],
        core_recv.at[1],
        place.sibling(),
    )

    @pl.when(second)
    def _():
        spill.start()
        key_back[:, block_len : block_len + 8] = jnp.zeros((slots, 8, width), WIDE)

    merge_pair(pairs - 1)
    reduction.start(PAIRS + pairs - 1)
    script.held -= set(range(PAIRS, PAIRS + pairs))
    out_copy.wait_send()

    @pl.when(first)
    def _():
        spill.wait_recv()

    spread_keys = script.points(pairs, 1, 1)

    def key_pair(pair, carry):
        spread_keys(pair, 0)
        window = lanes(pair)
        taps = vectors[ROW_TAPS : ROW_TAPS + 4, window]
        for slot in range(slots):
            total = taps[0:1] * key_back[slot, 0:block_len, window]
            for lag in range(1, 4):
                total = total + taps[lag : lag + 1] * key_back[slot, lag : lag + block_len, window]
            projected[1, slot, :, window] = total.astype(LOW)
        return carry

    lax.fori_loop(0, pairs, key_pair, 0)
    rows_all = projected[1].reshape(slots * block_len, width)
    out_stage[...] = nn(normed_turned[...], rows_all).astype(LOW).reshape(4, width // 4, width)
    for k in range(3):
        key_copy(k).start()
    script.tick(3)
    load(LOAD_TOKENS).wait()
    gain = vectors[0:1]
    gain_sum = jnp.zeros((1, width), WIDE)
    bias_sum = jnp.zeros((1, width), WIDE)
    for slot in range(slots):
        grad = nt(projected[0, slot], weights[0].reshape(width, width))
        for third in range(1, 3):
            grad = grad + nt(projected[third, slot], weights[third].reshape(width, width))
        if slot == 0:
            for k in range(3):
                key_copy(k).wait_recv()
                window = part(core * (width // 2) + k * PAIR, PAIR, 128)
                key_half[k] = key_half[k] + out_stage[:, :, window]
                reduction.start(KEYS + k)
            script.held.clear()
        script.tick(4)
        hat, scale = normalize(mixer[slot * block_len : (slot + 1) * block_len].astype(WIDE))
        gain_sum = gain_sum + jnp.sum(grad * hat, axis=0, keepdims=True)
        bias_sum = bias_sum + jnp.sum(grad, axis=0, keepdims=True)
        resid_grad[slot] = resid_grad[slot] + normalize_back(grad, hat, scale, gain)
        pltpu.make_async_copy(
            resid_grad.at[slot], input_grad_out.at[slot], save_sem.at[slot]
        ).start()
        script.tick(4)
    small[0:1], small[1:2] = gain_sum, bias_sum
    small[8:16] = two_sums[...]

    def small_copy(slot):
        flip_x = (place.dp + 1 - 2 * (place.dp % 2), core)
        flip_y = (place.dp + 2 - 4 * ((place.dp // 2) % 2), core)
        source = small if slot == 0 else small_sums.at[min(slot, 3) - 1]
        device = (place.sibling(), flip_x, flip_y)[slot] if slot < 3 else place.peer(slot - 2, 0, 0)
        return remote(source, small_from.at[slot], small_send.at[slot], small_recv.at[slot], device)

    small_copy(0).start()
    for slot in range(3):
        script.tick(2)
        small_copy(slot).wait_recv()
        before = small[...] if slot == 0 else small_sums[slot - 1]
        small_sums[slot] = before + small_from[slot]
        if slot < 2:
            small_copy(slot + 1).start()
    for slot in range(3, 6):
        small_copy(slot).start()
    script.tick()
    for slot in range(3, 6):
        small_copy(slot).wait_recv()
    small_from[2] = small_sums[2]
    total = jnp.zeros(small.shape, WIDE)
    for z in range(4):
        total = total + small_from[2 + (place.z + 4 - z) % 4]
    small_out[...] = total
    for which in range(len(shares)):
        reduction.land(which)
    ups = [up_final[tile, side] for tile in range(6) for side in range(2)]
    up_sum[...] = hidden_disorder(jnp.concatenate(ups, axis=1))
    for side in range(2):
        half = slice(side * 384, side * 384 + 384)
        for tile in range(tiles):
            down_sum[tile * 32 : tile * 32 + 32, half] = down_final[tile, side]
        out_sum[:, half] = wide_final[0, side]
        for k in range(3):
            start = width + side * 384 + k * PAIR
            qkv_sum[:, start : start + PAIR] = pair_final[pairs + k, side]
        for pair in range(pairs):
            start = 2 * width * side + pair * PAIR
            qkv_sum[:, start : start + PAIR] = pair_final[pair, side]
    reduction.drain()
    for slot in range(6):
        small_copy(slot).wait_send()
    for pair in range(pairs):
        pair_copy(pair).wait_send()
    for k in range(3):
        key_copy(k).wait_send()

    @pl.when(second)
    def _():
        spill.wait_send()

    for slot in range(slots):
        pltpu.make_async_copy(
            resid_grad.at[slot], input_grad_out.at[slot], save_sem.at[slot]
        ).wait()


TICKS_BACK = 2


def back(
    resid_grad, mixer, qkv, edges, state_in, normed, tokens, weights, vectors, two_sums, up_half, down_half, up_b, down_b,
):
    slots, block_len, width = tokens.shape
    count = slots * block_len
    pairs = width // PAIR
    shape = jax.ShapeDtypeStruct
    outs = [
        shape(tokens.shape, WIDE),
        shape((width // 16, 4 * width), WIDE),
        shape((4 * width // 16, width), WIDE),
        shape((width // 16, width), WIDE),
        shape((width // 16, 3 * width), WIDE),
        shape((16, width), WIDE),
    ]
    low = lambda *dims: pltpu.VMEM(dims, LOW)
    wide = lambda *dims: pltpu.VMEM(dims, WIDE)
    dma = pltpu.SemaphoreType.DMA
    vmem = pl.BlockSpec(memory_space=pltpu.VMEM)
    anywhere = pl.BlockSpec(memory_space=pltpu.HBM)
    tiles = EARLY + up_half.shape[0]
    held = (resid_grad, mixer.reshape(count, width), qkv, edges, state_in, normed, weights, vectors, up_half, down_half)

    def stages(lead, rows, columns):
        return [
            low(lead, 2, 4, rows, columns), low(lead, 4, rows, columns),
            low(lead, 3, rows, columns), wide(lead, 2, rows, columns),
        ]

    return pl.pallas_call(
        back_kernel,
        out_shape=outs,
        in_specs=[anywhere] * 9 + [vmem] + [anywhere] * 4,
        out_specs=[anywhere] + [vmem] * 5,
        scratch_shapes=[pltpu.VMEM(array.shape, array.dtype) for array in held]
        + [
            wide(slots, block_len + 8, width),
            low(count, width),
            low(slots, block_len, width),
            low(3, slots, block_len, width),
            wide(slots, block_len + 8, width),
            low(width, count),
            low(pairs, slots, PAIR, PAIR),
            low(pairs, slots, PAIR, PAIR),
            low(4, width // 4, width),
            low(4, width // 4, width // 2),
            low(pairs, 2, 4, width // 4, PAIR),
            low(pairs, 4, width // 4, PAIR),
            low(3, 4, width // 4, PAIR),
        ]
        + stages(tiles, 48, 256) + stages(tiles, 32, 384) + stages(1, 48, 384) + stages(pairs + 3, 48, PAIR)
        + [
            wide(16, width),
            wide(3, 16, width),
            wide(6, 16, width),
            dma((22, 7)),
            dma((22, 7)),
            dma((13,)),
            dma((2,)),
            dma((3,)),
            dma((3,)),
            dma((6,)),
            dma((6,)),
            dma((6,)),
            dma((6,)),
            dma((3,)),
            dma((3,)),
        ],
        compiler_params=pltpu.CompilerParams(
            collective_id=1, has_side_effects=True, vmem_limit_bytes=63 * MIB
        ),
        name="backward_reduce",
    )(
        resid_grad, mixer.reshape(count, width), qkv, edges, state_in, normed, tokens.reshape(count, width), weights, vectors,
        two_sums, up_half, down_half, up_b, down_b,
    )


def from_behind(value, axis, steps):
    count = lax.axis_size(axis)
    leading, last = (max(0, -steps), min(count, count - steps))
    return lax.ppermute(value, axis, [(source, source + steps) for source in range(leading, last)])


def as_sent(array):

    def short(part):
        return part.astype(jnp.bfloat16) if part.dtype == jnp.float32 else part

    return jax.tree.map(short, array)


def layer_norm(values, norm_gain, offset):
    center = jnp.mean(values, axis=-1, keepdims=True)
    centered = values - center
    spread = jnp.mean(centered * centered, axis=-1, keepdims=True)
    return centered * lax.rsqrt(spread + 1e-05) * norm_gain + offset


def shift_mix(extended, tap_table):
    block_len = extended.shape[-2] - 3
    mixed_sum = tap_table[0] * extended[..., 3 : 3 + block_len, :]
    for lag_step in range(1, 4):
        mixed_sum = (
            mixed_sum
            + tap_table[lag_step] * extended[..., 3 - lag_step : 3 - lag_step + block_len, :]
        )
    return mixed_sum


def factors(queries, key_rows, rate_vector):
    block_len = queries.shape[1]
    rate_grid = rate_vector.reshape(queries.shape[2], -1)
    positions = jnp.arange(block_len, dtype=jnp.float32)[:, None, None]
    decayed = queries * jnp.exp(-rate_grid * positions)
    lifted = key_rows * jnp.exp(rate_grid * positions)
    tail_keys = key_rows * jnp.exp(-rate_grid * (block_len - 1.0 - positions))
    reaching = queries * jnp.exp(-rate_grid * (positions + 1.0))
    carry_decay = jnp.exp(-rate_grid * block_len)
    return (decayed, lifted, tail_keys, reaching, carry_decay)


def outer_sum(left_rows, right_rows):
    return lax.dot_general(
        left_rows, right_rows, (((0,), (0,)), ((), ())), preferred_element_type=jnp.float32
    )


def back_product(grad_rows, weight):
    return lax.dot_general(
        grad_rows, weight, (((1,), (1,)), ((), ())), preferred_element_type=jnp.float32
    )


def general(
    tokens,
    ln1_gain,
    ln1_bias,
    qkv_weight,
    shift_taps,
    decay_rates,
    out_weight,
    ln2_gain,
    ln2_bias,
    up_weight,
    down_weight,
    lengths,
    out_grad,
):
    slot_count, block_len, model_width = tokens.shape
    token_count = slot_count * block_len
    gathered = (
        lax.all_gather(ln1_gain, "dp", axis=0, tiled=True),
        lax.all_gather(ln1_bias, "dp", axis=0, tiled=True),
        lax.all_gather(qkv_weight, "dp", axis=0, tiled=True),
        lax.all_gather(shift_taps, "dp", axis=1, tiled=True),
        lax.all_gather(decay_rates, "dp", axis=0, tiled=True),
        lax.all_gather(out_weight, "dp", axis=0, tiled=True),
        lax.all_gather(ln2_gain, "dp", axis=0, tiled=True),
        lax.all_gather(ln2_bias, "dp", axis=0, tiled=True),
        lax.all_gather(up_weight, "dp", axis=0, tiled=True),
        lax.all_gather(down_weight, "dp", axis=0, tiled=True),
    )
    gain_one = gathered[0].astype(jnp.float32)
    bias_one = gathered[1].astype(jnp.float32)
    tap_table = gathered[3].astype(jnp.float32)
    rate_vector = gathered[4].astype(jnp.float32)
    gain_two = gathered[6].astype(jnp.float32)
    bias_two = gathered[7].astype(jnp.float32)
    qkv_full = gathered[2]
    out_full = gathered[5]
    up_full = gathered[8]
    down_full = gathered[9]
    inputs = tokens.reshape(token_count, model_width).astype(jnp.float32)
    normed_one = layer_norm(inputs, gain_one, bias_one).astype(jnp.bfloat16)
    projected = jnp.dot(normed_one, qkv_full, preferred_element_type=jnp.float32).astype(
        jnp.bfloat16
    )
    projected = projected.reshape(slot_count, block_len, 3 * model_width)
    key_rows = projected[:, :, model_width : 2 * model_width]
    edge_rows = from_behind(key_rows[:, block_len - 3 :], "seq", 1)
    extended = jnp.concatenate([edge_rows, key_rows], axis=1).astype(jnp.float32)
    shifted = shift_mix(extended, tap_table)
    head_shape = (slot_count, block_len, HEADS, HEAD_DIM)
    flat_shape = (slot_count, block_len, model_width)
    head_queries = projected[:, :, :model_width].astype(jnp.float32).reshape(head_shape)
    head_keys = shifted.reshape(head_shape)
    head_values = projected[:, :, 2 * model_width :].reshape(head_shape)
    decayed, lifted, tail_keys, reaching, carry_decay = factors(
        head_queries, head_keys, rate_vector
    )
    decayed_low = decayed.astype(jnp.bfloat16)
    lifted_low = lifted.astype(jnp.bfloat16)
    tail_low = tail_keys.astype(jnp.bfloat16)
    reach_wide = reaching.astype(jnp.bfloat16).astype(jnp.float32)
    position_ids = jnp.arange(block_len)
    causal = position_ids[:, None] >= position_ids[None, :]
    scores = jnp.einsum(
        "bthk,bshk->bhts", decayed_low, lifted_low, preferred_element_type=jnp.float32
    )
    scores_low = jnp.where(causal, scores, 0.0).astype(jnp.bfloat16)
    within = jnp.einsum(
        "bhts,bshv->bthv", scores_low, head_values, preferred_element_type=jnp.float32
    )
    fresh_state = jnp.einsum(
        "bshk,bshv->bhkv", tail_low, head_values, preferred_element_type=jnp.float32
    )
    empty_state = jnp.zeros_like(fresh_state)
    state_in = empty_state
    for relay_turn in range(lax.axis_size("seq") - 1):
        state_in = from_behind(carry_decay[None, :, :, None] * state_in + fresh_state, "seq", 1)
    inter = jnp.einsum("bthk,bhkv->bthv", reach_wide, state_in, precision=precise)
    mixer = (within + inter).reshape(token_count, model_width).astype(jnp.bfloat16)
    resid = inputs + jnp.dot(mixer, out_full, preferred_element_type=jnp.float32)
    normed_two = layer_norm(resid, gain_two, bias_two).astype(jnp.bfloat16)
    hidden_pre = jnp.dot(normed_two, up_full, preferred_element_type=jnp.float32)
    hidden = jax.nn.gelu(hidden_pre).astype(jnp.bfloat16)
    result = resid + jnp.dot(hidden, down_full, preferred_element_type=jnp.float32)
    mixed = result.reshape(flat_shape).astype(jnp.bfloat16)
    qkv_full, out_full, up_full, down_full = (
        lax.all_gather(qkv_weight, "dp", axis=0, tiled=True),
        lax.all_gather(out_weight, "dp", axis=0, tiled=True),
        lax.all_gather(up_weight, "dp", axis=0, tiled=True),
        lax.all_gather(down_weight, "dp", axis=0, tiled=True),
    )
    positions = lax.axis_index("seq") * block_len + jnp.arange(block_len, dtype=jnp.int32)
    keep_mask = (positions[None, :] < lengths[:, None]).astype(jnp.float32)
    grad_rows = (out_grad.astype(jnp.float32) * keep_mask[:, :, None]).reshape(
        token_count, model_width
    )
    grad_low = grad_rows.astype(jnp.bfloat16)
    down_grad = outer_sum(hidden, grad_low)
    hidden_grad = back_product(grad_low, down_full)
    _, gelu_back = jax.vjp(jax.nn.gelu, hidden_pre)
    pre_grad = gelu_back(hidden_grad)[0].astype(jnp.bfloat16)
    up_grad = outer_sum(normed_two, pre_grad)
    _, norm_two_back = jax.vjp(layer_norm, resid, gain_two, bias_two)
    resid_part, gain_two_grad, bias_two_grad = norm_two_back(back_product(pre_grad, up_full))
    resid_grad = grad_rows + resid_part
    branch_grad = resid_grad.astype(jnp.bfloat16)
    proj_grad = outer_sum(mixer, branch_grad)
    mixer_low = back_product(branch_grad, out_full).astype(jnp.bfloat16).reshape(head_shape)
    mixer_wide = mixer_low.astype(jnp.float32)
    local_grad = jnp.einsum("bthk,bthv->bhkv", reach_wide, mixer_wide, precision=precise)
    state_grad = empty_state
    for relay_turn in range(lax.axis_size("seq") - 1):
        state_grad = from_behind(
            as_sent(carry_decay[None, :, :, None] * state_grad + local_grad), "seq", -1
        )
    score_grad = jnp.einsum(
        "bthv,bshv->bhts", mixer_low, head_values, preferred_element_type=jnp.float32
    ).astype(jnp.bfloat16)
    score_grad = jnp.where(causal, score_grad, jnp.zeros_like(score_grad))
    decayed_grad = jnp.einsum(
        "bhts,bshk->bthk", score_grad, lifted_low, preferred_element_type=jnp.float32
    )
    lifted_grad = jnp.einsum(
        "bhts,bthk->bshk", score_grad, decayed_low, preferred_element_type=jnp.float32
    )
    value_grad = jnp.einsum(
        "bhts,bthv->bshv", scores_low, mixer_low, preferred_element_type=jnp.float32
    )
    value_grad = value_grad + jnp.einsum(
        "bshk,bhkv->bshv", tail_low.astype(jnp.float32), state_grad, precision=precise
    )
    tail_grad = jnp.einsum(
        "bshv,bhkv->bshk", head_values.astype(jnp.float32), state_grad, precision=precise
    )
    reach_grad = jnp.einsum("bthv,bhkv->bthk", mixer_wide, state_in, precision=precise)
    carry_grad = jnp.sum(state_grad * state_in, axis=(0, 3))
    _, factor_back = jax.vjp(factors, head_queries, head_keys, rate_vector)
    query_grad, key_grad, rate_grad = factor_back(
        (decayed_grad, lifted_grad, tail_grad, reach_grad, carry_grad)
    )
    _, shift_back = jax.vjp(shift_mix, extended, tap_table)
    extended_grad, taps_grad = shift_back(key_grad.reshape(flat_shape))
    spill = from_behind(extended_grad[:, :3], "seq", -1)
    keys_grad = jnp.concatenate(
        [extended_grad[:, 3:block_len], extended_grad[:, block_len:] + spill], axis=1
    )
    qkv_grad_low = jnp.concatenate(
        [query_grad.reshape(flat_shape), keys_grad, value_grad.reshape(flat_shape)], axis=2
    )
    qkv_grad_low = qkv_grad_low.reshape(token_count, 3 * model_width).astype(jnp.bfloat16)
    qkv_grad = outer_sum(normed_one, qkv_grad_low)
    _, norm_one_back = jax.vjp(layer_norm, inputs, gain_one, bias_one)
    input_part, gain_one_grad, bias_one_grad = norm_one_back(back_product(qkv_grad_low, qkv_full))
    input_grad = (resid_grad + input_part).reshape(flat_shape)
    reduced = (
        lax.psum_scatter(gain_one_grad, "dp", scatter_dimension=0, tiled=True),
        lax.psum_scatter(bias_one_grad, "dp", scatter_dimension=0, tiled=True),
        lax.psum_scatter(qkv_grad, "dp", scatter_dimension=0, tiled=True),
        lax.psum_scatter(taps_grad, "dp", scatter_dimension=1, tiled=True),
        lax.psum_scatter(rate_grad, "dp", scatter_dimension=0, tiled=True),
        lax.psum_scatter(proj_grad, "dp", scatter_dimension=0, tiled=True),
        lax.psum_scatter(gain_two_grad, "dp", scatter_dimension=0, tiled=True),
        lax.psum_scatter(bias_two_grad, "dp", scatter_dimension=0, tiled=True),
        lax.psum_scatter(up_grad, "dp", scatter_dimension=0, tiled=True),
        lax.psum_scatter(down_grad, "dp", scatter_dimension=0, tiled=True),
    )
    summed = lax.psum(
        (
            reduced[0],
            reduced[1],
            reduced[2],
            reduced[3],
            reduced[4],
            reduced[5],
            reduced[6],
            reduced[7],
            reduced[8],
            reduced[9],
        ),
        "seq",
    )
    return (
        mixed,
        input_grad,
        summed[0],
        summed[1],
        summed[2],
        summed[3],
        summed[4],
        summed[5],
        summed[6],
        summed[7],
        summed[8],
        summed[9],
    )


def near(
    tokens,
    ln1_gain,
    ln1_bias,
    qkv_weight,
    shift_taps,
    decay_rates,
    out_weight,
    ln2_gain,
    ln2_bias,
    up_weight,
    down_weight,
    lengths,
    out_grad,
):
    width = tokens.shape[2]
    own = ln1_gain.shape[0]
    packed = jnp.concatenate(
        [
            jnp.stack([ln1_gain, ln1_bias, decay_rates, ln2_gain, ln2_bias]),
            shift_taps,
            jnp.zeros((7, own), LOW),
        ],
        axis=0,
    )
    start = lax.axis_index("dp") * own
    packed = lax.dynamic_update_slice(jnp.zeros((16, width), LOW), packed, (0, start))
    (
        mixed, normed, qkv, edges, state_in, mixer, resid_grad, weights, vectors, two_sums, up_half, down_half, up_b, down_b,
    ) = front(packed, qkv_weight, out_weight, up_weight, down_weight, tokens, out_grad, lengths)
    input_grad, up_sum, down_sum, out_sum, qkv_sum, small = back(
        resid_grad, mixer, qkv, edges, state_in, normed, tokens, weights, vectors, two_sums, up_half, down_half, up_b, down_b,
    )
    small = lax.dynamic_slice(small, (0, start), (16, own))
    return (
        mixed, input_grad, small[0], small[1], qkv_sum, small[3:7], small[2], out_sum, small[8], small[9],
        up_sum, down_sum,
    )


def solution(mesh):
    in_specs = (
        P("dp", "seq", None),
        P("dp"),
        P("dp"),
        P("dp", None),
        P(None, "dp"),
        P("dp"),
        P("dp", None),
        P("dp"),
        P("dp"),
        P("dp", None),
        P("dp", None),
        P("dp"),
        P("dp", "seq", None),
    )
    out_specs = (
        P("dp", "seq", None),
        P("dp", "seq", None),
        P("dp"),
        P("dp"),
        P("dp", None),
        P(None, "dp"),
        P("dp"),
        P("dp", None),
        P("dp"),
        P("dp"),
        P("dp", None),
        P("dp", None),
    )
    local = near if dict(mesh.shape) == {"dp": 16, "seq": 2} else general
    return jax.shard_map(local, mesh=mesh, in_specs=in_specs, out_specs=out_specs, check_vma=False)
```

```python
import functools

import jax
import jax.numpy as jnp
from jax import lax
from jax.experimental import pallas as pl
from jax.experimental.pallas import tpu as pltpu
from jax.sharding import PartitionSpec as P

HEADS = 12
HEAD_DIM = 64
PAIR = 2 * HEAD_DIM
MESH = pl.DeviceIdType.MESH
MIB = 2**20
GELU_A = 0.7978845608028654
GELU_B = 0.044715
ROW_RATE, ROW_TAPS = 2, 5
LOW = jnp.bfloat16
WIDE = jnp.float32


precise = lax.Precision.HIGHEST


class Place:
    def __init__(self):
        self.dp = lax.axis_index("dp")
        self.core = lax.axis_index("seq")
        self.z = self.dp // 4
        self.stride_a = 2 - self.core
        self.stride_b = 1 + self.core
        self.a = (self.dp // self.stride_a) % 2
        self.b = (self.dp // self.stride_b) % 2

    def spot(self, da, db):
        return (self.a + da) % 2 * self.stride_a + (self.b + db) % 2 * self.stride_b

    def sibling_spot(self, da, db):
        return (self.b + da) % 2 * self.stride_b + (self.a + db) % 2 * self.stride_a

    def peer(self, dz, da, db):
        return ((self.z + dz) % 4 * 4 + self.spot(da, db), self.core)

    def sibling(self):
        return (self.dp, 1 - self.core)


PEERS = ((1, 0, 0), (2, 0, 0), (3, 0, 0), (0, 1, 0), (0, 0, 1))


def enter(place):
    barrier = pltpu.get_barrier_semaphore()
    for step in PEERS:
        pl.semaphore_signal(barrier, inc=1, device_id=place.peer(*step), device_id_type=MESH)
    pl.semaphore_signal(barrier, inc=1, device_id=place.sibling(), device_id_type=MESH)
    pl.semaphore_wait(barrier, len(PEERS) + 1)


def enter_all(place):
    barrier = pltpu.get_barrier_semaphore()
    for step in range(1, 16):
        pl.semaphore_signal(
            barrier, inc=1, device_id=((place.dp + step) % 16, place.core), device_id_type=MESH
        )
    pl.semaphore_signal(barrier, inc=1, device_id=place.sibling(), device_id_type=MESH)
    pl.semaphore_wait(barrier, 16)


def small_start(dp):
    tile = dp * 3 // 8
    return (tile - tile // 5) * 128


def remote(source, target, send_sem, recv_sem, device):
    return pltpu.make_async_remote_copy(
        src_ref=source,
        dst_ref=target,
        send_sem=send_sem,
        recv_sem=recv_sem,
        device_id=device,
        device_id_type=MESH,
    )


def part(start, size, step):
    return pl.ds(pl.multiple_of(start, step), size)


class Unit:
    def __init__(self, shard, buffer, rows, tiles=None, start=0, width=None, shared=False, plane=False):
        self.shard, self.buffer, self.rows, self.tiles = shard, buffer, rows, tiles
        self.start, self.width, self.shared, self.plane = start, width, shared, plane

    def columns(self, side):
        if self.shared:
            return slice(None)
        return part(self.start + side * (self.width // 2), self.width // 2, 128)

    def own(self, side):
        if self.shared:
            return self.shard[0]
        columns = part(self.shard[1] + side * (self.width // 2), self.width // 2, 128)
        if self.tiles:
            return self.shard[0].at[pl.ds(*self.tiles), :, columns]
        return self.shard[0].at[:, columns]

    def at(self, z, rows, columns):
        if self.tiles:
            return self.buffer.at[pl.ds(*self.tiles), z, rows, columns]
        return self.buffer.at[z, rows, columns]

    def slab(self, spot, columns):
        return self.at(slice(None), part(spot * self.rows, self.rows, 16), columns)

    def floor(self, z, columns):
        return self.at(z, slice(None), columns)

    def block(self, z, spot, columns):
        return self.at(z, part(spot * self.rows, self.rows, 16), columns)


class Script:
    def __init__(self, events):
        self.events, self.done, self.held = events, 0, set()

    def take(self, count):
        chosen = []
        while len(chosen) < count and self.done < len(self.events):
            which, event = self.events[self.done]
            if which in self.held:
                break
            chosen.append(event)
            self.done += 1
        return chosen

    def tick(self, count=1000):
        for event in self.take(count):
            event()

    def points(self, trips, count, each=1, release=None):
        chosen = []
        for trip in range(trips):
            if release is not None:
                self.held -= release(trip)
            for _ in range(count):
                chosen.append(self.take(each))

        def run(index, point):
            for trip in range(trips):
                events = chosen[trip * count + point]
                if events:
                    @pl.when(index == trip)
                    def _(events=events):
                        for event in events:
                            event()

        return run


class Gather:
    def __init__(self, place, units, send_sem, recv_sem, local_sem):
        self.place, self.units = place, units
        self.send_sem, self.recv_sem, self.local_sem = send_sem, recv_sem, local_sem
        self.script = Script([])
        self.ready = {}
        events = self.script.events
        count = len(units)
        for turn in range(count + 2):
            for lag, step in enumerate((self.one, self.two, self.three)):
                if 0 <= turn - lag < count:
                    which = ORDER[turn - lag]
                    events.append((which, functools.partial(step, which)))
                    self.ready[which] = len(events)

    def need(self, which):
        self.script.tick(max(0, self.ready[which] - self.script.done))
        self.land(which)

    def land(self, which):
        unit, place = self.units[which], self.place
        if unit.shared:
            return
        other = unit.columns(1 - place.core)
        for slot, (da, db) in enumerate(((0, 0), (1, 0), (0, 1), (1, 1))):
            if unit.plane:
                window = unit.floor((place.z + slot) % 4, other)
            else:
                window = unit.slab(place.sibling_spot(da, db), other)
            pltpu.make_async_copy(window, window, self.recv_sem.at[which, 6 + slot]).wait()

    def copy(self, which, slot):
        unit, place = self.units[which], self.place
        mine = unit.columns(place.core)
        landing = slot
        if slot >= 6:
            device = place.sibling()
        elif unit.plane:
            device = place.peer(*((0, 1, 0), (0, 0, 1), (0, 0, 1), (1, 0, 0), (2, 0, 0), (3, 0, 0))[slot])
            landing = 8 - slot if slot >= 3 else slot
        else:
            device = place.peer(*((1, 0, 0), (2, 0, 0), (3, 0, 0), (0, 1, 0), (0, 0, 1), (0, 0, 1))[slot])
            landing = 2 - slot if slot < 3 else slot
        if unit.plane and slot < 3:
            target = unit.block(place.z, place.spot(1 if slot == 2 else 0, 0), mine)
            source = target if slot == 2 else unit.own(place.core)
        elif unit.plane:
            source = target = unit.floor((place.z + max(0, slot - 6)) % 4, mine)
        elif slot < 3:
            source, target = unit.own(place.core), unit.block(place.z, place.spot(0, 0), mine)
        else:
            da, db = ((0, 0), (0, 0), (1, 0), (0, 0), (1, 0), (0, 1), (1, 1))[slot - 3]
            source = target = unit.slab(place.spot(da, db), mine)
        return remote(
            source, target, self.send_sem.at[which, slot], self.recv_sem.at[which, landing], device
        )

    def stay(self, which):
        unit, place = self.units[which], self.place
        return pltpu.make_async_copy(
            unit.own(place.core),
            unit.block(place.z, place.spot(0, 0), unit.columns(place.core)),
            self.local_sem.at[which],
        )

    def start(self, which):
        self.stay(which).start()
        for slot in range(2 if self.units[which].plane else 3):
            self.copy(which, slot).start()

    def arrive(self, which, slot):
        unit, place = self.units[which], self.place
        mine = unit.columns(place.core)
        if unit.plane and slot < 3:
            window = unit.block(place.z, place.spot(*((1, 0), (0, 1), (1, 1))[slot]), mine)
        elif unit.plane:
            window = unit.floor((place.z + slot - 2) % 4, mine)
        elif slot < 3:
            window = unit.block((place.z + slot + 1) % 4, place.spot(0, 0), mine)
        else:
            window = unit.slab(place.spot(*((1, 0), (0, 1), (1, 1))[slot - 3]), mine)
        pltpu.make_async_copy(window, window, self.recv_sem.at[which, slot]).wait()

    def send(self, which, *slots):
        for slot in slots:
            if slot < 6 or not self.units[which].shared:
                self.copy(which, slot).start()

    def one(self, which):
        self.stay(which).wait()
        if self.units[which].plane:
            self.arrive(which, 0)
            self.send(which, 2)
            return
        for slot in range(3):
            self.arrive(which, slot)
        self.send(which, 3, 4, 6)

    def two(self, which):
        if self.units[which].plane:
            self.arrive(which, 1)
            self.arrive(which, 2)
            self.send(which, 3, 4, 5, 6)
            return
        self.arrive(which, 3)
        self.send(which, 5, 7)

    def three(self, which):
        if self.units[which].plane:
            for slot in range(3, 6):
                self.arrive(which, slot)
                self.send(which, slot + 4)
            return
        self.arrive(which, 4)
        self.send(which, 8)
        self.arrive(which, 5)
        self.send(which, 9)

    def drain(self):
        for which, unit in enumerate(self.units):
            for slot in range(6 if unit.shared else 10):
                self.copy(which, slot).wait_send()


def nt(left, right):
    return lax.dot_general(left, right, (((1,), (1,)), ((), ())), preferred_element_type=WIDE)


def tn(left, right):
    return lax.dot_general(left, right, (((0,), (0,)), ((), ())), preferred_element_type=WIDE)


def nn(left, right):
    return jnp.dot(left, right, preferred_element_type=WIDE)


def normalize(values):
    center = jnp.mean(values, axis=-1, keepdims=True)
    centered = values - center
    spread = jnp.mean(centered * centered, axis=-1, keepdims=True)
    scale = lax.rsqrt(spread + 1e-05)
    return centered * scale, scale


def normalize_back(grad, normed, scale, gain):
    weighted = grad * gain
    inner = weighted - jnp.mean(weighted, axis=-1, keepdims=True)
    inner = inner - normed * jnp.mean(weighted * normed, axis=-1, keepdims=True)
    return scale * inner


def lanes(pair):
    return pl.ds(pl.multiple_of(pair * PAIR, PAIR), PAIR)


def head_mask(rows, side):
    spots = lax.broadcasted_iota(jnp.int32, (rows, PAIR), 1)
    return (spots // HEAD_DIM) == side


def only(mask, values):
    return jnp.where(mask, values, jnp.zeros_like(values))


def same_head():
    first = lax.broadcasted_iota(jnp.int32, (PAIR, PAIR), 0) // HEAD_DIM
    second = lax.broadcasted_iota(jnp.int32, (PAIR, PAIR), 1) // HEAD_DIM
    return first == second


def lower(size):
    return lax.broadcasted_iota(jnp.int32, (size, size), 0) >= lax.broadcasted_iota(
        jnp.int32, (size, size), 1
    )


def split(values):
    high = values.astype(LOW)
    low = (values - high.astype(WIDE)).astype(LOW)
    return high, low


def spots_of(block_len):
    return lax.broadcasted_iota(jnp.int32, (block_len, 1), 0).astype(WIDE)


def shifted_keys(keys, slot, window, taps):
    block_len = keys.shape[1] - 8
    total = taps[0:1] * keys[slot, 8 : 8 + block_len, window]
    for lag in range(1, 4):
        total = total + taps[lag : lag + 1] * keys[slot, 8 - lag : 8 - lag + block_len, window]
    return total


LOTS = 6


def hidden_order(shard):
    size = shard.shape[1] // (16 * LOTS)
    pieces = [
        shard[:, (device * LOTS + lot) * size : (device * LOTS + lot + 1) * size]
        for lot in range(LOTS)
        for device in range(16)
    ]
    return jnp.concatenate(pieces, axis=1)


def hidden_disorder(columns):
    size = columns.shape[1] // (16 * LOTS)
    pieces = [
        columns[:, (lot * 16 + device) * size : (lot * 16 + device + 1) * size]
        for device in range(16)
        for lot in range(LOTS)
    ]
    return jnp.concatenate(pieces, axis=1)


VEC, KEY, VALUE, QUERY, OUT, DOWN, UP = range(7)
GROUPS = ((0, 2), (2, 2), (4, 1), (5, 1))
EARLY = 4
ORDER = tuple(range(13))
APART = 3


def front_kernel(
    lengths, packed, qkv_shard, out_shard, up_shard, down_shard, tokens_in, cotangent_in,
    mixed_out, normed_out, qkv_out, edges_out, state_out, mixer_out, resid_grad_out, weights_out,
    vectors_out, sums_out, up_out, down_out, up_b_out, down_b_out,
    vec_all, weights, up_all, down_all, up_own, tokens, grad_low, normed, qkv, edges, state_in,
    state_send, mixer, resid, normed_turned, keys, summed, vectors, sums,
    up_stage, down_stage, up_half, down_half, up_b, down_b,
    send_sem, recv_sem, local_sem, load_sem, save_sem, pair_send, pair_recv, tile_send, tile_recv,
    early_send, early_recv,
):
    slots, block_len, width = tokens.shape
    pairs = width // PAIR
    size = block_len // 2
    tiles = up_half.shape[0]
    place = Place()
    core = place.core
    first = core == 0
    queries, key_rows, values = qkv.at[0], qkv.at[1], qkv.at[2]
    normed_two, mixer_view = normed, mixer

    def load(slot, source, target):
        return pltpu.make_async_copy(source, target, load_sem.at[slot])

    def save(slot):
        source, target = (
            (mixer_view, mixed_out), (normed, normed_out), (qkv, qkv_out), (edges, edges_out),
            (state_in, state_out), (mixer, mixer_out), (keys.at[:, pl.ds(0, block_len)], resid_grad_out),
            (weights, weights_out), (vectors, vectors_out), (sums, sums_out),
            (up_half.at[pl.ds(EARLY, tiles - EARLY)], up_out),
            (down_half.at[pl.ds(EARLY, tiles - EARLY)], down_out), (up_b, up_b_out), (down_b, down_b_out),
        )[slot]
        return pltpu.make_async_copy(source, target, save_sem.at[slot])

    load(0, up_shard, up_own).start()
    load(1, tokens_in, tokens).start()
    load(2, cotangent_in, grad_low).start()
    enter(place)
    units = [
        Unit((packed, 0), vec_all, 16, shared=True),
        Unit((qkv_shard, width), weights.at[1], 48, width=width),
        Unit((qkv_shard, 2 * width), weights.at[2], 48, width=width),
        Unit((qkv_shard, 0), weights.at[0], 48, width=width),
        Unit((out_shard, 0), weights.at[3], 48, width=width),
    ]
    for lot, count in GROUPS:
        units.append(Unit((down_shard, 0), down_all, 32, tiles=(lot, count), width=width))
        units.append(Unit((up_own, lot * 512), up_all, 48, start=lot * 512, width=count * 512))
    gather = Gather(place, units, send_sem, recv_sem, local_sem)
    for which in range(5):
        gather.start(which)
    load(0, up_shard, up_own).wait()
    up_own[...] = hidden_order(up_own[...])
    for which in range(5, len(units)):
        gather.start(which)

    load(1, tokens_in, tokens).wait()
    for slot in range(slots):
        summed[slot], _ = normalize(tokens[slot].astype(WIDE))
    load(2, cotangent_in, grad_low).wait()
    base = core * block_len
    for slot in range(slots):
        keep = base + lax.broadcasted_iota(jnp.int32, (block_len, 1), 0) < lengths[slot]
        grad_low[slot] = (grad_low[slot].astype(WIDE) * keep.astype(WIDE)).astype(LOW)
    gather.need(VEC)
    vectors[...] = sum(
        vec_all[z, spot * 16 : spot * 16 + 16].astype(WIDE) for z in range(4) for spot in range(4)
    )
    gain, bias = vectors[0:1], vectors[1:2]
    for slot in range(slots):
        rows = slice(slot * block_len, (slot + 1) * block_len)
        normed[rows] = (summed[slot] * gain + bias).astype(LOW)
    save(1).start()
    save(8).start()

    def weight(which):
        return weights[which].reshape(width, width)

    def project(which):
        for slot in range(slots):
            rows = slice(slot * block_len, (slot + 1) * block_len)
            qkv[which, slot] = nn(normed[rows], weight(which)).astype(LOW)

    gather.need(KEY)
    project(1)
    edge_copy = remote(
        key_rows.at[:, pl.ds(block_len - 16, 16)], edges, pair_send.at[0], pair_recv.at[0], place.sibling()
    )

    @pl.when(first)
    def _():
        edge_copy.start()

    gather.need(VALUE)
    project(2)
    gather.need(QUERY)
    project(0)
    save(2).start()

    @pl.when(first)
    def _():
        edge_copy.wait_send()
        edges[...] = jnp.zeros_like(edges)

    @pl.when(core == 1)
    def _():
        edge_copy.wait_recv()

    save(3).start()
    for slot in range(slots):
        keys[slot, 0:8] = edges[slot].astype(WIDE)[8:16]
        keys[slot, 8:] = key_rows[slot].astype(WIDE)
    spots = spots_of(block_len)
    state_copy = remote(state_send, state_in, pair_send.at[1], pair_recv.at[1], place.sibling())

    @pl.when(first)
    def _():
        def fresh(pair, carry):
            window = lanes(pair)
            rate = vectors[ROW_RATE : ROW_RATE + 1, window]
            taps = vectors[ROW_TAPS : ROW_TAPS + 4, window]
            tail = jnp.exp(-rate * (block_len - 1.0 - spots))
            for slot in range(slots):
                tail_keys = (shifted_keys(keys, slot, window, taps) * tail).astype(LOW)
                state_send[pair, slot] = only(same_head(), tn(tail_keys, values[slot, :, window]))
            return carry

        lax.fori_loop(0, pairs, fresh, 0)
        state_copy.start()

    gather.script.tick(2)

    spread_within = gather.script.points(pairs, 1)

    def within(pair, carry):
        spread_within(pair, 0)
        window = lanes(pair)
        rate = vectors[ROW_RATE : ROW_RATE + 1, window]
        taps = vectors[ROW_TAPS : ROW_TAPS + 4, window]
        fall = jnp.exp(-rate * spots)
        rise = jnp.exp(rate * spots)
        for slot in range(slots):
            decayed = (queries[slot, :, window].astype(WIDE) * fall).astype(LOW)
            lifted = (shifted_keys(keys, slot, window, taps) * rise).astype(LOW)
            value = values[slot, :, window]
            top = jnp.zeros((size, PAIR), WIDE)
            low = jnp.zeros((size, PAIR), WIDE)
            for side in range(2):
                query_side = only(head_mask(block_len, side), decayed)
                value_side = only(head_mask(block_len, side), value)
                near = jnp.where(lower(size), nt(query_side[:size], lifted[:size]), 0.0)
                top = top + nn(near.astype(LOW), value_side[:size])
                far = nt(query_side[size:], lifted[:size]).astype(LOW)
                near = jnp.where(lower(size), nt(query_side[size:], lifted[size:]), 0.0)
                low = low + nn(far, value_side[:size]) + nn(near.astype(LOW), value_side[size:])
            summed[slot, :size, window] = top
            summed[slot, size:, window] = low
        return carry

    lax.fori_loop(0, pairs, within, 0)

    @pl.when(first)
    def _():
        state_copy.wait_send()
        state_in[...] = jnp.zeros_like(state_in)

    @pl.when(core == 1)
    def _():
        state_copy.wait_recv()

        def reach(pair, carry):
            window = lanes(pair)
            rate = vectors[ROW_RATE : ROW_RATE + 1, window]
            decay = jnp.exp(-rate * (spots + 1.0))
            for slot in range(slots):
                reaching = (queries[slot, :, window].astype(WIDE) * decay).astype(LOW)
                high, low = split(state_in[pair, slot])
                summed[slot, :, window] += nn(reaching, high) + nn(reaching, low)
            return carry

        lax.fori_loop(0, pairs, reach, 0)

    save(4).start()
    gather.need(OUT)
    save(7).start()
    gain_two, bias_two = vectors[3:4], vectors[4:5]
    for slot in range(slots):
        rows = slice(slot * block_len, (slot + 1) * block_len)
        if slot == 0:
            save(1).wait()
        mixer[slot] = summed[slot].astype(LOW)
        total = tokens[slot].astype(WIDE) + nn(mixer[slot], weight(3))
        resid[slot] = total
        summed[slot] = total
        hat, _ = normalize(total)
        normed_two[rows] = (hat * gain_two + bias_two).astype(LOW)
    save(5).start()
    normed_turned[...] = normed_two[...].T
    keys[:, 0:block_len] = jnp.zeros((slots, block_len, width), WIDE)
    gather.need(DOWN)
    gather.need(UP)

    def tile_copies(tile):
        slot = tile % 2
        other = 1 - core
        return (
            remote(
                up_stage.at[slot, :, :, part(other * 256, 256, 128)],
                up_half.at[tile],
                tile_send.at[tile, 0],
                tile_recv.at[tile, 0],
                place.sibling(),
            ),
            remote(
                down_stage.at[slot, :, :, part(other * 384, 384, 128)],
                down_half.at[tile],
                tile_send.at[tile, 1],
                tile_recv.at[tile, 1],
                place.sibling(),
            ),
        )

    def merge(tile):
        for copy in tile_copies(tile):
            copy.wait_recv()
        slot = tile % 2
        up_half[tile] = up_half[tile] + up_stage[slot, :, :, part(core * 256, 256, 128)]
        down_half[tile] = down_half[tile] + down_stage[slot, :, :, part(core * 384, 384, 128)]

    shares = [
        Share(up_half.at[k], up_half.at[k], up_b.at[k], None, None, None, 48) for k in range(EARLY)
    ] + [
        Share(down_half.at[k], down_half.at[k], down_b.at[k], None, None, None, 32) for k in range(EARLY)
    ]
    early = Reduction(place, shares, early_send, early_recv)
    spread = gather.script.points(tiles, 3)

    def ffn_tile(tile, carry):
        for group in range(1, len(GROUPS)):
            @pl.when(tile == GROUPS[group][0])
            def _(group=group):
                gather.land(DOWN + 2 * group)
                gather.land(UP + 2 * group)

        spread(tile, 0)
        columns = part(tile * 512, 512, 512)
        up = up_all[:, :, columns].reshape(width, 512)
        down = down_all[tile].reshape(512, width)
        cotangent = grad_low[...].reshape(slots * block_len, width)
        pre = nn(normed_two[...], up)
        wide = nt(cotangent, down)
        square = pre * pre
        ramp = jnp.tanh(pre * (GELU_A + (GELU_A * GELU_B) * square))
        half = 0.5 + 0.5 * ramp
        slope = half + (0.5 * pre) * (1.0 - ramp * ramp) * (
            GELU_A + (3.0 * GELU_A * GELU_B) * square
        )
        act = (pre * half).astype(LOW)
        back = (wide * slope).astype(LOW)
        spread(tile, 1)

        @pl.when(tile >= 1)
        def _():
            merge(tile - 1)

        for k in range(EARLY):
            @pl.when(tile == k + 1)
            def _(k=k):
                early.start(k)
                early.start(EARLY + k)

        for slot in range(slots):
            rows = slice(slot * block_len, (slot + 1) * block_len)
            summed[slot] += nn(act[rows], down)
            keys[slot, 0:block_len] += nt(back[rows], up)
        turn = tile % 2
        spread(tile, 2)

        @pl.when(tile >= 2)
        def _():
            for copy in tile_copies(tile - 2):
                copy.wait_send()

        up_stage[turn] = nn(normed_turned[...], back).astype(LOW).reshape(4, width // 4, 512)
        down_stage[turn] = tn(act, cotangent).astype(LOW).reshape(4, 128, width)
        for copy in tile_copies(tile):
            copy.start()
        return carry

    lax.fori_loop(0, tiles, ffn_tile, 0)
    sums[...] = jnp.zeros_like(sums)
    for slot in range(slots):
        if slot == 0:
            save(5).wait()
        mixer[slot] = summed[slot].astype(LOW)
        hat, scale = normalize(resid[slot])
        grad = keys[slot, 0:block_len]
        sums[0:1] += jnp.sum(grad * hat, axis=0, keepdims=True)
        sums[1:2] += jnp.sum(grad, axis=0, keepdims=True)
        keys[slot, 0:block_len] = grad_low[slot].astype(WIDE) + normalize_back(grad, hat, scale, gain_two)
    save(0).start()
    save(6).start()
    save(9).start()
    for k in range(EARLY):
        early.merge_b(k)
        early.merge_b(EARLY + k)
    save(12).start()
    save(13).start()
    merge(tiles - 1)
    save(10).start()
    save(11).start()
    for tile in (tiles - 2, tiles - 1):
        for copy in tile_copies(tile):
            copy.wait_send()
    gather.script.tick()
    gather.drain()
    early.drain()
    for slot in (0, 2, 3, 4, 6, 7, 8, 9, 10, 11, 12, 13):
        save(slot).wait()


def front(packed, qkv_weight, out_weight, up_weight, down_weight, tokens, cotangent, lengths):
    slots, block_len, width = tokens.shape
    count = slots * block_len
    pairs = width // PAIR
    hidden = up_weight.shape[1]
    tiles = hidden // 512
    shape = jax.ShapeDtypeStruct
    outs = [
        shape(tokens.shape, LOW),
        shape((count, width), LOW),
        shape((3, slots, block_len, width), LOW),
        shape((slots, 16, width), LOW),
        shape((pairs, slots, PAIR, PAIR), WIDE),
        shape(tokens.shape, LOW),
        shape(tokens.shape, WIDE),
        shape((4, 4, width // 4, width), LOW),
        shape((16, width), WIDE),
        shape((8, width), WIDE),
        shape((tiles - EARLY, 4, width // 4, 256), LOW),
        shape((tiles - EARLY, 4, 128, width // 2), LOW),
        shape((EARLY, 2, 4, width // 16, 256), LOW),
        shape((EARLY, 2, 4, 32, width // 2), LOW),
    ]
    vmem = lambda *dims: pltpu.VMEM(dims, LOW)
    wide = lambda *dims: pltpu.VMEM(dims, WIDE)
    dma = pltpu.SemaphoreType.DMA
    anywhere = pl.BlockSpec(memory_space=pltpu.HBM)
    return pl.pallas_call(
        front_kernel,
        out_shape=outs,
        in_specs=[pl.BlockSpec(memory_space=pltpu.SMEM)] + [anywhere] * 7,
        out_specs=[anywhere] * len(outs),
        scratch_shapes=[
            vmem(4, 64, width),
            vmem(4, 4, width // 4, width),
            vmem(4, width // 4, hidden),
            vmem(tiles, 4, 128, width),
            vmem(width // 16, hidden),
            vmem(slots, block_len, width),
            vmem(slots, block_len, width),
            vmem(count, width),
            vmem(3, slots, block_len, width),
            vmem(slots, 16, width),
            wide(pairs, slots, PAIR, PAIR),
            wide(pairs, slots, PAIR, PAIR),
            vmem(slots, block_len, width),
            wide(slots, block_len, width),
            vmem(width, count),
            wide(slots, block_len + 8, width),
            wide(slots, block_len, width),
            wide(16, width),
            wide(8, width),
            vmem(2, 4, width // 4, 512),
            vmem(2, 4, 128, width),
            vmem(tiles, 4, width // 4, 256),
            vmem(tiles, 4, 128, width // 2),
            vmem(EARLY, 2, 4, width // 16, 256),
            vmem(EARLY, 2, 4, 32, width // 2),
            dma((13, 10)),
            dma((13, 10)),
            dma((13,)),
            dma((3,)),
            dma((14,)),
            dma((2,)),
            dma((2,)),
            dma((tiles, 2)),
            dma((tiles, 2)),
            dma((2 * EARLY, 2)),
            dma((2 * EARLY, 2)),
        ],
        compiler_params=pltpu.CompilerParams(
            collective_id=0, has_side_effects=True, vmem_limit_bytes=63 * MIB
        ),
        name="gather_forward_ffn",
    )(
        lengths, packed, qkv_weight, out_weight, up_weight, down_weight.reshape(tiles, 32, width), tokens,
        cotangent,
    )


class Share:
    def __init__(self, source, own, from_b, from_a, from_z, final, rows):
        self.source, self.own, self.rows = source, own, rows
        self.from_b, self.from_a, self.from_z, self.final = from_b, from_a, from_z, final

    def slab(self, ref, spot):
        return ref.at[:, part(spot * self.rows, self.rows, 16)]


class Reduction:
    def __init__(self, place, shares, send_sem, recv_sem):
        self.place, self.shares = place, shares
        self.send_sem, self.recv_sem = send_sem, recv_sem

    def copy(self, which, slot):
        share, place = self.shares[which], self.place
        if slot < 2:
            da = 1 - slot
            source = share.slab(share.source, place.spot(da, 1))
            target = share.from_b.at[(place.a + da) % 2]
            device = place.peer(0, 0, 1)
        elif slot == 2:
            source, target = share.from_b.at[1 - place.a], share.from_a
            device = place.peer(0, 1, 0)
        elif slot < 6:
            dz = slot - 2
            source, target = share.from_a.at[(place.z + dz) % 4], share.from_z.at[dz - 1]
            device = place.peer(dz, 0, 0)
        else:
            source = target = share.final.at[place.core]
            device = place.sibling()
        return remote(source, target, self.send_sem.at[which, slot], self.recv_sem.at[which, slot], device)

    def start(self, which):
        if self.shares[which].source is None:
            self.copy(which, 2).start()
            return
        for slot in range(2):
            self.copy(which, slot).start()

    def merge_b(self, which):
        share, place = self.shares[which], self.place
        for slot in range(2):
            self.copy(which, slot).wait_recv()
            da = 1 - slot
            a = (place.a + da) % 2
            rows = part(place.spot(da, 0) * share.rows, share.rows, 16)
            share.from_b[a] = share.from_b[a] + share.own[:, rows]
            if slot == 0 and share.from_a is not None:
                self.copy(which, 2).start()

    def merge_a(self, which):
        share = self.shares[which]
        self.copy(which, 2).wait_recv()
        share.from_a[...] = share.from_a[...] + share.from_b[self.place.a]
        for slot in range(3, 6):
            self.copy(which, slot).start()

    def finish(self, which):
        share, place = self.shares[which], self.place
        total = share.from_a[place.z].astype(WIDE)
        for slot in range(3):
            self.copy(which, 3 + slot).wait_recv()
            total = total + share.from_z[slot].astype(WIDE)
        share.final[place.core] = total
        self.copy(which, 6).start()

    def land(self, which):
        share, place = self.shares[which], self.place
        other = share.final.at[1 - place.core]
        pltpu.make_async_copy(other, other, self.recv_sem.at[which, 6]).wait()

    def drain(self):
        for which, share in enumerate(self.shares):
            first = 2 if share.source is None else 0
            for slot in range(first, 2 if share.from_a is None else 7):
                self.copy(which, slot).wait_send()

    def events(self, order):
        steps = []
        for which in order:
            own = [self.merge_b] if self.shares[which].source is not None else []
            steps.append([functools.partial(f, which) for f in own + [self.merge_a, self.finish]])
        events = []
        for turn in range(len(steps) + 3 * APART):
            for which in range(len(steps)):
                step, rest = divmod(turn - which, APART)
                if rest == 0 and 0 <= step < len(steps[which]):
                    events.append((order[which], steps[which][step]))
        return events


UPS, DOWNS, OUTS, PAIRS, KEYS = 0, 6, 12, 13, 19


def back_kernel(
    resid_grad_in, mixer_in, qkv_in, edges_in, state_in_in, normed_in, tokens_in, weights_in,
    vectors_in, two_sums, up_in, down_in, up_b_in, down_b_in,
    input_grad_out, up_sum, down_sum, out_sum, qkv_sum, small_out,
    resid_grad, mixer, qkv, edges, state_in, normed, weights, vectors, up_half, down_half,
    keys, branch, back_rows, projected, key_back, normed_turned, state_send, state_grad,
    out_stage, out_half, pair_stage, pair_half, key_half,
    up_b, up_a, up_z, up_final, down_b, down_a, down_z, down_final, wide_b, wide_a, wide_z, wide_final,
    pair_b, pair_a, pair_z, pair_final, small, small_other, small_sum, small_from,
    send_sem, recv_sem, load_sem, save_sem, core_send, core_recv, pair_send, pair_recv,
    small_send, small_recv, key_send, key_recv,
):
    slots, block_len, width = resid_grad.shape
    pairs = width // PAIR
    size = block_len // 2
    place = Place()
    core = place.core
    first = core == 0
    second = core == 1
    queries, key_rows, values = qkv.at[0], qkv.at[1], qkv.at[2]
    inputs = (
        (resid_grad_in, resid_grad), (weights_in, weights), (vectors_in, vectors), (qkv_in, qkv),
        (mixer_in, mixer), (edges_in, edges), (state_in_in, state_in), (normed_in, normed),
        (up_in, up_half), (down_in, down_half), (up_b_in, up_b.at[pl.ds(0, EARLY)]),
        (down_b_in, down_b.at[pl.ds(0, EARLY)]), (tokens_in, mixer),
    )
    LOAD_GRAD, LOAD_WEIGHTS, LOAD_VECTORS, LOAD_QKV, LOAD_MIXER, LOAD_EDGES, LOAD_STATE = range(7)
    LOAD_NORMED, LOAD_UP, LOAD_DOWN, LOAD_UP_B, LOAD_DOWN_B, LOAD_TOKENS = range(7, 13)

    def load(slot):
        return pltpu.make_async_copy(*inputs[slot], load_sem.at[slot])

    for slot in (
        LOAD_UP, LOAD_DOWN, LOAD_UP_B, LOAD_DOWN_B, LOAD_GRAD, LOAD_WEIGHTS, LOAD_VECTORS, LOAD_QKV,
        LOAD_MIXER, LOAD_EDGES, LOAD_STATE, LOAD_NORMED,
    ):
        load(slot).start()
    enter_all(place)
    tiles = EARLY + up_half.shape[0]

    def tile_share(k, halves, from_b, from_a, from_z, final, rows):
        own = None if k < EARLY else halves.at[k - EARLY]
        return Share(own, own, from_b.at[k], from_a.at[k], from_z.at[k], final.at[k], rows)

    def column_share(half, k):
        return Share(half, half, wide_b.at[k], wide_a.at[k], wide_z.at[k], wide_final.at[k], 48)

    def pair_share(half, k):
        return Share(half, half, pair_b.at[k], pair_a.at[k], pair_z.at[k], pair_final.at[k], 48)

    shares = [tile_share(k, up_half, up_b, up_a, up_z, up_final, 48) for k in range(tiles)]
    shares += [tile_share(k, down_half, down_b, down_a, down_z, down_final, 32) for k in range(tiles)]
    shares.append(column_share(out_half, 0))
    shares += [pair_share(pair_half.at[k], k) for k in range(pairs)]
    shares += [pair_share(key_half.at[k], pairs + k) for k in range(3)]
    reduction = Reduction(place, shares, send_sem, recv_sem)
    for slot in (LOAD_UP, LOAD_DOWN, LOAD_UP_B, LOAD_DOWN_B):
        load(slot).wait()
    order = [kind + k for k in range(tiles) for kind in (UPS, DOWNS)]
    for which in order[2 * EARLY :] + order[: 2 * EARLY]:
        reduction.start(which)
    order += [OUTS, *range(PAIRS, PAIRS + pairs), *range(KEYS, KEYS + 3)]
    script = Script(reduction.events(order))
    script.held = {OUTS, *range(PAIRS, PAIRS + pairs), *range(KEYS, KEYS + 3)}
    spots = spots_of(block_len)

    load(LOAD_GRAD).wait()
    load(LOAD_WEIGHTS).wait()
    out_weight = weights[3].reshape(width, width)
    for slot in range(slots):
        rows = slice(slot * block_len, (slot + 1) * block_len)
        branch[rows] = resid_grad[slot].astype(LOW)
        back_rows[slot] = nt(branch[rows], out_weight).astype(LOW)
    load(LOAD_VECTORS).wait()
    load(LOAD_QKV).wait()
    state_copy = remote(state_send, state_grad, core_send.at[0], core_recv.at[0], place.sibling())

    @pl.when(second)
    def _():
        def gather_state(pair, carry):
            window = lanes(pair)
            rate = vectors[ROW_RATE : ROW_RATE + 1, window]
            decay = jnp.exp(-rate * (spots + 1.0))
            for slot in range(slots):
                reaching = (queries[slot, :, window].astype(WIDE) * decay).astype(LOW)
                back = back_rows[slot, :, window]
                state_send[pair, slot] = only(same_head(), tn(reaching, back)).astype(LOW)
            return carry

        lax.fori_loop(0, pairs, gather_state, 0)
        state_copy.start()

    load(LOAD_MIXER).wait()
    normed_turned[...] = mixer[...].T
    out_stage[...] = nn(normed_turned[...], branch[...]).astype(LOW).reshape(4, width // 4, width)

    load(LOAD_TOKENS).start()

    def key_copy(k):
        window = part((1 - core) * (width // 2) + k * PAIR, PAIR, 128)
        return remote(
            out_stage.at[:, :, window], key_half.at[k], key_send.at[k], key_recv.at[k], place.sibling()
        )

    out_copy = remote(
        out_stage.at[:, :, part((1 - core) * (width // 2), width // 2, 128)],
        out_half,
        core_send.at[2],
        core_recv.at[2],
        place.sibling(),
    )
    out_copy.start()
    load(LOAD_EDGES).wait()
    load(LOAD_STATE).wait()
    load(LOAD_NORMED).wait()
    normed_turned[...] = normed[...].T
    for slot in range(slots):
        keys[slot, 0:8] = edges[slot].astype(WIDE)[8:16]
        keys[slot, 8:] = key_rows[slot].astype(WIDE)
    out_copy.wait_recv()
    out_half[...] = out_half[...] + out_stage[:, :, part(core * (width // 2), width // 2, 128)]
    reduction.start(OUTS)
    script.held -= {OUTS}

    @pl.when(second)
    def _():
        state_copy.wait_send()
        state_grad[...] = jnp.zeros_like(state_grad)

    @pl.when(first)
    def _():
        state_copy.wait_recv()

    def pair_copy(pair):
        return remote(
            pair_stage.at[pair, 1 - core], pair_half.at[pair], pair_send.at[pair], pair_recv.at[pair],
            place.sibling(),
        )

    def merge_pair(pair):
        pair_copy(pair).wait_recv()
        pair_half[pair] = pair_half[pair] + pair_stage[pair, core]

    spread = script.points(
        pairs, 2, TICKS_BACK, lambda trip: {PAIRS + trip - 2} if trip >= 2 else set()
    )

    def back_pair(pair, carry):
        spread(pair, 0)
        window = lanes(pair)
        rate = vectors[ROW_RATE : ROW_RATE + 1, window]
        taps = vectors[ROW_TAPS : ROW_TAPS + 4, window]
        fall = jnp.exp(-rate * spots)
        rise = jnp.exp(rate * spots)
        tail = jnp.exp(-rate * (block_len - 1.0 - spots))
        decay = jnp.exp(-rate * (spots + 1.0))
        rate_grad = jnp.zeros((1, PAIR), WIDE)
        taps_grad = [jnp.zeros((1, PAIR), WIDE) for _ in range(4)]
        weight_grad = jnp.zeros((width, 2 * PAIR), WIDE)
        for slot in range(slots):
            if slot == 1:
                spread(pair, 1)
            query = queries[slot, :, window].astype(WIDE)
            key = shifted_keys(keys, slot, window, taps)
            value = values[slot, :, window]
            back = back_rows[slot, :, window]
            wide_decayed, wide_lifted = query * fall, key * rise
            wide_tail, wide_reach = key * tail, query * decay
            decayed, lifted = wide_decayed.astype(LOW), wide_lifted.astype(LOW)
            tail_keys = wide_tail.astype(LOW)
            decayed_turned, back_turned = decayed.T, back.T
            decayed_top = jnp.zeros((size, PAIR), WIDE)
            decayed_low = jnp.zeros((size, PAIR), WIDE)
            lifted_top = jnp.zeros((PAIR, size), WIDE)
            lifted_low = jnp.zeros((PAIR, size), WIDE)
            value_top = jnp.zeros((PAIR, size), WIDE)
            value_low = jnp.zeros((PAIR, size), WIDE)
            row_head = lax.broadcasted_iota(jnp.int32, (PAIR, block_len), 0) // HEAD_DIM
            for side in range(2):
                mask = head_mask(block_len, side)
                query_side, back_side = only(mask, decayed), only(mask, back)
                lifted_side = only(mask, lifted)
                query_turned = only(row_head == side, decayed_turned)
                back_side_turned = only(row_head == side, back_turned)
                causal = lower(size)
                halves_of = (slice(0, size), slice(size, block_len))
                for t, s in ((0, 0), (1, 0), (1, 1)):
                    score = nt(query_side[halves_of[t]], lifted[halves_of[s]])
                    grad = nt(back_side[halves_of[t]], value[halves_of[s]])
                    if t == s:
                        score, grad = jnp.where(causal, score, 0.0), jnp.where(causal, grad, 0.0)
                    score, grad = score.astype(LOW), grad.astype(LOW)
                    query_part = nn(grad, lifted_side[halves_of[s]])
                    lifted_part = nn(query_turned[:, halves_of[t]], grad)
                    value_part = nn(back_side_turned[:, halves_of[t]], score)
                    if t == 0:
                        decayed_top = decayed_top + query_part
                    else:
                        decayed_low = decayed_low + query_part
                    if s == 0:
                        lifted_top, value_top = lifted_top + lifted_part, value_top + value_part
                    else:
                        lifted_low, value_low = lifted_low + lifted_part, value_low + value_part
            decayed_grad = jnp.concatenate([decayed_top, decayed_low], axis=0)
            lifted_grad = jnp.concatenate([lifted_top.T, lifted_low.T], axis=0)
            value_grad = jnp.concatenate([value_top.T, value_low.T], axis=0)
            leaving = state_grad[pair, slot]
            entering = state_in[pair, slot]
            high, low = split(entering)
            value_grad = value_grad + nn(tail_keys, leaving)
            tail_grad = nt(value, leaving)
            reach_grad = nt(back, high) + nt(back, low)
            carry_grad = jnp.sum((leaving.astype(WIDE) * entering).T, axis=0, keepdims=True)
            key_grad = lifted_grad * rise + tail_grad * tail
            steps = (
                spots * (lifted_grad * wide_lifted - decayed_grad * wide_decayed)
                - (block_len - 1.0 - spots) * (tail_grad * wide_tail)
                - (spots + 1.0) * (reach_grad * wide_reach)
            )
            rate_grad = rate_grad + jnp.sum(steps, axis=0, keepdims=True)
            rate_grad = rate_grad - block_len * jnp.exp(-rate * block_len) * carry_grad
            query_low = (decayed_grad * fall + reach_grad * decay).astype(LOW)
            value_low_grad = value_grad.astype(LOW)
            projected[0, slot, :, window] = query_low
            projected[2, slot, :, window] = value_low_grad
            key_back[slot, 0:block_len, window] = key_grad
            for lag in range(4):
                lagged = keys[slot, 8 - lag : 8 - lag + block_len, window]
                taps_grad[lag] = taps_grad[lag] + jnp.sum(lagged * key_grad, axis=0, keepdims=True)
            rows = slice(slot * block_len, (slot + 1) * block_len)
            weight_grad = weight_grad + nn(
                normed_turned[:, rows], jnp.concatenate([query_low, value_low_grad], axis=1)
            )
        small[0:8, window] = jnp.concatenate(
            [jnp.zeros((2, PAIR), WIDE), rate_grad, *taps_grad, jnp.zeros((1, PAIR), WIDE)], axis=0
        )
        for side in range(2):
            pair_stage[pair, side] = (
                weight_grad[:, side * PAIR : (side + 1) * PAIR].astype(LOW).reshape(4, width // 4, PAIR)
            )
        pair_copy(pair).start()

        @pl.when(pair >= 1)
        def _():
            merge_pair(pair - 1)

        for k in range(1, pairs):
            @pl.when(pair == k)
            def _(k=k):
                reduction.start(PAIRS + k - 1)

        return carry

    lax.fori_loop(0, pairs, back_pair, 0)
    spill = remote(
        key_back.at[:, pl.ds(0, 8)],
        key_back.at[:, pl.ds(block_len, 8)],
        core_send.at[1],
        core_recv.at[1],
        place.sibling(),
    )

    @pl.when(second)
    def _():
        spill.start()
        key_back[:, block_len : block_len + 8] = jnp.zeros((slots, 8, width), WIDE)

    merge_pair(pairs - 1)
    reduction.start(PAIRS + pairs - 1)
    script.held -= set(range(PAIRS, PAIRS + pairs))
    out_copy.wait_send()

    @pl.when(first)
    def _():
        spill.wait_recv()

    spread_keys = script.points(pairs, 1, 1)

    def key_pair(pair, carry):
        spread_keys(pair, 0)
        window = lanes(pair)
        taps = vectors[ROW_TAPS : ROW_TAPS + 4, window]
        for slot in range(slots):
            total = taps[0:1] * key_back[slot, 0:block_len, window]
            for lag in range(1, 4):
                total = total + taps[lag : lag + 1] * key_back[slot, lag : lag + block_len, window]
            projected[1, slot, :, window] = total.astype(LOW)
        return carry

    lax.fori_loop(0, pairs, key_pair, 0)
    rows_all = projected[1].reshape(slots * block_len, width)
    out_stage[...] = nn(normed_turned[...], rows_all).astype(LOW).reshape(4, width // 4, width)
    for k in range(3):
        key_copy(k).start()
    script.tick(3)
    load(LOAD_TOKENS).wait()
    gain = vectors[0:1]
    gain_sum = jnp.zeros((1, width), WIDE)
    bias_sum = jnp.zeros((1, width), WIDE)
    for slot in range(slots):
        grad = nt(projected[0, slot], weights[0].reshape(width, width))
        for third in range(1, 3):
            grad = grad + nt(projected[third, slot], weights[third].reshape(width, width))
        if slot == 0:
            for k in range(3):
                key_copy(k).wait_recv()
                window = part(core * (width // 2) + k * PAIR, PAIR, 128)
                key_half[k] = key_half[k] + out_stage[:, :, window]
                reduction.start(KEYS + k)
            script.held.clear()
        script.tick(4)
        hat, scale = normalize(mixer[slot * block_len : (slot + 1) * block_len].astype(WIDE))
        gain_sum = gain_sum + jnp.sum(grad * hat, axis=0, keepdims=True)
        bias_sum = bias_sum + jnp.sum(grad, axis=0, keepdims=True)
        resid_grad[slot] = resid_grad[slot] + normalize_back(grad, hat, scale, gain)
        pltpu.make_async_copy(
            resid_grad.at[slot], input_grad_out.at[slot], save_sem.at[slot]
        ).start()
        script.tick(4)
    small[0:1], small[1:2] = gain_sum, bias_sum
    small[8:16] = two_sums[...]

    def small_copy(step):
        if step == 0:
            return remote(small, small_other, small_send.at[0], small_recv.at[0], place.sibling())
        target = (place.dp + step) % 16
        return remote(
            small_sum.at[:, part(small_start(target), 256, 128)],
            small_from.at[place.dp],
            small_send.at[step],
            small_recv.at[step],
            (target, core),
        )

    small_copy(0).start()
    script.tick(2)
    small_copy(0).wait_recv()
    small_sum[...] = small[...] + small_other[...]
    for step in range(1, 16):
        small_copy(step).start()
    small_from[place.dp] = small_sum[:, part(small_start(place.dp), 256, 128)]
    script.tick()
    for step in range(1, 16):
        window = small_from.at[(place.dp + 16 - step) % 16]
        pltpu.make_async_copy(window, window, small_recv.at[step]).wait()
    total = small_from[0]
    for source in range(1, 16):
        total = total + small_from[source]
    small_out[...] = total
    for which in range(len(shares)):
        reduction.land(which)
    ups = [up_final[tile, side] for tile in range(6) for side in range(2)]
    up_sum[...] = hidden_disorder(jnp.concatenate(ups, axis=1))
    for side in range(2):
        half = slice(side * 384, side * 384 + 384)
        for tile in range(tiles):
            down_sum[tile * 32 : tile * 32 + 32, half] = down_final[tile, side]
        out_sum[:, half] = wide_final[0, side]
        for k in range(3):
            start = width + side * 384 + k * PAIR
            qkv_sum[:, start : start + PAIR] = pair_final[pairs + k, side]
        for pair in range(pairs):
            start = 2 * width * side + pair * PAIR
            qkv_sum[:, start : start + PAIR] = pair_final[pair, side]
    reduction.drain()
    for step in range(16):
        small_copy(step).wait_send()
    for pair in range(pairs):
        pair_copy(pair).wait_send()
    for k in range(3):
        key_copy(k).wait_send()

    @pl.when(second)
    def _():
        spill.wait_send()

    for slot in range(slots):
        pltpu.make_async_copy(
            resid_grad.at[slot], input_grad_out.at[slot], save_sem.at[slot]
        ).wait()


TICKS_BACK = 2


def back(
    resid_grad, mixer, qkv, edges, state_in, normed, tokens, weights, vectors, two_sums, up_half, down_half, up_b, down_b,
):
    slots, block_len, width = tokens.shape
    count = slots * block_len
    pairs = width // PAIR
    shape = jax.ShapeDtypeStruct
    outs = [
        shape(tokens.shape, WIDE),
        shape((width // 16, 4 * width), WIDE),
        shape((4 * width // 16, width), WIDE),
        shape((width // 16, width), WIDE),
        shape((width // 16, 3 * width), WIDE),
        shape((16, 256), WIDE),
    ]
    low = lambda *dims: pltpu.VMEM(dims, LOW)
    wide = lambda *dims: pltpu.VMEM(dims, WIDE)
    dma = pltpu.SemaphoreType.DMA
    vmem = pl.BlockSpec(memory_space=pltpu.VMEM)
    anywhere = pl.BlockSpec(memory_space=pltpu.HBM)
    tiles = EARLY + up_half.shape[0]
    held = (resid_grad, mixer.reshape(count, width), qkv, edges, state_in, normed, weights, vectors, up_half, down_half)

    def stages(lead, rows, columns):
        return [
            low(lead, 2, 4, rows, columns), low(lead, 4, rows, columns),
            low(lead, 3, rows, columns), wide(lead, 2, rows, columns),
        ]

    return pl.pallas_call(
        back_kernel,
        out_shape=outs,
        in_specs=[anywhere] * 9 + [vmem] + [anywhere] * 4,
        out_specs=[anywhere] + [vmem] * 5,
        scratch_shapes=[pltpu.VMEM(array.shape, array.dtype) for array in held]
        + [
            wide(slots, block_len + 8, width),
            low(count, width),
            low(slots, block_len, width),
            low(3, slots, block_len, width),
            wide(slots, block_len + 8, width),
            low(width, count),
            low(pairs, slots, PAIR, PAIR),
            low(pairs, slots, PAIR, PAIR),
            low(4, width // 4, width),
            low(4, width // 4, width // 2),
            low(pairs, 2, 4, width // 4, PAIR),
            low(pairs, 4, width // 4, PAIR),
            low(3, 4, width // 4, PAIR),
        ]
        + stages(tiles, 48, 256) + stages(tiles, 32, 384) + stages(1, 48, 384) + stages(pairs + 3, 48, PAIR)
        + [
            wide(16, width),
            wide(16, width),
            wide(16, width),
            wide(16, 16, 256),
            dma((22, 7)),
            dma((22, 7)),
            dma((13,)),
            dma((2,)),
            dma((3,)),
            dma((3,)),
            dma((6,)),
            dma((6,)),
            dma((16,)),
            dma((16,)),
            dma((3,)),
            dma((3,)),
        ],
        compiler_params=pltpu.CompilerParams(
            collective_id=1, has_side_effects=True, vmem_limit_bytes=63 * MIB
        ),
        name="backward_reduce",
    )(
        resid_grad, mixer.reshape(count, width), qkv, edges, state_in, normed, tokens.reshape(count, width), weights, vectors,
        two_sums, up_half, down_half, up_b, down_b,
    )


def from_behind(value, axis, steps):
    count = lax.axis_size(axis)
    leading, last = (max(0, -steps), min(count, count - steps))
    return lax.ppermute(value, axis, [(source, source + steps) for source in range(leading, last)])


def as_sent(array):

    def short(part):
        return part.astype(jnp.bfloat16) if part.dtype == jnp.float32 else part

    return jax.tree.map(short, array)


def layer_norm(values, norm_gain, offset):
    center = jnp.mean(values, axis=-1, keepdims=True)
    centered = values - center
    spread = jnp.mean(centered * centered, axis=-1, keepdims=True)
    return centered * lax.rsqrt(spread + 1e-05) * norm_gain + offset


def shift_mix(extended, tap_table):
    block_len = extended.shape[-2] - 3
    mixed_sum = tap_table[0] * extended[..., 3 : 3 + block_len, :]
    for lag_step in range(1, 4):
        mixed_sum = (
            mixed_sum
            + tap_table[lag_step] * extended[..., 3 - lag_step : 3 - lag_step + block_len, :]
        )
    return mixed_sum


def factors(queries, key_rows, rate_vector):
    block_len = queries.shape[1]
    rate_grid = rate_vector.reshape(queries.shape[2], -1)
    positions = jnp.arange(block_len, dtype=jnp.float32)[:, None, None]
    decayed = queries * jnp.exp(-rate_grid * positions)
    lifted = key_rows * jnp.exp(rate_grid * positions)
    tail_keys = key_rows * jnp.exp(-rate_grid * (block_len - 1.0 - positions))
    reaching = queries * jnp.exp(-rate_grid * (positions + 1.0))
    carry_decay = jnp.exp(-rate_grid * block_len)
    return (decayed, lifted, tail_keys, reaching, carry_decay)


def outer_sum(left_rows, right_rows):
    return lax.dot_general(
        left_rows, right_rows, (((0,), (0,)), ((), ())), preferred_element_type=jnp.float32
    )


def back_product(grad_rows, weight):
    return lax.dot_general(
        grad_rows, weight, (((1,), (1,)), ((), ())), preferred_element_type=jnp.float32
    )


def general(
    tokens,
    ln1_gain,
    ln1_bias,
    qkv_weight,
    shift_taps,
    decay_rates,
    out_weight,
    ln2_gain,
    ln2_bias,
    up_weight,
    down_weight,
    lengths,
    out_grad,
):
    slot_count, block_len, model_width = tokens.shape
    token_count = slot_count * block_len
    gathered = (
        lax.all_gather(ln1_gain, "dp", axis=0, tiled=True),
        lax.all_gather(ln1_bias, "dp", axis=0, tiled=True),
        lax.all_gather(qkv_weight, "dp", axis=0, tiled=True),
        lax.all_gather(shift_taps, "dp", axis=1, tiled=True),
        lax.all_gather(decay_rates, "dp", axis=0, tiled=True),
        lax.all_gather(out_weight, "dp", axis=0, tiled=True),
        lax.all_gather(ln2_gain, "dp", axis=0, tiled=True),
        lax.all_gather(ln2_bias, "dp", axis=0, tiled=True),
        lax.all_gather(up_weight, "dp", axis=0, tiled=True),
        lax.all_gather(down_weight, "dp", axis=0, tiled=True),
    )
    gain_one = gathered[0].astype(jnp.float32)
    bias_one = gathered[1].astype(jnp.float32)
    tap_table = gathered[3].astype(jnp.float32)
    rate_vector = gathered[4].astype(jnp.float32)
    gain_two = gathered[6].astype(jnp.float32)
    bias_two = gathered[7].astype(jnp.float32)
    qkv_full = gathered[2]
    out_full = gathered[5]
    up_full = gathered[8]
    down_full = gathered[9]
    inputs = tokens.reshape(token_count, model_width).astype(jnp.float32)
    normed_one = layer_norm(inputs, gain_one, bias_one).astype(jnp.bfloat16)
    projected = jnp.dot(normed_one, qkv_full, preferred_element_type=jnp.float32).astype(
        jnp.bfloat16
    )
    projected = projected.reshape(slot_count, block_len, 3 * model_width)
    key_rows = projected[:, :, model_width : 2 * model_width]
    edge_rows = from_behind(key_rows[:, block_len - 3 :], "seq", 1)
    extended = jnp.concatenate([edge_rows, key_rows], axis=1).astype(jnp.float32)
    shifted = shift_mix(extended, tap_table)
    head_shape = (slot_count, block_len, HEADS, HEAD_DIM)
    flat_shape = (slot_count, block_len, model_width)
    head_queries = projected[:, :, :model_width].astype(jnp.float32).reshape(head_shape)
    head_keys = shifted.reshape(head_shape)
    head_values = projected[:, :, 2 * model_width :].reshape(head_shape)
    decayed, lifted, tail_keys, reaching, carry_decay = factors(
        head_queries, head_keys, rate_vector
    )
    decayed_low = decayed.astype(jnp.bfloat16)
    lifted_low = lifted.astype(jnp.bfloat16)
    tail_low = tail_keys.astype(jnp.bfloat16)
    reach_wide = reaching.astype(jnp.bfloat16).astype(jnp.float32)
    position_ids = jnp.arange(block_len)
    causal = position_ids[:, None] >= position_ids[None, :]
    scores = jnp.einsum(
        "bthk,bshk->bhts", decayed_low, lifted_low, preferred_element_type=jnp.float32
    )
    scores_low = jnp.where(causal, scores, 0.0).astype(jnp.bfloat16)
    within = jnp.einsum(
        "bhts,bshv->bthv", scores_low, head_values, preferred_element_type=jnp.float32
    )
    fresh_state = jnp.einsum(
        "bshk,bshv->bhkv", tail_low, head_values, preferred_element_type=jnp.float32
    )
    empty_state = jnp.zeros_like(fresh_state)
    state_in = empty_state
    for relay_turn in range(lax.axis_size("seq") - 1):
        state_in = from_behind(carry_decay[None, :, :, None] * state_in + fresh_state, "seq", 1)
    inter = jnp.einsum("bthk,bhkv->bthv", reach_wide, state_in, precision=precise)
    mixer = (within + inter).reshape(token_count, model_width).astype(jnp.bfloat16)
    resid = inputs + jnp.dot(mixer, out_full, preferred_element_type=jnp.float32)
    normed_two = layer_norm(resid, gain_two, bias_two).astype(jnp.bfloat16)
    hidden_pre = jnp.dot(normed_two, up_full, preferred_element_type=jnp.float32)
    hidden = jax.nn.gelu(hidden_pre).astype(jnp.bfloat16)
    result = resid + jnp.dot(hidden, down_full, preferred_element_type=jnp.float32)
    mixed = result.reshape(flat_shape).astype(jnp.bfloat16)
    qkv_full, out_full, up_full, down_full = (
        lax.all_gather(qkv_weight, "dp", axis=0, tiled=True),
        lax.all_gather(out_weight, "dp", axis=0, tiled=True),
        lax.all_gather(up_weight, "dp", axis=0, tiled=True),
        lax.all_gather(down_weight, "dp", axis=0, tiled=True),
    )
    positions = lax.axis_index("seq") * block_len + jnp.arange(block_len, dtype=jnp.int32)
    keep_mask = (positions[None, :] < lengths[:, None]).astype(jnp.float32)
    grad_rows = (out_grad.astype(jnp.float32) * keep_mask[:, :, None]).reshape(
        token_count, model_width
    )
    grad_low = grad_rows.astype(jnp.bfloat16)
    down_grad = outer_sum(hidden, grad_low)
    hidden_grad = back_product(grad_low, down_full)
    _, gelu_back = jax.vjp(jax.nn.gelu, hidden_pre)
    pre_grad = gelu_back(hidden_grad)[0].astype(jnp.bfloat16)
    up_grad = outer_sum(normed_two, pre_grad)
    _, norm_two_back = jax.vjp(layer_norm, resid, gain_two, bias_two)
    resid_part, gain_two_grad, bias_two_grad = norm_two_back(back_product(pre_grad, up_full))
    resid_grad = grad_rows + resid_part
    branch_grad = resid_grad.astype(jnp.bfloat16)
    proj_grad = outer_sum(mixer, branch_grad)
    mixer_low = back_product(branch_grad, out_full).astype(jnp.bfloat16).reshape(head_shape)
    mixer_wide = mixer_low.astype(jnp.float32)
    local_grad = jnp.einsum("bthk,bthv->bhkv", reach_wide, mixer_wide, precision=precise)
    state_grad = empty_state
    for relay_turn in range(lax.axis_size("seq") - 1):
        state_grad = from_behind(
            as_sent(carry_decay[None, :, :, None] * state_grad + local_grad), "seq", -1
        )
    score_grad = jnp.einsum(
        "bthv,bshv->bhts", mixer_low, head_values, preferred_element_type=jnp.float32
    ).astype(jnp.bfloat16)
    score_grad = jnp.where(causal, score_grad, jnp.zeros_like(score_grad))
    decayed_grad = jnp.einsum(
        "bhts,bshk->bthk", score_grad, lifted_low, preferred_element_type=jnp.float32
    )
    lifted_grad = jnp.einsum(
        "bhts,bthk->bshk", score_grad, decayed_low, preferred_element_type=jnp.float32
    )
    value_grad = jnp.einsum(
        "bhts,bthv->bshv", scores_low, mixer_low, preferred_element_type=jnp.float32
    )
    value_grad = value_grad + jnp.einsum(
        "bshk,bhkv->bshv", tail_low.astype(jnp.float32), state_grad, precision=precise
    )
    tail_grad = jnp.einsum(
        "bshv,bhkv->bshk", head_values.astype(jnp.float32), state_grad, precision=precise
    )
    reach_grad = jnp.einsum("bthv,bhkv->bthk", mixer_wide, state_in, precision=precise)
    carry_grad = jnp.sum(state_grad * state_in, axis=(0, 3))
    _, factor_back = jax.vjp(factors, head_queries, head_keys, rate_vector)
    query_grad, key_grad, rate_grad = factor_back(
        (decayed_grad, lifted_grad, tail_grad, reach_grad, carry_grad)
    )
    _, shift_back = jax.vjp(shift_mix, extended, tap_table)
    extended_grad, taps_grad = shift_back(key_grad.reshape(flat_shape))
    spill = from_behind(extended_grad[:, :3], "seq", -1)
    keys_grad = jnp.concatenate(
        [extended_grad[:, 3:block_len], extended_grad[:, block_len:] + spill], axis=1
    )
    qkv_grad_low = jnp.concatenate(
        [query_grad.reshape(flat_shape), keys_grad, value_grad.reshape(flat_shape)], axis=2
    )
    qkv_grad_low = qkv_grad_low.reshape(token_count, 3 * model_width).astype(jnp.bfloat16)
    qkv_grad = outer_sum(normed_one, qkv_grad_low)
    _, norm_one_back = jax.vjp(layer_norm, inputs, gain_one, bias_one)
    input_part, gain_one_grad, bias_one_grad = norm_one_back(back_product(qkv_grad_low, qkv_full))
    input_grad = (resid_grad + input_part).reshape(flat_shape)
    reduced = (
        lax.psum_scatter(gain_one_grad, "dp", scatter_dimension=0, tiled=True),
        lax.psum_scatter(bias_one_grad, "dp", scatter_dimension=0, tiled=True),
        lax.psum_scatter(qkv_grad, "dp", scatter_dimension=0, tiled=True),
        lax.psum_scatter(taps_grad, "dp", scatter_dimension=1, tiled=True),
        lax.psum_scatter(rate_grad, "dp", scatter_dimension=0, tiled=True),
        lax.psum_scatter(proj_grad, "dp", scatter_dimension=0, tiled=True),
        lax.psum_scatter(gain_two_grad, "dp", scatter_dimension=0, tiled=True),
        lax.psum_scatter(bias_two_grad, "dp", scatter_dimension=0, tiled=True),
        lax.psum_scatter(up_grad, "dp", scatter_dimension=0, tiled=True),
        lax.psum_scatter(down_grad, "dp", scatter_dimension=0, tiled=True),
    )
    summed = lax.psum(
        (
            reduced[0],
            reduced[1],
            reduced[2],
            reduced[3],
            reduced[4],
            reduced[5],
            reduced[6],
            reduced[7],
            reduced[8],
            reduced[9],
        ),
        "seq",
    )
    return (
        mixed,
        input_grad,
        summed[0],
        summed[1],
        summed[2],
        summed[3],
        summed[4],
        summed[5],
        summed[6],
        summed[7],
        summed[8],
        summed[9],
    )


def near(
    tokens,
    ln1_gain,
    ln1_bias,
    qkv_weight,
    shift_taps,
    decay_rates,
    out_weight,
    ln2_gain,
    ln2_bias,
    up_weight,
    down_weight,
    lengths,
    out_grad,
):
    width = tokens.shape[2]
    own = ln1_gain.shape[0]
    packed = jnp.concatenate(
        [
            jnp.stack([ln1_gain, ln1_bias, decay_rates, ln2_gain, ln2_bias]),
            shift_taps,
            jnp.zeros((7, own), LOW),
        ],
        axis=0,
    )
    start = lax.axis_index("dp") * own
    packed = lax.dynamic_update_slice(jnp.zeros((16, width), LOW), packed, (0, start))
    (
        mixed, normed, qkv, edges, state_in, mixer, resid_grad, weights, vectors, two_sums, up_half, down_half, up_b, down_b,
    ) = front(packed, qkv_weight, out_weight, up_weight, down_weight, tokens, out_grad, lengths)
    input_grad, up_sum, down_sum, out_sum, qkv_sum, small = back(
        resid_grad, mixer, qkv, edges, state_in, normed, tokens, weights, vectors, two_sums, up_half, down_half, up_b, down_b,
    )
    small = lax.dynamic_slice(small, (0, start - small_start(lax.axis_index("dp"))), (16, own))
    return (
        mixed, input_grad, small[0], small[1], qkv_sum, small[3:7], small[2], out_sum, small[8], small[9],
        up_sum, down_sum,
    )


def solution(mesh):
    in_specs = (
        P("dp", "seq", None),
        P("dp"),
        P("dp"),
        P("dp", None),
        P(None, "dp"),
        P("dp"),
        P("dp", None),
        P("dp"),
        P("dp"),
        P("dp", None),
        P("dp", None),
        P("dp"),
        P("dp", "seq", None),
    )
    out_specs = (
        P("dp", "seq", None),
        P("dp", "seq", None),
        P("dp"),
        P("dp"),
        P("dp", None),
        P(None, "dp"),
        P("dp"),
        P("dp", None),
        P("dp"),
        P("dp"),
        P("dp", None),
        P("dp", None),
    )
    local = near if dict(mesh.shape) == {"dp": 16, "seq": 2} else general
    return jax.shard_map(local, mesh=mesh, in_specs=in_specs, out_specs=out_specs, check_vma=False)
```
